128 devices in a mesh: rows: 8 (over x, core), cols: 16 (over z, y).
Axes of the slice: x: 4, y: 4, z: 4, core: 2. Of those that a mesh axis runs over, the one named last changes fastest.
Arguments:
- tokens: bfloat16 [5120, 8192], P(('rows', 'cols')), may hold values from -6 to 6
- norm_gain: float32 [8192], replicated, may hold values from 0.1 to 1.9
- gate_weight: bfloat16 [8192, 14336], P('rows', 'cols'), may hold values from -0.09375 to 0.09375
- up_weight: bfloat16 [8192, 14336], P('rows', 'cols'), may hold values from -0.09375 to 0.09375
- down_weight: bfloat16 [14336, 8192], P('cols'), may hold values from -0.125 to 0.125
- gate_mask: int32 [128, 224], P('rows', 'cols'), may hold values 0 or 1
- up_mask: int32 [128, 224], P('rows', 'cols'), may hold values 0 or 1
- down_mask: int32 [224, 128], P('cols'), may hold values 0 or 1
Outputs:
- branch_out: bfloat16 [5120, 8192], P(('rows', 'cols'))
The draws below stay inside these ranges and needn't reach their ends.
All inputs are finite; a program needn't handle non-finite values. No bound on the sum of `gate_mask` or of `up_mask` or of `down_mask` on one device may be relied on, other than what follows from the above.
Results may differ from the reference program's by a relative error of at most 0.025.
Values may be sent and summed in bfloat16 or wider, within the bound.
A program may use at most 192 MiB of HBM per device.

```python
import jax
import jax.numpy as jnp
from jax import lax

D = 8192
FF = 14336
BLOCK = 64
TOKENS = 5120
N_ROWS = 8
N_COLS = 16


def plant(entries, own_key, low, top_value):
    shape = entries.shape
    spot = [jax.random.randint(jax.random.fold_in(own_key, axis), (), 0, shape[axis]) for axis in range(len(shape))]
    entries = entries.at[tuple(spot)].set(low)
    longest = shape.index(max(shape))
    spot[longest] = (spot[longest] + 1) % shape[longest]
    return entries.at[tuple(spot)].set(top_value)


def levels(stream_key, shape, split, smallest, high):
    level = 1.0
    for position, shards_of in split:
        draws = jax.random.uniform(jax.random.fold_in(jax.random.fold_in(stream_key, 6), position), (shards_of,), jnp.float32, smallest / len(split), high / len(split))
        level = level * jnp.repeat(jnp.exp(draws), shape[position] // shards_of).reshape((-1,) + (1,) * (len(shape) - 1 - position))
    return level


def normal_values(key, dims, deviation, limit, pieces=(), kind=jnp.bfloat16):
    gain = levels(key, dims, pieces, -0.22, 0.18) if pieces else 1.0
    drawn = jax.random.normal(key, dims, jnp.float32) * deviation * gain
    return jnp.minimum(jnp.maximum(drawn, -limit), limit).astype(kind)


def setup_inputs(seed: int = 0) -> dict:
    streams_of = jax.random.split(jax.random.key(seed), 9)
    return {
        "tokens": normal_values(streams_of[0], (TOKENS, D), 1.0, 6.0, ((0, 128),)),
        "norm_gain": jnp.clip(1.0 + 0.18 * jax.random.normal(streams_of[1], (D,), jnp.float32), 0.1, 1.9),
        "gate_weight": normal_values(streams_of[2], (D, FF), (D // 2) ** -0.5, 0.09375, ((0, 8), (1, 16))),
        "up_weight": normal_values(streams_of[3], (D, FF), (D // 2) ** -0.5, 0.09375, ((0, 8), (1, 16))),
        "down_weight": normal_values(streams_of[4], (FF, D), (FF // 8) ** -0.5, 0.125, ((0, 16),)),
        "gate_mask": plant((jax.random.randint(streams_of[5], (D // BLOCK, FF // BLOCK), 0, 2) < 1).astype(jnp.int32), jax.random.fold_in(streams_of[5], 1), 0, 1),
        "up_mask": plant((jax.random.randint(streams_of[6], (D // BLOCK, FF // BLOCK), 0, 2) < 1).astype(jnp.int32), jax.random.fold_in(streams_of[6], 1), 0, 1),
        "down_mask": plant((jax.random.randint(streams_of[7], (FF // BLOCK, D // BLOCK), 0, 2) < 1).astype(jnp.int32), jax.random.fold_in(streams_of[7], 1), 0, 1),
    }


def expand(mask):
    return jnp.repeat(jnp.repeat(mask, BLOCK, 0), BLOCK, 1).astype(jnp.bfloat16)

def grouped_sum(left, right, groups):
    inner = left.shape[1] // groups
    left_groups = jnp.transpose(left.reshape(left.shape[0], groups, inner), (1, 0, 2))
    right_groups = right.reshape(groups, inner, right.shape[1])

    def add_group(total, pair):
        part = jnp.dot(pair[0], pair[1], preferred_element_type=jnp.float32).astype(jnp.bfloat16)
        part = lax.optimization_barrier(part)
        return (total + part.astype(jnp.float32), None)
    start = jnp.zeros((left.shape[0], right.shape[1]), jnp.float32)
    total, _ = lax.scan(add_group, start, (left_groups, right_groups))
    return total

def reference(tokens, norm_gain, gate_weight, up_weight, down_weight, gate_mask, up_mask, down_mask):
    values = tokens.astype(jnp.float32)
    meansq = lax.optimization_barrier(jnp.mean(values * values, axis=-1, keepdims=True))
    normed = (values * lax.rsqrt(meansq + 1e-05) * norm_gain).astype(jnp.bfloat16)
    gate_kept = gate_weight * expand(gate_mask)
    up_kept = up_weight * expand(up_mask)
    down_kept = down_weight * expand(down_mask)
    gate = grouped_sum(normed, gate_kept, N_ROWS)
    up = grouped_sum(normed, up_kept, N_ROWS)
    hidden = (jax.nn.silu(gate) * up).astype(jnp.bfloat16)
    total = grouped_sum(hidden, down_kept, N_COLS)
    return total.astype(jnp.bfloat16)
```

```python
import functools

import jax
import jax.numpy as jnp
from jax import lax
from jax.experimental import pallas as pl
from jax.experimental.pallas import tpu as pltpu
from jax.sharding import PartitionSpec as P

BLOCK = 64
STAGES = 5
SUB = 8
RING = 4
TILE = 2 * SUB
MESH = pl.DeviceIdType.MESH
BF16, F32 = jnp.bfloat16, jnp.float32


def kernel(
    tok, gain, gate_w, up_w, down_w, gate_m, up_m, down_m, out,
    toks, sent, mixed, gath, wgu, wd, mgu, md, part, mate, xrel, xfin, hid,
    outp, yrel, yfin, ysum, y2rel, y2fin, res, obuf,
    ld_sem, a2a_s, a2a_r, ag_s, ag_r, q_s, q_r, xr_s, xr_r, h_s, h_r, yr_s, yr_r, o_s, o_r,
):
    r, c = lax.axis_index("rows"), lax.axis_index("cols")
    x, q = r // 2, r % 2
    z, y = c // RING, c % RING
    width = wgu.shape[1] // 2
    feats = wgu.shape[0]
    half_d = wd.shape[1]
    col_h = half_d // 2
    rows_h = part.shape[2] // 2
    rel = rows_h // 2

    def nb(v, d):
        return (v + d + RING) % RING

    def dev_x(d):
        return {"rows": nb(x, d) * 2 + q, "cols": c}

    def dev_yz(axis, d):
        if axis == "y":
            return {"rows": r, "cols": z * RING + nb(y, d)}
        return {"rows": r, "cols": nb(z, d) * RING + y}

    partner = {"rows": x * 2 + (1 - q), "cols": c}

    def copy(src, dst, ss, rs, dev):
        return pltpu.make_async_remote_copy(
            src_ref=src, dst_ref=dst, send_sem=ss, recv_sem=rs, device_id=dev, device_id_type=MESH
        )

    def send(src, dst, ss, rs, dev):
        copy(src, dst, ss, rs, dev).start()

    def got(dst, ss, rs):
        copy(dst, dst, ss, rs, partner).wait_recv()

    def left(src, ss, rs):
        copy(src, src, ss, rs, partner).wait_send()

    ld_tok = pltpu.make_async_copy(tok, toks, ld_sem.at[0])
    ld_gate = pltpu.make_async_copy(gate_w, wgu.at[:, pl.ds(0, width)], ld_sem.at[1])
    ld_up = pltpu.make_async_copy(up_w, wgu.at[:, pl.ds(width, width)], ld_sem.at[2])
    ld_down = pltpu.make_async_copy(
        down_w.at[:, pl.ds(pl.multiple_of(q * half_d, half_d), half_d)], wd, ld_sem.at[3]
    )
    ld_tok.start()
    ld_gate.start()
    ld_up.start()
    ld_down.start()

    barrier = pltpu.get_barrier_semaphore()

    def row_peer(i):
        return (r + i) % (2 * RING)

    for i in range(1, 2 * RING):
        pl.semaphore_signal(barrier, inc=1, device_id={"rows": row_peer(i), "cols": c}, device_id_type=MESH)
    for axis in ("y", "z"):
        for d in (1, -1):
            pl.semaphore_signal(barrier, inc=1, device_id=dev_yz(axis, d), device_id_type=MESH)

    ld_tok.wait()

    def norm(k, carry):
        values = toks[k].astype(F32)
        meansq = jnp.mean(values * values, axis=-1, keepdims=True)
        sent[k] = (values * lax.rsqrt(meansq + 1e-05) * gain[...]).astype(BF16)
        return carry

    lax.fori_loop(0, STAGES, norm, 0)
    pl.semaphore_wait(barrier, 2 * RING + 3)

    spans = ((0, 1), (1, STAGES - 1))
    for s, (first, count) in enumerate(spans):
        for i in range(1, 2 * RING):
            peer = row_peer(i)
            send(
                sent.at[pl.ds(first, count), :, pl.ds(pl.multiple_of(peer * feats, feats), feats)],
                mixed.at[pl.ds(first, count), x, q],
                a2a_s.at[s, i],
                a2a_r.at[s, i],
                {"rows": peer, "cols": c},
            )
    mixed[:, x, q] = sent[:, :, pl.ds(pl.multiple_of(r * feats, feats), feats)]

    def spread(mask, first, count):
        blocks = mask.shape[1]
        row = lax.broadcasted_iota(jnp.int32, (blocks, count * BLOCK), 0)
        col = lax.broadcasted_iota(jnp.int32, (blocks, count * BLOCK), 1)
        onehot = (row == col // BLOCK + first).astype(F32).astype(BF16)
        return jnp.dot(mask[...].astype(F32).astype(BF16), onehot, preferred_element_type=F32)

    mgu[:, 0:width] = spread(gate_m, 0, width // BLOCK)
    mgu[:, width : 2 * width] = spread(up_m, 0, width // BLOCK)
    ld_gate.wait()
    ld_up.wait()

    def keep_gu(b, carry):
        rows = pl.ds(pl.multiple_of(b * BLOCK, BLOCK), BLOCK)
        wgu[rows, :] = wgu[rows, :] * mgu[pl.ds(b, 1), :].astype(BF16)
        return carry

    lax.fori_loop(0, feats // BLOCK, keep_gu, 0)

    def keep_d(b, carry):
        rows = pl.ds(pl.multiple_of(b * BLOCK, BLOCK), BLOCK)
        wd[rows, :] = wd[rows, :] * md[pl.ds(b, 1), :].astype(BF16)
        return carry

    def a2a_wait(s):
        first, count = spans[s]
        for i in range(1, 2 * RING):
            origin = (r - i + 2 * RING) % (2 * RING)
            got(mixed.at[pl.ds(first, count), origin // 2, origin % 2], a2a_s.at[s, i], a2a_r.at[s, i])

    def block(k, xs, axis, i):
        return gath.at[k, xs, z, i] if axis == "y" else gath.at[k, xs, i, y]

    def slab(k, xs, axis, i):
        return gath.at[k, xs, i] if axis == "z" else gath.at[k, xs, :, i]

    def axes(h):
        return (("y", y), ("z", z)) if h == 0 else (("z", z), ("y", y))

    def both(h):
        return pl.ds(2 * h, 2)

    def ag0(k):
        for xi in range(RING):
            gath[k, xi, z, y] = jnp.concatenate([mixed[k, xi, 0], mixed[k, xi, 1]], axis=0)
        for h in range(2):
            (a, i), _ = axes(h)
            own = block(k, both(h), a, i)
            send(own, own, ag_s.at[k, h, 0], ag_r.at[k, h, 0], dev_yz(a, 1))
            send(own, own, ag_s.at[k, h, 1], ag_r.at[k, h, 1], dev_yz(a, -1))

    def ag1(k):
        for h in range(2):
            (a, i), _ = axes(h)
            for n, d in ((0, -1), (1, 1)):
                got(block(k, both(h), a, nb(i, d)), ag_s.at[k, h, n], ag_r.at[k, h, n])
                piece = block(k, 2 * h + n, a, nb(i, d))
                send(piece, piece, ag_s.at[k, h, 2 + n], ag_r.at[k, h, 2 + n], dev_yz(a, -d))

    def ag2(k):
        for h in range(2):
            (a, i), (b, j) = axes(h)
            for n in range(2):
                got(block(k, 2 * h + n, a, nb(i, 2)), ag_s.at[k, h, 2 + n], ag_r.at[k, h, 2 + n])
            own = slab(k, both(h), b, j)
            send(own, own, ag_s.at[k, h, 4], ag_r.at[k, h, 4], dev_yz(b, 1))
            send(own, own, ag_s.at[k, h, 5], ag_r.at[k, h, 5], dev_yz(b, -1))

    def ag3(k):
        for h in range(2):
            _, (b, j) = axes(h)
            for n, d in ((0, -1), (1, 1)):
                got(slab(k, both(h), b, nb(j, d)), ag_s.at[k, h, 4 + n], ag_r.at[k, h, 4 + n])
                piece = slab(k, 2 * h + n, b, nb(j, d))
                send(piece, piece, ag_s.at[k, h, 6 + n], ag_r.at[k, h, 6 + n], dev_yz(b, -d))

    def ag4(k):
        for h in range(2):
            _, (b, j) = axes(h)
            for n in range(2):
                got(slab(k, 2 * h + n, b, nb(j, 2)), ag_s.at[k, h, 6 + n], ag_r.at[k, h, 6 + n])

    def ag_left(k):
        for h in range(2):
            (a, i), (b, j) = axes(h)
            for n in range(2):
                left(block(k, both(h), a, i), ag_s.at[k, h, n], ag_r.at[k, h, n])
                left(block(k, 2 * h, a, i), ag_s.at[k, h, 2 + n], ag_r.at[k, h, 2 + n])
                left(slab(k, both(h), b, j), ag_s.at[k, h, 4 + n], ag_r.at[k, h, 4 + n])
                left(slab(k, 2 * h, b, j), ag_s.at[k, h, 6 + n], ag_r.at[k, h, 6 + n])

    order = (2, 1, -1, 0)
    mine = pl.multiple_of(q * rows_h, rows_h)
    theirs = pl.multiple_of((1 - q) * rows_h, rows_h)

    def gu_tile(k, n):
        xi, s = nb(x, order[n]), k % 2
        lhs = gath[k, xi].reshape(part.shape[2], feats)
        for j in range(0, 2 * width, 256):
            part[s, xi, :, pl.ds(j, 256)] = jnp.dot(
                lhs, wgu[:, pl.ds(j, 256)], preferred_element_type=F32
            ).astype(BF16)
        send(
            part.at[s, xi, pl.ds(theirs, rows_h)], mate.at[s, xi], q_s.at[k, n], q_r.at[k, n], partner
        )

    def add(ref_a, ref_b):
        return (ref_a[...].astype(F32) + ref_b[...].astype(F32)).astype(BF16)

    def xrows(s, d, lo, count):
        return part.at[s, nb(x, d), pl.ds(pl.multiple_of(mine + lo, rel), count)]

    def gu_finish(k, n):
        d, s = order[n], k % 2
        xi = nb(x, d)
        got(mate.at[s, xi], q_s.at[k, n], q_r.at[k, n])
        whole = xrows(s, d, 0, rows_h)
        whole[...] = add(whole, mate.at[s, xi])
        if d == 2:
            send(xrows(s, 2, 0, rel), xrel.at[k, 0], xr_s.at[k, 0], xr_r.at[k, 0], dev_x(1))
            send(xrows(s, 2, rel, rel), xrel.at[k, 1], xr_s.at[k, 1], xr_r.at[k, 1], dev_x(-1))
        elif d == 1:
            send(xrows(s, 1, rel, rel), xfin.at[k, 0, pl.ds(rel, rel)], xr_s.at[k, 2], xr_r.at[k, 2], dev_x(1))
        elif d == -1:
            send(xrows(s, -1, 0, rel), xfin.at[k, 1, pl.ds(0, rel)], xr_s.at[k, 3], xr_r.at[k, 3], dev_x(-1))

    def x_relay(k):
        s = k % 2
        for n, d in ((0, 1), (1, -1)):
            got(xrel.at[k, n], xr_s.at[k, n], xr_r.at[k, n])
            own = xrows(s, d, n * rel, rel)
            own[...] = add(own, xrel.at[k, n])
            send(own, xfin.at[k, n, pl.ds(n * rel, rel)], xr_s.at[k, 4 + n], xr_r.at[k, 4 + n], dev_x(d))

    def hidden(k):
        s = k % 2
        for n in range(4):
            lo = rel if n in (0, 3) else 0
            got(xfin.at[k, n % 2, pl.ds(lo, rel)], xr_s.at[k, 2 + n], xr_r.at[k, 2 + n])
        own = xrows(s, 0, 0, rows_h)

        def piece(i, carry):
            rows = pl.ds(pl.multiple_of(i * 16, 16), 16)

            def total(cols):
                return (
                    own[rows, cols].astype(F32)
                    + xfin[k, 0, rows, cols].astype(F32)
                    + xfin[k, 1, rows, cols].astype(F32)
                )

            gate, up = total(pl.ds(0, width)), total(pl.ds(width, width))
            act = gate / (1.0 + jnp.exp(-gate)) * up
            hid[k, pl.ds(pl.multiple_of(mine + i * 16, 16), 16), :] = act.astype(BF16)
            return carry

        lax.fori_loop(0, rows_h // 16, piece, 0)
        own_h = hid.at[k, pl.ds(mine, rows_h)]
        send(own_h, own_h, h_s.at[k], h_r.at[k], partner)

    def hidden_got(k):
        got(hid.at[k, pl.ds(theirs, rows_h)], h_s.at[k], h_r.at[k])

    def down_half(k, h):
        s = k % 2
        lhs = hid[k]
        for j in range(h * col_h, (h + 1) * col_h, 256):
            outp[s, :, :, :, pl.ds(j, 256)] = (
                jnp.dot(lhs, wd[:, pl.ds(j, 256)], preferred_element_type=F32)
                .astype(BF16)
                .reshape(RING, RING, TILE, 256)
            )

    halves = (pl.ds(0, 2), pl.ds(2, 2))
    cols2 = (pl.ds(0, col_h // 2), pl.ds(col_h // 2, col_h // 2))

    def chunk(k, h, i, others):
        cols = pl.ds(h * col_h, col_h)
        if h == 0:
            return outp.at[k % 2, i, others, :, cols]
        return outp.at[k % 2, others, i, :, cols]

    def raxes(h):
        return (("z", z), ("y", y)) if h == 0 else (("y", y), ("z", z))

    def yr0(k, h):
        (a, i), _ = raxes(h)
        ss, rs = yr_s.at[k, h, 0], yr_r.at[k, h, 0]
        send(chunk(k, h, nb(i, 2), halves[0]), yrel.at[k, h, 0], ss.at[0], rs.at[0], dev_yz(a, 1))
        send(chunk(k, h, nb(i, 2), halves[1]), yrel.at[k, h, 1], ss.at[1], rs.at[1], dev_yz(a, -1))
        send(chunk(k, h, nb(i, 1), halves[1]), yfin.at[k, h, 0, halves[1]], ss.at[2], rs.at[2], dev_yz(a, 1))
        send(chunk(k, h, nb(i, -1), halves[0]), yfin.at[k, h, 1, halves[0]], ss.at[3], rs.at[3], dev_yz(a, -1))

    def yr1(k, h):
        (a, i), _ = raxes(h)
        ss, rs = yr_s.at[k, h, 0], yr_r.at[k, h, 0]
        for n, d in ((0, 1), (1, -1)):
            got(yrel.at[k, h, n], ss.at[n], rs.at[n])
            own = chunk(k, h, nb(i, d), halves[n])
            own[...] = add(own, yrel.at[k, h, n])
            send(own, yfin.at[k, h, n, halves[n]], ss.at[4 + n], rs.at[4 + n], dev_yz(a, d))

    def yr2(k, h):
        (a, i), (b, j) = raxes(h)
        ss, rs = yr_s.at[k, h, 0], yr_r.at[k, h, 0]
        for n in range(4):
            got(yfin.at[k, h, n % 2, halves[1 if n in (0, 3) else 0]], ss.at[2 + n], rs.at[2 + n])
        own = chunk(k, h, i, pl.ds(0, RING))
        for o in range(RING):
            ysum[k % 2, h, o] = (
                own[o].astype(F32) + yfin[k, h, 0, o].astype(F32) + yfin[k, h, 1, o].astype(F32)
            ).astype(BF16)
        ss, rs = yr_s.at[k, h, 1], yr_r.at[k, h, 1]

        def sums(i, n):
            return ysum.at[k % 2, h, i, :, cols2[n]]

        send(sums(nb(j, 2), 0), y2rel.at[k, h, 0], ss.at[0], rs.at[0], dev_yz(b, 1))
        send(sums(nb(j, 2), 1), y2rel.at[k, h, 1], ss.at[1], rs.at[1], dev_yz(b, -1))
        send(sums(nb(j, 1), 1), y2fin.at[k, h, 0, :, cols2[1]], ss.at[2], rs.at[2], dev_yz(b, 1))
        send(sums(nb(j, -1), 0), y2fin.at[k, h, 1, :, cols2[0]], ss.at[3], rs.at[3], dev_yz(b, -1))

    def yr3(k, h):
        _, (b, j) = raxes(h)
        ss, rs = yr_s.at[k, h, 1], yr_r.at[k, h, 1]
        for n, d in ((0, 1), (1, -1)):
            got(y2rel.at[k, h, n], ss.at[n], rs.at[n])
            own = ysum.at[k % 2, h, nb(j, d), :, cols2[n]]
            own[...] = add(own, y2rel.at[k, h, n])
            send(own, y2fin.at[k, h, n, :, cols2[n]], ss.at[4 + n], rs.at[4 + n], dev_yz(b, d))

    def yr4(k, h):
        _, (b, j) = raxes(h)
        ss, rs = yr_s.at[k, h, 1], yr_r.at[k, h, 1]
        for n in range(4):
            got(y2fin.at[k, h, n % 2, :, cols2[1 if n in (0, 3) else 0]], ss.at[2 + n], rs.at[2 + n])
        total = (
            ysum[k % 2, h, j].astype(F32) + y2fin[k, h, 0].astype(F32) + y2fin[k, h, 1].astype(F32)
        )
        top, bottom = total[0:SUB], total[SUB:TILE]
        first = q == 0
        res[k, :, pl.ds(pl.multiple_of(q * half_d + h * col_h, col_h), col_h)] = jnp.where(first, top, bottom).astype(BF16)
        obuf[k, :, pl.ds(h * col_h, col_h)] = jnp.where(first, bottom, top).astype(BF16)

    def swap(k):
        send(
            obuf.at[k],
            res.at[k, :, pl.ds(pl.multiple_of(q * half_d, half_d), half_d)],
            o_s.at[k],
            o_r.at[k],
            partner,
        )

    def swap_got(k):
        got(res.at[k, :, pl.ds(pl.multiple_of((1 - q) * half_d, half_d), half_d)], o_s.at[k], o_r.at[k])

    def x_left(k):
        for n in range(4):
            left(mate.at[0, 0], q_s.at[k, n], q_r.at[k, n])
        for n in range(6):
            left(xrel.at[0, 0], xr_s.at[k, n], xr_r.at[k, n])

    def y_left(k):
        for h in range(2):
            for n in range(6):
                left(yrel.at[k, h, 0], yr_s.at[k, h, 0, n], yr_r.at[k, h, 0, n])
                left(y2rel.at[k, h, 0], yr_s.at[k, h, 1, n], yr_r.at[k, h, 1, n])

    def at(k, step, *args):
        @pl.when((k >= 0) & (k < STAGES))
        def _():
            step(k, *args)

    a2a_wait(0)
    ag0(0)
    md[...] = spread(down_m, q * (half_d // BLOCK), half_d // BLOCK)
    a2a_wait(1)
    ag1(0)
    ag0(1)
    ag2(0)
    ld_down.wait()
    lax.fori_loop(0, wd.shape[0] // BLOCK, keep_d, 0)
    ag3(0)
    ag1(1)

    def iteration(t, carry):
        at(t, ag4)
        at(t + 1, ag2)
        at(t - 2, x_left)
        at(t, gu_tile, 0)
        at(t + 2, ag0)
        at(t - 2, yr1, 0)
        at(t - 2, yr1, 1)
        at(t, gu_tile, 1)
        at(t, gu_finish, 0)
        at(t + 1, ag3)
        at(t, gu_tile, 2)
        at(t, gu_finish, 1)
        at(t + 2, ag1)
        at(t - 2, yr2, 0)
        at(t - 2, yr2, 1)
        at(t, gu_tile, 3)
        at(t, gu_finish, 2)
        at(t - 1, hidden)
        at(t, gu_finish, 3)
        at(t - 2, yr3, 0)
        at(t - 2, yr3, 1)
        at(t - 3, y_left)
        at(t - 1, hidden_got)
        at(t - 1, down_half, 0)
        at(t - 1, yr0, 0)
        at(t, x_relay)
        at(t - 1, down_half, 1)
        at(t - 1, yr0, 1)
        at(t - 2, yr4, 0)
        at(t - 2, yr4, 1)
        at(t - 2, swap)
        return carry

    lax.fori_loop(0, STAGES + 2, iteration, 0)

    y_left(STAGES - 1)

    def finish(k, carry):
        swap_got(k)
        ag_left(k)
        left(hid.at[k, pl.ds(mine, rows_h)], h_s.at[k], h_r.at[k])
        left(obuf.at[k], o_s.at[k], o_r.at[k])
        return carry

    lax.fori_loop(0, STAGES, finish, 0)
    store = pltpu.make_async_copy(res, out, ld_sem.at[4])
    store.start()
    for s, (first, count) in enumerate(spans):
        for i in range(1, 2 * RING):
            left(mixed.at[pl.ds(first, count), 0, 0], a2a_s.at[s, i], a2a_r.at[s, i])
    store.wait()


def body(tokens, norm_gain, gate_weight, up_weight, down_weight, gate_mask, up_mask, down_mask):
    own, model = tokens.shape
    feats, width = gate_weight.shape
    half_d = model // 2
    rows = RING * RING * TILE
    dma = pltpu.SemaphoreType.DMA
    vmem, anyspace = pl.BlockSpec(memory_space=pltpu.VMEM), pl.BlockSpec(memory_space=pl.ANY)
    result = pl.pallas_call(
        kernel,
        out_shape=jax.ShapeDtypeStruct((STAGES, SUB, model), BF16),
        in_specs=[anyspace, vmem, anyspace, anyspace, anyspace, vmem, vmem, vmem],
        out_specs=anyspace,
        scratch_shapes=[
            pltpu.VMEM((STAGES, SUB, model), BF16),
            pltpu.VMEM((STAGES, SUB, model), BF16),
            pltpu.VMEM((STAGES, RING, 2, SUB, feats), BF16),
            pltpu.VMEM((STAGES, RING, RING, RING, TILE, feats), BF16),
            pltpu.VMEM((feats, 2 * width), BF16),
            pltpu.VMEM((width, half_d), BF16),
            pltpu.VMEM((feats // BLOCK, 2 * width), F32),
            pltpu.VMEM((width // BLOCK, half_d), F32),
            pltpu.VMEM((2, RING, rows, 2 * width), BF16),
            pltpu.VMEM((2, RING, rows // 2, 2 * width), BF16),
            pltpu.VMEM((STAGES, 2, rows // 4, 2 * width), BF16),
            pltpu.VMEM((STAGES, 2, rows // 2, 2 * width), BF16),
            pltpu.VMEM((STAGES, rows, width), BF16),
            pltpu.VMEM((2, RING, RING, TILE, half_d), BF16),
            pltpu.VMEM((STAGES, 2, 2, 2, TILE, half_d // 2), BF16),
            pltpu.VMEM((STAGES, 2, 2, RING, TILE, half_d // 2), BF16),
            pltpu.VMEM((2, 2, RING, TILE, half_d // 2), BF16),
            pltpu.VMEM((STAGES, 2, 2, TILE, half_d // 4), BF16),
            pltpu.VMEM((STAGES, 2, 2, TILE, half_d // 2), BF16),
            pltpu.VMEM((STAGES, SUB, model), BF16),
            pltpu.VMEM((STAGES, SUB, half_d), BF16),
            dma((5,)),
            dma((2, 2 * RING)),
            dma((2, 2 * RING)),
            dma((STAGES, 2, 8)),
            dma((STAGES, 2, 8)),
            dma((STAGES, 4)),
            dma((STAGES, 4)),
            dma((STAGES, 6)),
            dma((STAGES, 6)),
            dma((STAGES,)),
            dma((STAGES,)),
            dma((STAGES, 2, 2, 6)),
            dma((STAGES, 2, 2, 6)),
            dma((STAGES,)),
            dma((STAGES,)),
        ],
        compiler_params=pltpu.CompilerParams(
            collective_id=0, has_side_effects=True, vmem_limit_bytes=67_000_000
        ),
    )(
        tokens.reshape(STAGES, SUB, model),
        norm_gain.reshape(1, model),
        gate_weight,
        up_weight,
        down_weight,
        gate_mask,
        up_mask,
        down_mask,
    )
    return result.reshape(own, model)


def solution(mesh):
    return jax.shard_map(
        body,
        mesh=mesh,
        in_specs=(
            P(("rows", "cols"), None),
            P(),
            P("rows", "cols"),
            P("rows", "cols"),
            P("cols", None),
            P("rows", "cols"),
            P("rows", "cols"),
            P("cols", None),
        ),
        out_specs=P(("rows", "cols"), None),
        check_vma=False,
    )
```

```python
import functools

import jax
import jax.numpy as jnp
from jax import lax
from jax.experimental import pallas as pl
from jax.experimental.pallas import tpu as pltpu
from jax.sharding import PartitionSpec as P

BLOCK = 64
STAGES = 5
SUB = 8
RING = 4
TILE = 2 * SUB
MESH = pl.DeviceIdType.MESH
BF16, F32 = jnp.bfloat16, jnp.float32

ORDER = (
    ("ag0", 0), ("ag1", 0, 0, 0), ("ag1", 0, 0, 1), ("ag1", 0, 1, 0), ("ag1", 0, 1, 1), ("ag0", 1), ("ag2", 0, 0),
    ("ag2", 0, 1), ("ag1", 1, 0, 0), ("ag1", 1, 0, 1), ("ag1", 1, 1, 0), ("ag1", 1, 1, 1), ("ag0", 2),
    ("ag3", 0, 0, 0), ("ag3", 0, 0, 1), ("ag3", 0, 1, 0), ("ag3", 0, 1, 1), ("ag2", 1, 1), ("ag2", 1, 0),
    ("ag1", 2, 1, 0), ("ag1", 2, 0, 0), ("ag1", 2, 0, 1), ("ag1", 2, 1, 1), ("ag0", 3), ("ag4", 0), ("gu", 0, 0),
    ("gu", 0, 1), ("gu", 0, 2), ("gf", 0, 0), ("gu", 0, 3), ("gf", 0, 1), ("ag3", 1, 0, 0), ("ag3", 1, 0, 1),
    ("ag3", 1, 1, 0), ("ag3", 1, 1, 1), ("gf", 0, 2), ("ag2", 2, 0), ("ag2", 2, 1), ("gf", 0, 3), ("ag1", 3, 0, 0),
    ("ag1", 3, 0, 1), ("ag1", 3, 1, 0), ("ag1", 3, 1, 1), ("ag0", 4), ("ag4", 1), ("xr", 0, 0), ("xr", 0, 1),
    ("gu", 1, 0), ("gu", 1, 1), ("gu", 1, 2), ("gf", 1, 0), ("gu", 1, 3), ("ag3", 2, 0, 0), ("ag3", 2, 0, 1),
    ("ag3", 2, 1, 0), ("ag3", 2, 1, 1), ("gf", 1, 1), ("gf", 1, 2), ("ag2", 3, 0), ("ag2", 3, 1), ("ag1", 4, 1, 0),
    ("gf", 1, 3), ("ag1", 4, 0, 0), ("ag1", 4, 0, 1), ("ag1", 4, 1, 1), ("hid", 0), ("ag4", 2), ("hg", 0),
    ("xleft", 0), ("dn", 0, 0), ("dn", 0, 1), ("xr", 1, 0), ("xr", 1, 1), ("gu", 2, 0), ("ag3", 3, 0, 0),
    ("ag3", 3, 0, 1), ("ag3", 3, 1, 0), ("ag3", 3, 1, 1), ("gu", 2, 1), ("gu", 2, 2), ("yr1", 0, 0, 0),
    ("yr1", 0, 0, 1), ("yr1", 0, 1, 0), ("yr1", 0, 1, 1), ("gf", 2, 0), ("gf", 2, 1), ("gf", 2, 2), ("gu", 2, 3),
    ("ag2", 4, 0), ("ag2", 4, 1), ("hid", 1), ("gf", 2, 3), ("ag4", 3), ("hg", 1), ("xleft", 1), ("dn", 1, 0),
    ("dn", 1, 1), ("xr", 2, 0), ("xr", 2, 1), ("yr2", 0, 0), ("yr2", 0, 1), ("gu", 3, 0), ("gu", 3, 1),
    ("ag3", 4, 0, 0), ("ag3", 4, 0, 1), ("gu", 3, 2), ("ag3", 4, 1, 0), ("ag3", 4, 1, 1), ("gf", 3, 0), ("gu", 3, 3),
    ("yr1", 1, 0, 0), ("yr1", 1, 0, 1), ("yr1", 1, 1, 0), ("yr1", 1, 1, 1), ("gf", 3, 1), ("gf", 3, 2), ("gf", 3, 3),
    ("hid", 2), ("yr3", 0, 1, 0), ("yr3", 0, 1, 1), ("yr3", 0, 0, 0), ("yr3", 0, 0, 1), ("yleft", 0), ("hg", 2),
    ("xleft", 2), ("dn", 2, 0), ("dn", 2, 1), ("xr", 3, 0), ("xr", 3, 1), ("ag4", 4), ("gu", 4, 0), ("yr2", 1, 0),
    ("yr4", 0, 1), ("yr2", 1, 1), ("yr4", 0, 0), ("swap", 0), ("gf", 4, 0), ("gu", 4, 1), ("yr1", 2, 0, 0),
    ("yr1", 2, 0, 1), ("yr1", 2, 1, 0), ("yr1", 2, 1, 1), ("gu", 4, 2), ("gf", 4, 1), ("gu", 4, 3), ("yr3", 1, 1, 0),
    ("yr3", 1, 1, 1), ("yr3", 1, 0, 0), ("yr3", 1, 0, 1), ("hid", 3), ("yleft", 1), ("gf", 4, 2), ("gf", 4, 3),
    ("hg", 3), ("xleft", 3), ("dn", 3, 0), ("dn", 3, 1), ("xr", 4, 0), ("xr", 4, 1), ("yr4", 1, 0), ("yr4", 1, 1),
    ("swap", 1), ("yr2", 2, 0), ("yr2", 2, 1), ("yr1", 3, 0, 0), ("yr1", 3, 0, 1), ("yr1", 3, 1, 0), ("yr1", 3, 1, 1),
    ("yr3", 2, 1, 0), ("yr3", 2, 1, 1), ("yr3", 2, 0, 0), ("yr3", 2, 0, 1), ("yleft", 2), ("hid", 4), ("yr2", 3, 0),
    ("yr4", 2, 1), ("hg", 4), ("xleft", 4), ("dn", 4, 0), ("dn", 4, 1), ("yr3", 3, 0, 0), ("yr3", 3, 0, 1),
    ("yr2", 3, 1), ("yr4", 2, 0), ("swap", 2), ("yr1", 4, 0, 0), ("yr1", 4, 0, 1), ("yr1", 4, 1, 0), ("yr1", 4, 1, 1),
    ("yr3", 3, 1, 0), ("yr3", 3, 1, 1), ("yleft", 3), ("yr4", 3, 0), ("yr2", 4, 0), ("yr2", 4, 1), ("yr4", 3, 1),
    ("swap", 3), ("yr3", 4, 0, 0), ("yr3", 4, 0, 1), ("yr3", 4, 1, 0), ("yr3", 4, 1, 1), ("yleft", 4), ("yr4", 4, 0),
    ("yr4", 4, 1), ("swap", 4),
)


def kernel(
    tok, gain, gate_w, up_w, down_w, gate_m, up_m, down_m, out,
    toks, sent, mixed, gath, wgu, wd, mgu, md, part, mate, xrel, xfin, hid,
    outp, yrel, yfin, ysum, y2rel, y2fin, res, obuf,
    ld_sem, a2a_s, a2a_r, ag_s, ag_r, q_s, q_r, xr_s, xr_r, h_s, h_r, yr_s, yr_r, o_s, o_r,
):
    r, c = lax.axis_index("rows"), lax.axis_index("cols")
    x, q = r // 2, r % 2
    z, y = c // RING, c % RING
    width = wgu.shape[1] // 2
    feats = wgu.shape[0]
    half_d = wd.shape[1]
    col_h = half_d // 2
    rows_h = part.shape[2] // 2
    rel = rows_h // 2

    def nb(v, d):
        return (v + d + RING) % RING

    def dev_x(d):
        return {"rows": nb(x, d) * 2 + q, "cols": c}

    def dev_yz(axis, d):
        if axis == "y":
            return {"rows": r, "cols": z * RING + nb(y, d)}
        return {"rows": r, "cols": nb(z, d) * RING + y}

    partner = {"rows": x * 2 + (1 - q), "cols": c}

    def copy(src, dst, ss, rs, dev):
        return pltpu.make_async_remote_copy(
            src_ref=src, dst_ref=dst, send_sem=ss, recv_sem=rs, device_id=dev, device_id_type=MESH
        )

    def send(src, dst, ss, rs, dev):
        copy(src, dst, ss, rs, dev).start()

    def got(dst, ss, rs):
        copy(dst, dst, ss, rs, partner).wait_recv()

    def left(src, ss, rs):
        copy(src, src, ss, rs, partner).wait_send()

    ld_tok = pltpu.make_async_copy(tok, toks, ld_sem.at[0])
    ld_gate = pltpu.make_async_copy(gate_w, wgu.at[:, pl.ds(0, width)], ld_sem.at[1])
    ld_up = pltpu.make_async_copy(up_w, wgu.at[:, pl.ds(width, width)], ld_sem.at[2])
    ld_down = pltpu.make_async_copy(
        down_w.at[:, pl.ds(pl.multiple_of(q * half_d, half_d), half_d)], wd, ld_sem.at[3]
    )
    ld_tok.start()
    ld_gate.start()
    ld_up.start()
    ld_down.start()

    barrier = pltpu.get_barrier_semaphore()

    def row_peer(i):
        return (r + i) % (2 * RING)

    for i in range(1, 2 * RING):
        pl.semaphore_signal(barrier, inc=1, device_id={"rows": row_peer(i), "cols": c}, device_id_type=MESH)
    for axis in ("y", "z"):
        for d in (1, -1):
            pl.semaphore_signal(barrier, inc=1, device_id=dev_yz(axis, d), device_id_type=MESH)

    ld_tok.wait()

    def norm(k, carry):
        values = toks[k].astype(F32)
        meansq = jnp.mean(values * values, axis=-1, keepdims=True)
        sent[k] = (values * lax.rsqrt(meansq + 1e-05) * gain[...]).astype(BF16)
        return carry

    norm(0, 0)
    pl.semaphore_wait(barrier, 2 * RING + 3)

    spans = ((0, 1), (1, STAGES - 1))
    for s, (first, count) in enumerate(spans):
        if s == 1:
            lax.fori_loop(1, STAGES, norm, 0)
        for i in range(1, 2 * RING):
            peer = row_peer(i)
            send(
                sent.at[pl.ds(first, count), :, pl.ds(pl.multiple_of(peer * feats, feats), feats)],
                mixed.at[pl.ds(first, count), x, q],
                a2a_s.at[s, i],
                a2a_r.at[s, i],
                {"rows": peer, "cols": c},
            )
    mixed[:, x, q] = sent[:, :, pl.ds(pl.multiple_of(r * feats, feats), feats)]

    def spread(mask, first, count):
        blocks = mask.shape[1]
        row = lax.broadcasted_iota(jnp.int32, (blocks, count * BLOCK), 0)
        col = lax.broadcasted_iota(jnp.int32, (blocks, count * BLOCK), 1)
        onehot = (row == col // BLOCK + first).astype(F32).astype(BF16)
        return jnp.dot(mask[...].astype(F32).astype(BF16), onehot, preferred_element_type=F32)

    mgu[:, 0:width] = spread(gate_m, 0, width // BLOCK)
    mgu[:, width : 2 * width] = spread(up_m, 0, width // BLOCK)
    ld_gate.wait()
    ld_up.wait()

    def keep_gu(b, carry):
        rows = pl.ds(pl.multiple_of(b * BLOCK, BLOCK), BLOCK)
        wgu[rows, :] = wgu[rows, :] * mgu[pl.ds(b, 1), :].astype(BF16)
        return carry

    lax.fori_loop(0, feats // BLOCK, keep_gu, 0)

    def keep_d(b, carry):
        rows = pl.ds(pl.multiple_of(b * BLOCK, BLOCK), BLOCK)
        wd[rows, :] = wd[rows, :] * md[pl.ds(b, 1), :].astype(BF16)
        return carry

    def a2a_wait(s):
        first, count = spans[s]
        for i in range(1, 2 * RING):
            origin = (r - i + 2 * RING) % (2 * RING)
            got(mixed.at[pl.ds(first, count), origin // 2, origin % 2], a2a_s.at[s, i], a2a_r.at[s, i])

    def block(k, xs, axis, i):
        return gath.at[k, xs, z, i] if axis == "y" else gath.at[k, xs, i, y]

    def slab(k, xs, axis, i):
        return gath.at[k, xs, i] if axis == "z" else gath.at[k, xs, :, i]

    def axes(h):
        return (("y", y), ("z", z)) if h == 0 else (("z", z), ("y", y))

    def both(h):
        return pl.ds(2 * h, 2)

    def ag0(k):
        for xi in range(RING):
            gath[k, xi, z, y] = jnp.concatenate([mixed[k, xi, 0], mixed[k, xi, 1]], axis=0)
        for h in range(2):
            (a, i), _ = axes(h)
            own = block(k, both(h), a, i)
            send(own, own, ag_s.at[k, h, 0], ag_r.at[k, h, 0], dev_yz(a, 1))
            send(own, own, ag_s.at[k, h, 1], ag_r.at[k, h, 1], dev_yz(a, -1))

    def ag1(k, h, n):
        (a, i), _ = axes(h)
        d = 2 * n - 1
        got(block(k, both(h), a, nb(i, d)), ag_s.at[k, h, n], ag_r.at[k, h, n])
        piece = block(k, 2 * h + n, a, nb(i, d))
        send(piece, piece, ag_s.at[k, h, 2 + n], ag_r.at[k, h, 2 + n], dev_yz(a, -d))

    def ag2(k, h):
        (a, i), (b, j) = axes(h)
        for n in range(2):
            got(block(k, 2 * h + n, a, nb(i, 2)), ag_s.at[k, h, 2 + n], ag_r.at[k, h, 2 + n])
        own = slab(k, both(h), b, j)
        send(own, own, ag_s.at[k, h, 4], ag_r.at[k, h, 4], dev_yz(b, 1))
        send(own, own, ag_s.at[k, h, 5], ag_r.at[k, h, 5], dev_yz(b, -1))

    def ag3(k, h, n):
        _, (b, j) = axes(h)
        d = 2 * n - 1
        got(slab(k, both(h), b, nb(j, d)), ag_s.at[k, h, 4 + n], ag_r.at[k, h, 4 + n])
        piece = slab(k, 2 * h + n, b, nb(j, d))
        send(piece, piece, ag_s.at[k, h, 6 + n], ag_r.at[k, h, 6 + n], dev_yz(b, -d))

    def ag4(k):
        for h in range(2):
            _, (b, j) = axes(h)
            for n in range(2):
                got(slab(k, 2 * h + n, b, nb(j, 2)), ag_s.at[k, h, 6 + n], ag_r.at[k, h, 6 + n])

    def ag_left(k):
        for h in range(2):
            (a, i), (b, j) = axes(h)
            for n in range(2):
                left(block(k, both(h), a, i), ag_s.at[k, h, n], ag_r.at[k, h, n])
                left(block(k, 2 * h, a, i), ag_s.at[k, h, 2 + n], ag_r.at[k, h, 2 + n])
                left(slab(k, both(h), b, j), ag_s.at[k, h, 4 + n], ag_r.at[k, h, 4 + n])
                left(slab(k, 2 * h, b, j), ag_s.at[k, h, 6 + n], ag_r.at[k, h, 6 + n])

    order = (2, 1, -1, 0)
    mine = pl.multiple_of(q * rows_h, rows_h)
    theirs = pl.multiple_of((1 - q) * rows_h, rows_h)

    def gu_tile(k, n):
        xi, s = nb(x, order[n]), k % 2
        lhs = gath[k, xi].reshape(part.shape[2], feats)

        def columns(j, carry):
            cols = pl.ds(pl.multiple_of(j * 256, 256), 256)
            part[s, xi, :, cols] = jnp.dot(lhs, wgu[:, cols], preferred_element_type=F32).astype(BF16)
            return carry

        lax.fori_loop(0, 2 * width // 256, columns, 0)
        send(
            part.at[s, xi, pl.ds(theirs, rows_h)], mate.at[s, xi], q_s.at[k, n], q_r.at[k, n], partner
        )

    def add(ref_a, ref_b):
        return (ref_a[...].astype(F32) + ref_b[...].astype(F32)).astype(BF16)

    def xrows(s, d, lo, count):
        return part.at[s, nb(x, d), pl.ds(pl.multiple_of(mine + lo, rel), count)]

    def gu_finish(k, n):
        d, s = order[n], k % 2
        xi = nb(x, d)
        got(mate.at[s, xi], q_s.at[k, n], q_r.at[k, n])
        whole = xrows(s, d, 0, rows_h)
        whole[...] = add(whole, mate.at[s, xi])
        if d == 2:
            send(xrows(s, 2, 0, rel), xrel.at[k, 0], xr_s.at[k, 0], xr_r.at[k, 0], dev_x(1))
            send(xrows(s, 2, rel, rel), xrel.at[k, 1], xr_s.at[k, 1], xr_r.at[k, 1], dev_x(-1))
        elif d == 1:
            send(xrows(s, 1, rel, rel), xfin.at[k, 0, pl.ds(rel, rel)], xr_s.at[k, 2], xr_r.at[k, 2], dev_x(1))
        elif d == -1:
            send(xrows(s, -1, 0, rel), xfin.at[k, 1, pl.ds(0, rel)], xr_s.at[k, 3], xr_r.at[k, 3], dev_x(-1))

    def x_relay(k, n):
        s, d = k % 2, 1 - 2 * n
        got(xrel.at[k, n], xr_s.at[k, n], xr_r.at[k, n])
        own = xrows(s, d, n * rel, rel)
        own[...] = add(own, xrel.at[k, n])
        send(own, xfin.at[k, n, pl.ds(n * rel, rel)], xr_s.at[k, 4 + n], xr_r.at[k, 4 + n], dev_x(d))

    def hidden(k):
        s = k % 2
        for n in range(4):
            lo = rel if n in (0, 3) else 0
            got(xfin.at[k, n % 2, pl.ds(lo, rel)], xr_s.at[k, 2 + n], xr_r.at[k, 2 + n])
        own = xrows(s, 0, 0, rows_h)

        def piece(i, carry):
            rows = pl.ds(pl.multiple_of(i * 16, 16), 16)

            def total(cols):
                return (
                    own[rows, cols].astype(F32)
                    + xfin[k, 0, rows, cols].astype(F32)
                    + xfin[k, 1, rows, cols].astype(F32)
                )

            gate, up = total(pl.ds(0, width)), total(pl.ds(width, width))
            act = gate / (1.0 + jnp.exp(-gate)) * up
            hid[k, pl.ds(pl.multiple_of(mine + i * 16, 16), 16), :] = act.astype(BF16)
            return carry

        lax.fori_loop(0, rows_h // 16, piece, 0)
        own_h = hid.at[k, pl.ds(mine, rows_h)]
        send(own_h, own_h, h_s.at[k], h_r.at[k], partner)

    def hidden_got(k):
        got(hid.at[k, pl.ds(theirs, rows_h)], h_s.at[k], h_r.at[k])

    def down_half(k, h):
        s = k % 2
        lhs = hid[k]

        def columns(j, carry):
            cols = pl.ds(pl.multiple_of(h * col_h + j * 256, 256), 256)
            outp[s, :, :, :, cols] = (
                jnp.dot(lhs, wd[:, cols], preferred_element_type=F32)
                .astype(BF16)
                .reshape(RING, RING, TILE, 256)
            )
            return carry

        lax.fori_loop(0, col_h // 256, columns, 0)
        yr0(k, h)

    halves = (pl.ds(0, 2), pl.ds(2, 2))
    cols2 = (pl.ds(0, col_h // 2), pl.ds(col_h // 2, col_h // 2))

    def chunk(k, h, i, others):
        cols = pl.ds(h * col_h, col_h)
        if h == 0:
            return outp.at[k % 2, i, others, :, cols]
        return outp.at[k % 2, others, i, :, cols]

    def raxes(h):
        return (("z", z), ("y", y)) if h == 0 else (("y", y), ("z", z))

    def yr0(k, h):
        (a, i), _ = raxes(h)
        ss, rs = yr_s.at[k, h, 0], yr_r.at[k, h, 0]
        send(chunk(k, h, nb(i, 2), halves[0]), yrel.at[k, h, 0], ss.at[0], rs.at[0], dev_yz(a, 1))
        send(chunk(k, h, nb(i, 2), halves[1]), yrel.at[k, h, 1], ss.at[1], rs.at[1], dev_yz(a, -1))
        send(chunk(k, h, nb(i, 1), halves[1]), yfin.at[k, h, 0, halves[1]], ss.at[2], rs.at[2], dev_yz(a, 1))
        send(chunk(k, h, nb(i, -1), halves[0]), yfin.at[k, h, 1, halves[0]], ss.at[3], rs.at[3], dev_yz(a, -1))

    def yr1(k, h, n):
        (a, i), _ = raxes(h)
        ss, rs = yr_s.at[k, h, 0], yr_r.at[k, h, 0]
        d = 1 - 2 * n
        got(yrel.at[k, h, n], ss.at[n], rs.at[n])
        own = chunk(k, h, nb(i, d), halves[n])
        own[...] = add(own, yrel.at[k, h, n])
        send(own, yfin.at[k, h, n, halves[n]], ss.at[4 + n], rs.at[4 + n], dev_yz(a, d))

    def yr2(k, h):
        (a, i), (b, j) = raxes(h)
        ss, rs = yr_s.at[k, h, 0], yr_r.at[k, h, 0]
        for n in range(4):
            got(yfin.at[k, h, n % 2, halves[1 if n in (0, 3) else 0]], ss.at[2 + n], rs.at[2 + n])
        own = chunk(k, h, i, pl.ds(0, RING))
        for o in range(RING):
            ysum[k % 2, h, o] = (
                own[o].astype(F32) + yfin[k, h, 0, o].astype(F32) + yfin[k, h, 1, o].astype(F32)
            ).astype(BF16)
        ss, rs = yr_s.at[k, h, 1], yr_r.at[k, h, 1]

        def sums(i, n):
            return ysum.at[k % 2, h, i, :, cols2[n]]

        send(sums(nb(j, 2), 0), y2rel.at[k, h, 0], ss.at[0], rs.at[0], dev_yz(b, 1))
        send(sums(nb(j, 2), 1), y2rel.at[k, h, 1], ss.at[1], rs.at[1], dev_yz(b, -1))
        send(sums(nb(j, 1), 1), y2fin.at[k, h, 0, :, cols2[1]], ss.at[2], rs.at[2], dev_yz(b, 1))
        send(sums(nb(j, -1), 0), y2fin.at[k, h, 1, :, cols2[0]], ss.at[3], rs.at[3], dev_yz(b, -1))

    def yr3(k, h, n):
        _, (b, j) = raxes(h)
        ss, rs = yr_s.at[k, h, 1], yr_r.at[k, h, 1]
        d = 1 - 2 * n
        got(y2rel.at[k, h, n], ss.at[n], rs.at[n])
        own = ysum.at[k % 2, h, nb(j, d), :, cols2[n]]
        own[...] = add(own, y2rel.at[k, h, n])
        send(own, y2fin.at[k, h, n, :, cols2[n]], ss.at[4 + n], rs.at[4 + n], dev_yz(b, d))

    def yr4(k, h):
        _, (b, j) = raxes(h)
        ss, rs = yr_s.at[k, h, 1], yr_r.at[k, h, 1]
        for n in range(4):
            got(y2fin.at[k, h, n % 2, :, cols2[1 if n in (0, 3) else 0]], ss.at[2 + n], rs.at[2 + n])
        total = (
            ysum[k % 2, h, j].astype(F32) + y2fin[k, h, 0].astype(F32) + y2fin[k, h, 1].astype(F32)
        )
        top, bottom = total[0:SUB], total[SUB:TILE]
        first = q == 0
        res[k, :, pl.ds(pl.multiple_of(q * half_d + h * col_h, col_h), col_h)] = jnp.where(first, top, bottom).astype(BF16)
        obuf[k, :, pl.ds(h * col_h, col_h)] = jnp.where(first, bottom, top).astype(BF16)

    def swap(k):
        send(
            obuf.at[k],
            res.at[k, :, pl.ds(pl.multiple_of(q * half_d, half_d), half_d)],
            o_s.at[k],
            o_r.at[k],
            partner,
        )

    def swap_got(k):
        got(res.at[k, :, pl.ds(pl.multiple_of((1 - q) * half_d, half_d), half_d)], o_s.at[k], o_r.at[k])

    def x_left(k):
        for n in range(4):
            left(mate.at[0, 0], q_s.at[k, n], q_r.at[k, n])
        for n in range(6):
            left(xrel.at[0, 0], xr_s.at[k, n], xr_r.at[k, n])

    def y_left(k):
        for h in range(2):
            for n in range(6):
                left(yrel.at[k, h, 0], yr_s.at[k, h, 0, n], yr_r.at[k, h, 0, n])
                left(y2rel.at[k, h, 0], yr_s.at[k, h, 1, n], yr_r.at[k, h, 1, n])

    steps = {
        "ag0": ag0, "ag1": ag1, "ag2": ag2, "ag3": ag3, "ag4": ag4, "gu": gu_tile, "gf": gu_finish,
        "xr": x_relay, "hid": hidden, "hg": hidden_got, "dn": down_half, "yr1": yr1, "yr2": yr2,
        "yr3": yr3, "yr4": yr4, "swap": swap, "xleft": x_left, "yleft": y_left,
    }
    a2a_wait(0)
    for name, *args in ORDER:
        if (name, args) == ("ag0", [1]):
            md[...] = spread(down_m, q * (half_d // BLOCK), half_d // BLOCK)
            ld_down.wait()
            lax.fori_loop(0, wd.shape[0] // BLOCK, keep_d, 0)
            a2a_wait(1)
        steps[name](*args)

    def finish(k, carry):
        swap_got(k)
        ag_left(k)
        left(hid.at[k, pl.ds(mine, rows_h)], h_s.at[k], h_r.at[k])
        left(obuf.at[k], o_s.at[k], o_r.at[k])
        return carry

    lax.fori_loop(0, STAGES, finish, 0)
    store = pltpu.make_async_copy(res, out, ld_sem.at[4])
    store.start()
    for s, (first, count) in enumerate(spans):
        for i in range(1, 2 * RING):
            left(mixed.at[pl.ds(first, count), 0, 0], a2a_s.at[s, i], a2a_r.at[s, i])
    store.wait()


def body(tokens, norm_gain, gate_weight, up_weight, down_weight, gate_mask, up_mask, down_mask):
    own, model = tokens.shape
    feats, width = gate_weight.shape
    half_d = model // 2
    rows = RING * RING * TILE
    dma = pltpu.SemaphoreType.DMA
    vmem, anyspace = pl.BlockSpec(memory_space=pltpu.VMEM), pl.BlockSpec(memory_space=pl.ANY)
    result = pl.pallas_call(
        kernel,
        out_shape=jax.ShapeDtypeStruct((STAGES, SUB, model), BF16),
        in_specs=[anyspace, vmem, anyspace, anyspace, anyspace, vmem, vmem, vmem],
        out_specs=anyspace,
        scratch_shapes=[
            pltpu.VMEM((STAGES, SUB, model), BF16),
            pltpu.VMEM((STAGES, SUB, model), BF16),
            pltpu.VMEM((STAGES, RING, 2, SUB, feats), BF16),
            pltpu.VMEM((STAGES, RING, RING, RING, TILE, feats), BF16),
            pltpu.VMEM((feats, 2 * width), BF16),
            pltpu.VMEM((width, half_d), BF16),
            pltpu.VMEM((feats // BLOCK, 2 * width), F32),
            pltpu.VMEM((width // BLOCK, half_d), F32),
            pltpu.VMEM((2, RING, rows, 2 * width), BF16),
            pltpu.VMEM((2, RING, rows // 2, 2 * width), BF16),
            pltpu.VMEM((STAGES, 2, rows // 4, 2 * width), BF16),
            pltpu.VMEM((STAGES, 2, rows // 2, 2 * width), BF16),
            pltpu.VMEM((STAGES, rows, width), BF16),
            pltpu.VMEM((2, RING, RING, TILE, half_d), BF16),
            pltpu.VMEM((STAGES, 2, 2, 2, TILE, half_d // 2), BF16),
            pltpu.VMEM((STAGES, 2, 2, RING, TILE, half_d // 2), BF16),
            pltpu.VMEM((2, 2, RING, TILE, half_d // 2), BF16),
            pltpu.VMEM((STAGES, 2, 2, TILE, half_d // 4), BF16),
            pltpu.VMEM((STAGES, 2, 2, TILE, half_d // 2), BF16),
            pltpu.VMEM((STAGES, SUB, model), BF16),
            pltpu.VMEM((STAGES, SUB, half_d), BF16),
            dma((5,)),
            dma((2, 2 * RING)),
            dma((2, 2 * RING)),
            dma((STAGES, 2, 8)),
            dma((STAGES, 2, 8)),
            dma((STAGES, 4)),
            dma((STAGES, 4)),
            dma((STAGES, 6)),
            dma((STAGES, 6)),
            dma((STAGES,)),
            dma((STAGES,)),
            dma((STAGES, 2, 2, 6)),
            dma((STAGES, 2, 2, 6)),
            dma((STAGES,)),
            dma((STAGES,)),
        ],
        compiler_params=pltpu.CompilerParams(
            collective_id=0, has_side_effects=True, vmem_limit_bytes=67_000_000
        ),
    )(
        tokens.reshape(STAGES, SUB, model),
        norm_gain.reshape(1, model),
        gate_weight,
        up_weight,
        down_weight,
        gate_mask,
        up_mask,
        down_mask,
    )
    return result.reshape(own, model)


def solution(mesh):
    return jax.shard_map(
        body,
        mesh=mesh,
        in_specs=(
            P(("rows", "cols"), None),
            P(),
            P("rows", "cols"),
            P("rows", "cols"),
            P("cols", None),
            P("rows", "cols"),
            P("rows", "cols"),
            P("cols", None),
        ),
        out_specs=P(("rows", "cols"), None),
        check_vma=False,
    )
```

```python
import functools

import jax
import jax.numpy as jnp
from jax import lax
from jax.experimental import pallas as pl
from jax.experimental.pallas import tpu as pltpu
from jax.sharding import PartitionSpec as P

BLOCK = 64
STAGES = 5
SUB = 8
RING = 4
TILE = 2 * SUB
MESH = pl.DeviceIdType.MESH
BF16, F32 = jnp.bfloat16, jnp.float32

ORDER = (
    ("ag0", 0), ("ag1", 0, 0, 0), ("ag1", 0, 0, 1), ("ag1", 0, 1, 0), ("ag1", 0, 1, 1), ("ag0", 1), ("ag2", 0, 0),
    ("ag2", 0, 1), ("ag1", 1, 0, 0), ("ag1", 1, 0, 1), ("ag1", 1, 1, 0), ("ag1", 1, 1, 1), ("ag0", 2),
    ("ag3", 0, 0, 0), ("ag3", 0, 0, 1), ("ag3", 0, 1, 0), ("ag3", 0, 1, 1), ("ag2", 1, 1), ("ag2", 1, 0),
    ("ag1", 2, 1, 0), ("ag1", 2, 0, 0), ("ag1", 2, 0, 1), ("ag1", 2, 1, 1), ("ag0", 3), ("ag4", 0), ("gu", 0, 0),
    ("gu", 0, 1), ("gu", 0, 2), ("gf", 0, 0), ("gu", 0, 3), ("gf", 0, 1), ("ag3", 1, 0, 0), ("ag3", 1, 0, 1),
    ("ag3", 1, 1, 0), ("ag3", 1, 1, 1), ("gf", 0, 2), ("ag2", 2, 0), ("ag2", 2, 1), ("gf", 0, 3), ("ag1", 3, 0, 0),
    ("ag1", 3, 0, 1), ("ag1", 3, 1, 0), ("ag1", 3, 1, 1), ("ag0", 4), ("ag4", 1), ("xr", 0, 0), ("xr", 0, 1),
    ("gu", 1, 0), ("gu", 1, 1), ("gu", 1, 2), ("gf", 1, 0), ("gu", 1, 3), ("ag3", 2, 0, 0), ("ag3", 2, 0, 1),
    ("ag3", 2, 1, 0), ("ag3", 2, 1, 1), ("gf", 1, 1), ("gf", 1, 2), ("ag2", 3, 0), ("ag2", 3, 1), ("ag1", 4, 1, 0),
    ("gf", 1, 3), ("ag1", 4, 0, 0), ("ag1", 4, 0, 1), ("ag1", 4, 1, 1), ("hid", 0), ("ag4", 2), ("hg", 0),
    ("xleft", 0), ("dn", 0, 0), ("dn", 0, 1), ("xr", 1, 0), ("xr", 1, 1), ("gu", 2, 0), ("ag3", 3, 0, 0),
    ("ag3", 3, 0, 1), ("ag3", 3, 1, 0), ("ag3", 3, 1, 1), ("gu", 2, 1), ("gu", 2, 2), ("yr1", 0, 0, 0),
    ("yr1", 0, 0, 1), ("yr1", 0, 1, 0), ("yr1", 0, 1, 1), ("gf", 2, 0), ("gf", 2, 1), ("gf", 2, 2), ("gu", 2, 3),
    ("ag2", 4, 0), ("ag2", 4, 1), ("hid", 1), ("gf", 2, 3), ("ag4", 3), ("hg", 1), ("xleft", 1), ("dn", 1, 0),
    ("dn", 1, 1), ("xr", 2, 0), ("xr", 2, 1), ("yr2", 0, 0), ("yr2", 0, 1), ("gu", 3, 0), ("gu", 3, 1),
    ("ag3", 4, 0, 0), ("ag3", 4, 0, 1), ("gu", 3, 2), ("ag3", 4, 1, 0), ("ag3", 4, 1, 1), ("gf", 3, 0), ("gu", 3, 3),
    ("yr1", 1, 0, 0), ("yr1", 1, 0, 1), ("yr1", 1, 1, 0), ("yr1", 1, 1, 1), ("gf", 3, 1), ("gf", 3, 2), ("gf", 3, 3),
    ("hid", 2), ("yr3", 0, 1, 0), ("yr3", 0, 1, 1), ("yr3", 0, 0, 0), ("yr3", 0, 0, 1), ("yleft", 0), ("hg", 2),
    ("xleft", 2), ("dn", 2, 0), ("dn", 2, 1), ("xr", 3, 0), ("xr", 3, 1), ("ag4", 4), ("gu", 4, 0), ("yr2", 1, 0),
    ("yr4", 0, 1), ("yr2", 1, 1), ("yr4", 0, 0), ("swap", 0), ("gf", 4, 0), ("gu", 4, 1), ("yr1", 2, 0, 0),
    ("yr1", 2, 0, 1), ("yr1", 2, 1, 0), ("yr1", 2, 1, 1), ("gu", 4, 2), ("gf", 4, 1), ("gu", 4, 3), ("yr3", 1, 1, 0),
    ("yr3", 1, 1, 1), ("yr3", 1, 0, 0), ("yr3", 1, 0, 1), ("hid", 3), ("yleft", 1), ("gf", 4, 2), ("gf", 4, 3),
    ("hg", 3), ("xleft", 3), ("dn", 3, 0), ("dn", 3, 1), ("xr", 4, 0), ("xr", 4, 1), ("yr4", 1, 0), ("yr4", 1, 1),
    ("swap", 1), ("yr2", 2, 0), ("yr2", 2, 1), ("yr1", 3, 0, 0), ("yr1", 3, 0, 1), ("yr1", 3, 1, 0), ("yr1", 3, 1, 1),
    ("yr3", 2, 1, 0), ("yr3", 2, 1, 1), ("yr3", 2, 0, 0), ("yr3", 2, 0, 1), ("yleft", 2), ("hid", 4), ("yr2", 3, 0),
    ("yr4", 2, 1), ("hg", 4), ("xleft", 4), ("dn", 4, 0), ("dn", 4, 1), ("yr3", 3, 0, 0), ("yr3", 3, 0, 1),
    ("yr2", 3, 1), ("yr4", 2, 0), ("swap", 2), ("yr1", 4, 0, 0), ("yr1", 4, 0, 1), ("yr1", 4, 1, 0), ("yr1", 4, 1, 1),
    ("yr3", 3, 1, 0), ("yr3", 3, 1, 1), ("yleft", 3), ("yr4", 3, 0), ("yr2", 4, 0), ("yr2", 4, 1), ("yr4", 3, 1),
    ("swap", 3), ("yr3", 4, 0, 0), ("yr3", 4, 0, 1), ("yr3", 4, 1, 0), ("yr3", 4, 1, 1), ("yleft", 4), ("yr4", 4, 0),
    ("yr4", 4, 1), ("swap", 4),
)


def kernel(
    tok, gain, gate_w, up_w, down_w, gate_m, up_m, down_m, out,
    toks, sent, mixed, gath, wgu, wd, mgu, md, part, mate, xrel, xfin, hid,
    outp, yrel, yfin, ysum, y2rel, y2fin, res, obuf,
    ld_sem, a2a_s, a2a_r, ag_s, ag_r, q_s, q_r, xr_s, xr_r, h_s, h_r, yr_s, yr_r, o_s, o_r,
):
    r, c = lax.axis_index("rows"), lax.axis_index("cols")
    x, q = r // 2, r % 2
    z, y = c // RING, c % RING
    width = wgu.shape[1] // 2
    feats = wgu.shape[0]
    half_d = wd.shape[1]
    col_h = half_d // 2
    rows_h = part.shape[2] // 2
    rel = rows_h // 2

    def nb(v, d):
        return (v + d + RING) % RING

    def dev_x(d):
        return {"rows": nb(x, d) * 2 + q, "cols": c}

    def dev_yz(axis, d):
        if axis == "y":
            return {"rows": r, "cols": z * RING + nb(y, d)}
        return {"rows": r, "cols": nb(z, d) * RING + y}

    partner = {"rows": x * 2 + (1 - q), "cols": c}

    def copy(src, dst, ss, rs, dev):
        return pltpu.make_async_remote_copy(
            src_ref=src, dst_ref=dst, send_sem=ss, recv_sem=rs, device_id=dev, device_id_type=MESH
        )

    def send(src, dst, ss, rs, dev):
        copy(src, dst, ss, rs, dev).start()

    def got(dst, ss, rs):
        copy(dst, dst, ss, rs, partner).wait_recv()

    def left(src, ss, rs):
        copy(src, src, ss, rs, partner).wait_send()

    ld_tok = pltpu.make_async_copy(tok, toks, ld_sem.at[0])
    ld_gate = pltpu.make_async_copy(gate_w, wgu.at[:, pl.ds(0, width)], ld_sem.at[1])
    ld_up = pltpu.make_async_copy(up_w, wgu.at[:, pl.ds(width, width)], ld_sem.at[2])
    ld_down = pltpu.make_async_copy(
        down_w.at[:, pl.ds(pl.multiple_of(q * half_d, half_d), half_d)], wd, ld_sem.at[3]
    )
    ld_tok.start()
    ld_gate.start()
    ld_up.start()
    ld_down.start()

    barrier = pltpu.get_barrier_semaphore()

    def row_peer(i):
        return (r + i) % (2 * RING)

    for i in range(1, 2 * RING):
        pl.semaphore_signal(barrier, inc=1, device_id={"rows": row_peer(i), "cols": c}, device_id_type=MESH)
    for axis in ("y", "z"):
        for d in (1, -1):
            pl.semaphore_signal(barrier, inc=1, device_id=dev_yz(axis, d), device_id_type=MESH)

    ld_tok.wait()

    def norm(k, carry):
        values = toks[k].astype(F32)
        meansq = jnp.mean(values * values, axis=-1, keepdims=True)
        sent[k] = (values * lax.rsqrt(meansq + 1e-05) * gain[...]).astype(BF16)
        return carry

    norm(0, 0)
    pl.semaphore_wait(barrier, 2 * RING + 3)

    spans = ((0, 1), (1, STAGES - 1))
    for s, (first, count) in enumerate(spans):
        if s == 1:
            lax.fori_loop(1, STAGES, norm, 0)
        for i in range(1, 2 * RING):
            peer = row_peer(i)
            send(
                sent.at[pl.ds(first, count), :, pl.ds(pl.multiple_of(peer * feats, feats), feats)],
                mixed.at[pl.ds(first, count), x, q],
                a2a_s.at[s, i],
                a2a_r.at[s, i],
                {"rows": peer, "cols": c},
            )
    mixed[:, x, q] = sent[:, :, pl.ds(pl.multiple_of(r * feats, feats), feats)]

    def spread(mask, first, count):
        blocks = mask.shape[1]
        row = lax.broadcasted_iota(jnp.int32, (blocks, count * BLOCK), 0)
        col = lax.broadcasted_iota(jnp.int32, (blocks, count * BLOCK), 1)
        onehot = (row == col // BLOCK + first).astype(F32).astype(BF16)
        return jnp.dot(mask[...].astype(F32).astype(BF16), onehot, preferred_element_type=F32)

    mgu[:, 0:width] = spread(gate_m, 0, width // BLOCK)
    mgu[:, width : 2 * width] = spread(up_m, 0, width // BLOCK)
    ld_gate.wait()
    ld_up.wait()

    def keep_gu(b, carry):
        rows = pl.ds(pl.multiple_of(b * BLOCK, BLOCK), BLOCK)
        wgu[rows, :] = wgu[rows, :] * mgu[pl.ds(b, 1), :].astype(BF16)
        return carry

    lax.fori_loop(0, feats // BLOCK, keep_gu, 0)

    def keep_d(b, carry):
        rows = pl.ds(pl.multiple_of(b * BLOCK, BLOCK), BLOCK)
        wd[rows, :] = wd[rows, :] * md[pl.ds(b, 1), :].astype(BF16)
        return carry

    def a2a_wait(s):
        first, count = spans[s]
        for i in range(1, 2 * RING):
            origin = (r - i + 2 * RING) % (2 * RING)
            got(mixed.at[pl.ds(first, count), origin // 2, origin % 2], a2a_s.at[s, i], a2a_r.at[s, i])

    def block(k, xs, axis, i):
        return gath.at[k, xs, z, i] if axis == "y" else gath.at[k, xs, i, y]

    def slab(k, xs, axis, i):
        return gath.at[k, xs, i] if axis == "z" else gath.at[k, xs, :, i]

    def axes(h):
        return (("y", y), ("z", z)) if h == 0 else (("z", z), ("y", y))

    def both(h):
        return pl.ds(2 * h, 2)

    def ag0(k):
        for xi in range(RING):
            gath[k, xi, z, y] = jnp.concatenate([mixed[k, xi, 0], mixed[k, xi, 1]], axis=0)
        for h in range(2):
            (a, i), _ = axes(h)
            own = block(k, both(h), a, i)
            send(own, own, ag_s.at[k, h, 0], ag_r.at[k, h, 0], dev_yz(a, 1))
            send(own, own, ag_s.at[k, h, 1], ag_r.at[k, h, 1], dev_yz(a, -1))

    def ag1(k, h, n):
        (a, i), _ = axes(h)
        d = 2 * n - 1
        got(block(k, both(h), a, nb(i, d)), ag_s.at[k, h, n], ag_r.at[k, h, n])
        piece = block(k, 2 * h + n, a, nb(i, d))
        send(piece, piece, ag_s.at[k, h, 2 + n], ag_r.at[k, h, 2 + n], dev_yz(a, -d))

    def ag2(k, h):
        (a, i), (b, j) = axes(h)
        for n in range(2):
            got(block(k, 2 * h + n, a, nb(i, 2)), ag_s.at[k, h, 2 + n], ag_r.at[k, h, 2 + n])
        own = slab(k, both(h), b, j)
        send(own, own, ag_s.at[k, h, 4], ag_r.at[k, h, 4], dev_yz(b, 1))
        send(own, own, ag_s.at[k, h, 5], ag_r.at[k, h, 5], dev_yz(b, -1))

    def ag3(k, h, n):
        _, (b, j) = axes(h)
        d = 2 * n - 1
        got(slab(k, both(h), b, nb(j, d)), ag_s.at[k, h, 4 + n], ag_r.at[k, h, 4 + n])
        piece = slab(k, 2 * h + n, b, nb(j, d))
        send(piece, piece, ag_s.at[k, h, 6 + n], ag_r.at[k, h, 6 + n], dev_yz(b, -d))

    def ag4(k):
        for h in range(2):
            _, (b, j) = axes(h)
            for n in range(2):
                got(slab(k, 2 * h + n, b, nb(j, 2)), ag_s.at[k, h, 6 + n], ag_r.at[k, h, 6 + n])

    def ag_left(k):
        for h in range(2):
            (a, i), (b, j) = axes(h)
            for n in range(2):
                left(block(k, both(h), a, i), ag_s.at[k, h, n], ag_r.at[k, h, n])
                left(block(k, 2 * h, a, i), ag_s.at[k, h, 2 + n], ag_r.at[k, h, 2 + n])
                left(slab(k, both(h), b, j), ag_s.at[k, h, 4 + n], ag_r.at[k, h, 4 + n])
                left(slab(k, 2 * h, b, j), ag_s.at[k, h, 6 + n], ag_r.at[k, h, 6 + n])

    order = (2, 1, -1, 0)
    mine = pl.multiple_of(q * rows_h, rows_h)
    theirs = pl.multiple_of((1 - q) * rows_h, rows_h)

    def gu_tile(k, n):
        xi, s = nb(x, order[n]), k % 2
        lhs = gath[k, xi].reshape(part.shape[2], feats)
        for j in range(0, 2 * width, 256):
            cols = pl.ds(j, 256)
            part[s, xi, :, cols] = jnp.dot(lhs, wgu[:, cols], preferred_element_type=F32).astype(BF16)
        send(
            part.at[s, xi, pl.ds(theirs, rows_h)], mate.at[s, xi], q_s.at[k, n], q_r.at[k, n], partner
        )

    def add(ref_a, ref_b):
        return (ref_a[...].astype(F32) + ref_b[...].astype(F32)).astype(BF16)

    def add_rows(ref_a, ref_b):
        def piece(i, carry):
            rows = pl.ds(pl.multiple_of(i * 32, 32), 32)
            ref_a[rows, :] = (ref_a[rows, :].astype(F32) + ref_b[rows, :].astype(F32)).astype(BF16)
            return carry

        lax.fori_loop(0, ref_a.shape[0] // 32, piece, 0)

    def xrows(s, d, lo, count):
        return part.at[s, nb(x, d), pl.ds(pl.multiple_of(mine + lo, rel), count)]

    def gu_finish(k, n):
        d, s = order[n], k % 2
        xi = nb(x, d)
        got(mate.at[s, xi], q_s.at[k, n], q_r.at[k, n])
        whole = xrows(s, d, 0, rows_h)
        add_rows(whole, mate.at[s, xi])
        if d == 2:
            send(xrows(s, 2, 0, rel), xrel.at[k, 0], xr_s.at[k, 0], xr_r.at[k, 0], dev_x(1))
            send(xrows(s, 2, rel, rel), xrel.at[k, 1], xr_s.at[k, 1], xr_r.at[k, 1], dev_x(-1))
        elif d == 1:
            send(xrows(s, 1, rel, rel), xfin.at[k, 0, pl.ds(rel, rel)], xr_s.at[k, 2], xr_r.at[k, 2], dev_x(1))
        elif d == -1:
            send(xrows(s, -1, 0, rel), xfin.at[k, 1, pl.ds(0, rel)], xr_s.at[k, 3], xr_r.at[k, 3], dev_x(-1))

    def x_relay(k, n):
        s, d = k % 2, 1 - 2 * n
        got(xrel.at[k, n], xr_s.at[k, n], xr_r.at[k, n])
        own = xrows(s, d, n * rel, rel)
        add_rows(own, xrel.at[k, n])
        send(own, xfin.at[k, n, pl.ds(n * rel, rel)], xr_s.at[k, 4 + n], xr_r.at[k, 4 + n], dev_x(d))

    def hidden(k):
        s = k % 2
        for n in range(4):
            lo = rel if n in (0, 3) else 0
            got(xfin.at[k, n % 2, pl.ds(lo, rel)], xr_s.at[k, 2 + n], xr_r.at[k, 2 + n])
        own = xrows(s, 0, 0, rows_h)

        def piece(i, carry):
            rows = pl.ds(pl.multiple_of(i * 16, 16), 16)

            def total(cols):
                return (
                    own[rows, cols].astype(F32)
                    + xfin[k, 0, rows, cols].astype(F32)
                    + xfin[k, 1, rows, cols].astype(F32)
                )

            gate, up = total(pl.ds(0, width)), total(pl.ds(width, width))
            act = gate / (1.0 + jnp.exp(-gate)) * up
            hid[k, pl.ds(pl.multiple_of(mine + i * 16, 16), 16), :] = act.astype(BF16)
            return carry

        lax.fori_loop(0, rows_h // 16, piece, 0)
        own_h = hid.at[k, pl.ds(mine, rows_h)]
        send(own_h, own_h, h_s.at[k], h_r.at[k], partner)

    def hidden_got(k):
        got(hid.at[k, pl.ds(theirs, rows_h)], h_s.at[k], h_r.at[k])

    def down_half(k, h):
        s = k % 2
        lhs = hid[k]
        for j in range(h * col_h, (h + 1) * col_h, 256):
            cols = pl.ds(j, 256)
            outp[s, :, :, :, cols] = (
                jnp.dot(lhs, wd[:, cols], preferred_element_type=F32)
                .astype(BF16)
                .reshape(RING, RING, TILE, 256)
            )
        yr0(k, h)

    halves = (pl.ds(0, 2), pl.ds(2, 2))
    cols2 = (pl.ds(0, col_h // 2), pl.ds(col_h // 2, col_h // 2))

    def chunk(k, h, i, others):
        cols = pl.ds(h * col_h, col_h)
        if h == 0:
            return outp.at[k % 2, i, others, :, cols]
        return outp.at[k % 2, others, i, :, cols]

    def raxes(h):
        return (("z", z), ("y", y)) if h == 0 else (("y", y), ("z", z))

    def yr0(k, h):
        (a, i), _ = raxes(h)
        ss, rs = yr_s.at[k, h, 0], yr_r.at[k, h, 0]
        send(chunk(k, h, nb(i, 2), halves[0]), yrel.at[k, h, 0], ss.at[0], rs.at[0], dev_yz(a, 1))
        send(chunk(k, h, nb(i, 2), halves[1]), yrel.at[k, h, 1], ss.at[1], rs.at[1], dev_yz(a, -1))
        send(chunk(k, h, nb(i, 1), halves[1]), yfin.at[k, h, 0, halves[1]], ss.at[2], rs.at[2], dev_yz(a, 1))
        send(chunk(k, h, nb(i, -1), halves[0]), yfin.at[k, h, 1, halves[0]], ss.at[3], rs.at[3], dev_yz(a, -1))

    def yr1(k, h, n):
        (a, i), _ = raxes(h)
        ss, rs = yr_s.at[k, h, 0], yr_r.at[k, h, 0]
        d = 1 - 2 * n
        got(yrel.at[k, h, n], ss.at[n], rs.at[n])
        own = chunk(k, h, nb(i, d), halves[n])
        own[...] = add(own, yrel.at[k, h, n])
        send(own, yfin.at[k, h, n, halves[n]], ss.at[4 + n], rs.at[4 + n], dev_yz(a, d))

    def yr2(k, h):
        (a, i), (b, j) = raxes(h)
        ss, rs = yr_s.at[k, h, 0], yr_r.at[k, h, 0]
        for n in range(4):
            got(yfin.at[k, h, n % 2, halves[1 if n in (0, 3) else 0]], ss.at[2 + n], rs.at[2 + n])
        own = chunk(k, h, i, pl.ds(0, RING))

        def piece(o, carry):
            ysum[k % 2, h, o] = (
                own[o].astype(F32) + yfin[k, h, 0, o].astype(F32) + yfin[k, h, 1, o].astype(F32)
            ).astype(BF16)
            return carry

        lax.fori_loop(0, RING, piece, 0)
        ss, rs = yr_s.at[k, h, 1], yr_r.at[k, h, 1]

        def sums(i, n):
            return ysum.at[k % 2, h, i, :, cols2[n]]

        send(sums(nb(j, 2), 0), y2rel.at[k, h, 0], ss.at[0], rs.at[0], dev_yz(b, 1))
        send(sums(nb(j, 2), 1), y2rel.at[k, h, 1], ss.at[1], rs.at[1], dev_yz(b, -1))
        send(sums(nb(j, 1), 1), y2fin.at[k, h, 0, :, cols2[1]], ss.at[2], rs.at[2], dev_yz(b, 1))
        send(sums(nb(j, -1), 0), y2fin.at[k, h, 1, :, cols2[0]], ss.at[3], rs.at[3], dev_yz(b, -1))

    def yr3(k, h, n):
        _, (b, j) = raxes(h)
        ss, rs = yr_s.at[k, h, 1], yr_r.at[k, h, 1]
        d = 1 - 2 * n
        got(y2rel.at[k, h, n], ss.at[n], rs.at[n])
        own = ysum.at[k % 2, h, nb(j, d), :, cols2[n]]
        own[...] = add(own, y2rel.at[k, h, n])
        send(own, y2fin.at[k, h, n, :, cols2[n]], ss.at[4 + n], rs.at[4 + n], dev_yz(b, d))

    def yr4(k, h):
        _, (b, j) = raxes(h)
        ss, rs = yr_s.at[k, h, 1], yr_r.at[k, h, 1]
        for n in range(4):
            got(y2fin.at[k, h, n % 2, :, cols2[1 if n in (0, 3) else 0]], ss.at[2 + n], rs.at[2 + n])
        total = (
            ysum[k % 2, h, j].astype(F32) + y2fin[k, h, 0].astype(F32) + y2fin[k, h, 1].astype(F32)
        )
        top, bottom = total[0:SUB], total[SUB:TILE]
        first = q == 0
        res[k, :, pl.ds(pl.multiple_of(q * half_d + h * col_h, col_h), col_h)] = jnp.where(first, top, bottom).astype(BF16)
        obuf[k, :, pl.ds(h * col_h, col_h)] = jnp.where(first, bottom, top).astype(BF16)

    def swap(k):
        send(
            obuf.at[k],
            res.at[k, :, pl.ds(pl.multiple_of(q * half_d, half_d), half_d)],
            o_s.at[k],
            o_r.at[k],
            partner,
        )

    def swap_got(k):
        got(res.at[k, :, pl.ds(pl.multiple_of((1 - q) * half_d, half_d), half_d)], o_s.at[k], o_r.at[k])

    def x_left(k):
        for n in range(4):
            left(mate.at[0, 0], q_s.at[k, n], q_r.at[k, n])
        for n in range(6):
            left(xrel.at[0, 0], xr_s.at[k, n], xr_r.at[k, n])

    def y_left(k):
        for h in range(2):
            for n in range(6):
                left(yrel.at[k, h, 0], yr_s.at[k, h, 0, n], yr_r.at[k, h, 0, n])
                left(y2rel.at[k, h, 0], yr_s.at[k, h, 1, n], yr_r.at[k, h, 1, n])

    steps = {
        "ag0": ag0, "ag1": ag1, "ag2": ag2, "ag3": ag3, "ag4": ag4, "gu": gu_tile, "gf": gu_finish,
        "xr": x_relay, "hid": hidden, "hg": hidden_got, "dn": down_half, "yr1": yr1, "yr2": yr2,
        "yr3": yr3, "yr4": yr4, "swap": swap, "xleft": x_left, "yleft": y_left,
    }
    a2a_wait(0)
    for name, *args in ORDER:
        if (name, args) == ("ag0", [1]):
            md[...] = spread(down_m, q * (half_d // BLOCK), half_d // BLOCK)
            ld_down.wait()
            lax.fori_loop(0, wd.shape[0] // BLOCK, keep_d, 0)
            a2a_wait(1)
        steps[name](*args)

    def finish(k, carry):
        swap_got(k)
        ag_left(k)
        left(hid.at[k, pl.ds(mine, rows_h)], h_s.at[k], h_r.at[k])
        left(obuf.at[k], o_s.at[k], o_r.at[k])
        return carry

    lax.fori_loop(0, STAGES, finish, 0)
    store = pltpu.make_async_copy(res, out, ld_sem.at[4])
    store.start()
    for s, (first, count) in enumerate(spans):
        for i in range(1, 2 * RING):
            left(mixed.at[pl.ds(first, count), 0, 0], a2a_s.at[s, i], a2a_r.at[s, i])
    store.wait()


def body(tokens, norm_gain, gate_weight, up_weight, down_weight, gate_mask, up_mask, down_mask):
    own, model = tokens.shape
    feats, width = gate_weight.shape
    half_d = model // 2
    rows = RING * RING * TILE
    dma = pltpu.SemaphoreType.DMA
    vmem, anyspace = pl.BlockSpec(memory_space=pltpu.VMEM), pl.BlockSpec(memory_space=pl.ANY)
    result = pl.pallas_call(
        kernel,
        out_shape=jax.ShapeDtypeStruct((STAGES, SUB, model), BF16),
        in_specs=[anyspace, vmem, anyspace, anyspace, anyspace, vmem, vmem, vmem],
        out_specs=anyspace,
        scratch_shapes=[
            pltpu.VMEM((STAGES, SUB, model), BF16),
            pltpu.VMEM((STAGES, SUB, model), BF16),
            pltpu.VMEM((STAGES, RING, 2, SUB, feats), BF16),
            pltpu.VMEM((STAGES, RING, RING, RING, TILE, feats), BF16),
            pltpu.VMEM((feats, 2 * width), BF16),
            pltpu.VMEM((width, half_d), BF16),
            pltpu.VMEM((feats // BLOCK, 2 * width), F32),
            pltpu.VMEM((width // BLOCK, half_d), F32),
            pltpu.VMEM((2, RING, rows, 2 * width), BF16),
            pltpu.VMEM((2, RING, rows // 2, 2 * width), BF16),
            pltpu.VMEM((STAGES, 2, rows // 4, 2 * width), BF16),
            pltpu.VMEM((STAGES, 2, rows // 2, 2 * width), BF16),
            pltpu.VMEM((STAGES, rows, width), BF16),
            pltpu.VMEM((2, RING, RING, TILE, half_d), BF16),
            pltpu.VMEM((STAGES, 2, 2, 2, TILE, half_d // 2), BF16),
            pltpu.VMEM((STAGES, 2, 2, RING, TILE, half_d // 2), BF16),
            pltpu.VMEM((2, 2, RING, TILE, half_d // 2), BF16),
            pltpu.VMEM((STAGES, 2, 2, TILE, half_d // 4), BF16),
            pltpu.VMEM((STAGES, 2, 2, TILE, half_d // 2), BF16),
            pltpu.VMEM((STAGES, SUB, model), BF16),
            pltpu.VMEM((STAGES, SUB, half_d), BF16),
            dma((5,)),
            dma((2, 2 * RING)),
            dma((2, 2 * RING)),
            dma((STAGES, 2, 8)),
            dma((STAGES, 2, 8)),
            dma((STAGES, 4)),
            dma((STAGES, 4)),
            dma((STAGES, 6)),
            dma((STAGES, 6)),
            dma((STAGES,)),
            dma((STAGES,)),
            dma((STAGES, 2, 2, 6)),
            dma((STAGES, 2, 2, 6)),
            dma((STAGES,)),
            dma((STAGES,)),
        ],
        compiler_params=pltpu.CompilerParams(
            collective_id=0, has_side_effects=True, vmem_limit_bytes=67_000_000
        ),
    )(
        tokens.reshape(STAGES, SUB, model),
        norm_gain.reshape(1, model),
        gate_weight,
        up_weight,
        down_weight,
        gate_mask,
        up_mask,
        down_mask,
    )
    return result.reshape(own, model)


def solution(mesh):
    return jax.shard_map(
        body,
        mesh=mesh,
        in_specs=(
            P(("rows", "cols"), None),
            P(),
            P("rows", "cols"),
            P("rows", "cols"),
            P("cols", None),
            P("rows", "cols"),
            P("rows", "cols"),
            P("cols", None),
        ),
        out_specs=P(("rows", "cols"), None),
        check_vma=False,
    )
```

```python
import functools

import jax
import jax.numpy as jnp
from jax import lax
from jax.experimental import pallas as pl
from jax.experimental.pallas import tpu as pltpu
from jax.sharding import PartitionSpec as P

BLOCK = 64
STAGES = 5
SUB = 8
RING = 4
TILE = 2 * SUB
MESH = pl.DeviceIdType.MESH
BF16, F32 = jnp.bfloat16, jnp.float32

ORDER = (
    ("ag0", 0, 0), ("ag0", 0, 1), ("mgu", 0), ("mgu", 1), ("mgu", 2), ("mgu", 3), ("md", 0), ("ag1", 0, 0, 0, 0),
    ("ag1", 0, 0, 0, 1), ("ag1", 0, 0, 1, 0), ("ag1", 0, 0, 1, 1), ("ag1", 0, 1, 0, 0), ("ag1", 0, 1, 0, 1),
    ("ag1", 0, 1, 1, 0), ("ag1", 0, 1, 1, 1), ("ag0", 1, 0), ("ag0", 1, 1), ("ag0", 2, 0), ("md", 1),
    ("ag2", 0, 0, 0), ("ag2", 0, 0, 1), ("ag2", 0, 1, 0), ("ag2", 0, 1, 1), ("md", 2), ("ag1", 1, 0, 0, 0),
    ("ag1", 1, 0, 0, 1), ("ag1", 1, 0, 1, 0), ("ag1", 1, 0, 1, 1), ("ag1", 1, 1, 0, 0), ("ag1", 1, 1, 0, 1),
    ("ag1", 1, 1, 1, 0), ("ag1", 1, 1, 1, 1), ("ag1", 2, 0, 0, 0), ("ag1", 2, 0, 0, 1), ("ag1", 2, 0, 1, 0),
    ("ag1", 2, 0, 1, 1), ("md", 3), ("ag3", 0, 0, 0, 0), ("ag3", 0, 0, 0, 1), ("ag3", 0, 0, 1, 0),
    ("ag3", 0, 0, 1, 1), ("ag0", 2, 1), ("ag3", 0, 1, 0, 0), ("ag3", 0, 1, 0, 1), ("ag3", 0, 1, 1, 0),
    ("ag3", 0, 1, 1, 1), ("ag2", 1, 0, 0), ("ag2", 1, 0, 1), ("ag2", 1, 1, 0), ("ag2", 1, 1, 1), ("ag2", 2, 0, 0),
    ("ag2", 2, 0, 1), ("ag0", 3, 0), ("ag4", 0, 0), ("gu", 0, 0), ("ag1", 2, 1, 0, 0), ("ag1", 2, 1, 0, 1),
    ("ag1", 2, 1, 1, 0), ("ag1", 2, 1, 1, 1), ("gu", 0, 1), ("ag4", 0, 1), ("gu", 0, 2), ("gf", 0, 0),
    ("ag3", 1, 0, 0, 0), ("ag3", 1, 0, 0, 1), ("ag3", 1, 0, 1, 0), ("ag3", 1, 0, 1, 1), ("ag0", 3, 1), ("gf", 0, 1),
    ("gu", 0, 3), ("gf", 0, 2), ("ag3", 1, 1, 0, 0), ("ag3", 1, 1, 0, 1), ("ag3", 1, 1, 1, 0), ("ag3", 1, 1, 1, 1),
    ("ag0", 4, 0), ("gf", 0, 3), ("ag3", 2, 0, 0, 0), ("ag3", 2, 0, 0, 1), ("ag3", 2, 0, 1, 0), ("ag3", 2, 0, 1, 1),
    ("ag1", 3, 0, 0, 0), ("ag1", 3, 0, 0, 1), ("ag1", 3, 0, 1, 0), ("ag1", 3, 0, 1, 1), ("ag2", 2, 1, 0),
    ("ag2", 2, 1, 1), ("ag0", 4, 1), ("xr", 0, 0), ("ag4", 1, 0), ("xr", 0, 1), ("gu", 1, 0), ("ag1", 3, 1, 0, 0),
    ("ag1", 3, 1, 0, 1), ("ag1", 3, 1, 1, 0), ("ag4", 1, 1), ("ag1", 3, 1, 1, 1), ("gu", 1, 1), ("ag1", 4, 0, 0, 0),
    ("ag1", 4, 0, 0, 1), ("ag1", 4, 0, 1, 0), ("ag1", 4, 0, 1, 1), ("ag4", 2, 0), ("ag2", 3, 0, 0), ("ag2", 3, 0, 1),
    ("gf", 1, 0), ("gu", 1, 2), ("gf", 1, 1), ("gu", 1, 3), ("ag1", 4, 1, 0, 0), ("ag1", 4, 1, 0, 1),
    ("ag1", 4, 1, 1, 0), ("ag1", 4, 1, 1, 1), ("ag2", 3, 1, 0), ("ag2", 3, 1, 1), ("ag2", 4, 0, 0), ("ag2", 4, 0, 1),
    ("ag3", 2, 1, 0, 0), ("ag3", 2, 1, 0, 1), ("ag3", 2, 1, 1, 0), ("ag3", 2, 1, 1, 1), ("gf", 1, 2), ("gf", 1, 3),
    ("hid", 0), ("ag3", 3, 0, 0, 0), ("ag2", 4, 1, 0), ("ag2", 4, 1, 1), ("ag3", 3, 0, 0, 1), ("ag3", 3, 0, 1, 0),
    ("ag3", 3, 0, 1, 1), ("hg", 0), ("dn", 0, 0), ("ag3", 3, 1, 0, 0), ("ag3", 3, 1, 0, 1), ("ag3", 3, 1, 1, 0),
    ("ag3", 3, 1, 1, 1), ("xr", 1, 0), ("xr", 1, 1), ("dn", 0, 1), ("xleft", 0), ("gu", 2, 0), ("ag3", 4, 0, 0, 0),
    ("ag3", 4, 0, 0, 1), ("ag4", 2, 1), ("ag3", 4, 0, 1, 0), ("ag3", 4, 0, 1, 1), ("gu", 2, 1), ("gf", 2, 0),
    ("gu", 2, 2), ("ag3", 4, 1, 0, 1), ("ag3", 4, 1, 1, 0), ("ag3", 4, 1, 1, 1), ("gf", 2, 1), ("ag4", 3, 0),
    ("ag3", 4, 1, 0, 0), ("hid", 1), ("gf", 2, 2), ("gu", 2, 3), ("hg", 1), ("yr1", 0, 0, 0), ("yr1", 0, 0, 1),
    ("dn", 1, 0), ("yr1", 0, 1, 0), ("yr1", 0, 1, 1), ("xr", 2, 0), ("xr", 2, 1), ("gf", 2, 3), ("dn", 1, 1),
    ("ag4", 3, 1), ("xleft", 1), ("gu", 3, 0), ("ag4", 4, 0), ("gu", 3, 1), ("ag4", 4, 1), ("gu", 3, 2), ("gf", 3, 0),
    ("gu", 3, 3), ("yr2", 0, 0), ("yr2", 0, 1), ("gf", 3, 1), ("hid", 2), ("yr1", 1, 0, 0), ("yr1", 1, 0, 1),
    ("yr1", 1, 1, 0), ("yr1", 1, 1, 1), ("gf", 3, 2), ("hg", 2), ("gf", 3, 3), ("xleft", 2), ("gu", 4, 0),
    ("yr3", 0, 0, 0), ("yr3", 0, 0, 1), ("yr3", 0, 1, 0), ("yr3", 0, 1, 1), ("yleft", 0), ("xr", 3, 0), ("xr", 3, 1),
    ("dn", 2, 0), ("dn", 2, 1), ("yr2", 1, 0), ("yr2", 1, 1), ("yr4", 0, 0), ("yr4", 0, 1), ("swap", 0), ("gf", 4, 0),
    ("gu", 4, 1), ("gu", 4, 2), ("yr1", 2, 0, 0), ("yr1", 2, 0, 1), ("yr1", 2, 1, 0), ("gf", 4, 1), ("yr1", 2, 1, 1),
    ("hid", 3), ("yr3", 1, 1, 0), ("yr3", 1, 1, 1), ("gf", 4, 2), ("gu", 4, 3), ("hg", 3), ("yr3", 1, 0, 0),
    ("yr3", 1, 0, 1), ("yleft", 1), ("dn", 3, 0), ("yr2", 2, 0), ("xr", 4, 0), ("xr", 4, 1), ("yr2", 2, 1),
    ("gf", 4, 3), ("yr4", 1, 0), ("yr4", 1, 1), ("swap", 1), ("dn", 3, 1), ("xleft", 3), ("yr3", 2, 0, 0),
    ("yr3", 2, 0, 1), ("yr1", 3, 0, 0), ("yr1", 3, 0, 1), ("yr3", 2, 1, 0), ("yr3", 2, 1, 1), ("yleft", 2),
    ("yr1", 3, 1, 0), ("yr1", 3, 1, 1), ("hid", 4), ("yr2", 3, 0), ("hg", 4), ("dn", 4, 0), ("dn", 4, 1),
    ("yr2", 3, 1), ("xleft", 4), ("yr4", 2, 0), ("yr4", 2, 1), ("swap", 2), ("yr3", 3, 0, 0), ("yr3", 3, 0, 1),
    ("yr1", 4, 0, 0), ("yr1", 4, 0, 1), ("yr1", 4, 1, 0), ("yr1", 4, 1, 1), ("yr3", 3, 1, 0), ("yr3", 3, 1, 1),
    ("yleft", 3), ("yr4", 3, 0), ("yr2", 4, 0), ("yr2", 4, 1), ("yr4", 3, 1), ("swap", 3), ("yr3", 4, 0, 0),
    ("yr3", 4, 0, 1), ("yr3", 4, 1, 0), ("yr3", 4, 1, 1), ("yleft", 4), ("yr4", 4, 0), ("yr4", 4, 1), ("swap", 4),
)


def kernel(
    tok, gain, gate_w, up_w, down_w, gate_m, up_m, down_m, out,
    toks, sent, mixed, gath, wgu, wd, mgu, md, part, mate, xrel, xfin, hid,
    outp, yrel, yfin, ysum, y2rel, y2fin, res, obuf,
    ld_sem, st_sem, a2a_s, a2a_r, ag_s, ag_r, q_s, q_r, xr_s, xr_r, h_s, h_r, yr_s, yr_r, o_s, o_r,
):
    r, c = lax.axis_index("rows"), lax.axis_index("cols")
    x, q = r // 2, r % 2
    z, y = c // RING, c % RING
    width = wgu.shape[1] // 2
    feats = wgu.shape[0]
    half_d = wd.shape[1]
    col_h = half_d // 2
    rows_h = part.shape[2] // 2
    rel = rows_h // 2

    def nb(v, d):
        return (v + d + RING) % RING

    def dev_x(d):
        return {"rows": nb(x, d) * 2 + q, "cols": c}

    def dev_yz(axis, d):
        if axis == "y":
            return {"rows": r, "cols": z * RING + nb(y, d)}
        return {"rows": r, "cols": nb(z, d) * RING + y}

    partner = {"rows": x * 2 + (1 - q), "cols": c}

    def copy(src, dst, ss, rs, dev):
        return pltpu.make_async_remote_copy(
            src_ref=src, dst_ref=dst, send_sem=ss, recv_sem=rs, device_id=dev, device_id_type=MESH
        )

    def send(src, dst, ss, rs, dev):
        copy(src, dst, ss, rs, dev).start()

    def got(dst, ss, rs):
        copy(dst, dst, ss, rs, partner).wait_recv()

    def left(src, ss, rs):
        copy(src, src, ss, rs, partner).wait_send()

    ld_tok = pltpu.make_async_copy(tok, toks, ld_sem.at[0])
    ld_gate = pltpu.make_async_copy(gate_w, wgu.at[:, pl.ds(0, width)], ld_sem.at[1])
    ld_up = pltpu.make_async_copy(up_w, wgu.at[:, pl.ds(width, width)], ld_sem.at[2])
    ld_down = pltpu.make_async_copy(
        down_w.at[:, pl.ds(pl.multiple_of(q * half_d, half_d), half_d)], wd, ld_sem.at[3]
    )
    ld_tok.start()

    barrier = pltpu.get_barrier_semaphore()

    def row_peer(i):
        return (r + i) % (2 * RING)

    for i in range(1, 2 * RING):
        pl.semaphore_signal(barrier, inc=1, device_id={"rows": row_peer(i), "cols": c}, device_id_type=MESH)
    for axis in ("y", "z"):
        for d in (1, -1):
            pl.semaphore_signal(barrier, inc=1, device_id=dev_yz(axis, d), device_id_type=MESH)

    ld_tok.wait()
    ld_gate.start()
    ld_up.start()
    ld_down.start()

    def norm(k, carry):
        values = toks[k].astype(F32)
        meansq = jnp.mean(values * values, axis=-1, keepdims=True)
        sent[k] = (values * lax.rsqrt(meansq + 1e-05) * gain[...]).astype(BF16)
        return carry

    norm(0, 0)
    pl.semaphore_wait(barrier, 2 * RING + 3)

    spans = ((0, 1), (1, STAGES - 1))
    for s, (first, count) in enumerate(spans):
        if s == 1:
            lax.fori_loop(1, STAGES, norm, 0)
        for i in range(1, 2 * RING):
            peer = row_peer(i)
            send(
                sent.at[pl.ds(first, count), :, pl.ds(pl.multiple_of(peer * feats, feats), feats)],
                mixed.at[pl.ds(first, count), x, q],
                a2a_s.at[s, i],
                a2a_r.at[s, i],
                {"rows": peer, "cols": c},
            )
    mixed[:, x, q] = sent[:, :, pl.ds(pl.multiple_of(r * feats, feats), feats)]

    def spread(mask, first, count):
        blocks = mask.shape[1]
        row = lax.broadcasted_iota(jnp.int32, (blocks, count * BLOCK), 0)
        col = lax.broadcasted_iota(jnp.int32, (blocks, count * BLOCK), 1)
        onehot = (row == col // BLOCK + first).astype(F32).astype(BF16)
        return jnp.dot(mask[...].astype(F32).astype(BF16), onehot, preferred_element_type=F32)

    def keep(weight, mask, first, count):
        def rows_of(b, carry):
            rows = pl.ds(pl.multiple_of(b * BLOCK, BLOCK), BLOCK)
            weight[rows, :] = weight[rows, :] * mask[pl.ds(b, 1), :].astype(BF16)
            return carry

        lax.fori_loop(first, first + count, rows_of, 0)

    def mask_gu(part_of):
        if part_of == 0:
            mgu[:, 0:width] = spread(gate_m, 0, width // BLOCK)
            mgu[:, width : 2 * width] = spread(up_m, 0, width // BLOCK)
            ld_gate.wait()
            ld_up.wait()
        blocks = feats // BLOCK
        keep(wgu, mgu, part_of * blocks // 4, blocks // 4)

    def mask_d(part_of):
        if part_of == 0:
            md[...] = spread(down_m, q * (half_d // BLOCK), half_d // BLOCK)
            ld_down.wait()
        blocks = width // BLOCK
        first = part_of * blocks // 4
        keep(wd, md, first, (part_of + 1) * blocks // 4 - first)

    def a2a_wait(s):
        first, count = spans[s]
        for i in range(1, 2 * RING):
            origin = (r - i + 2 * RING) % (2 * RING)
            got(mixed.at[pl.ds(first, count), origin // 2, origin % 2], a2a_s.at[s, i], a2a_r.at[s, i])

    order = (2, 1, -1, 0)

    def tile(u, h):
        return nb(x, order[2 * u + h])

    def axes(h):
        return (("y", y), ("z", z)) if h == 0 else (("z", z), ("y", y))

    def block(k, u, h, i, n=None):
        at = (k, tile(u, h), z, i) if h == 0 else (k, tile(u, h), i, y)
        return gath.at[at] if n is None else gath.at[(*at, slice(None), pl.ds(n * (feats // 2), feats // 2))]

    def slab(k, u, h, i, n=None):
        part_of = slice(None) if n is None else pl.ds(2 * n, 2)
        return gath.at[k, tile(u, h), i, part_of] if h == 0 else gath.at[k, tile(u, h), part_of, i]

    def ag_send(k, u, h, n, what, axis, d):
        send(what, what, ag_s.at[k, u, h, n], ag_r.at[k, u, h, n], dev_yz(axis, d))

    def ag_got(k, u, h, n, what):
        got(what, ag_s.at[k, u, h, n], ag_r.at[k, u, h, n])

    def ag0(k, u):
        for h in range(2):
            (a, i), _ = axes(h)
            xi = tile(u, h)
            gath[k, xi, z, y] = jnp.concatenate([mixed[k, xi, 0], mixed[k, xi, 1]], axis=0)
            for n in range(2):
                ag_send(k, u, h, n, block(k, u, h, i), a, 1 - 2 * n)

    def ag1(k, u, h, n):
        (a, i), _ = axes(h)
        d = 2 * n - 1
        ag_got(k, u, h, n, block(k, u, h, nb(i, d)))
        ag_send(k, u, h, 2 + n, block(k, u, h, nb(i, d), n), a, -d)

    def ag2(k, u, h):
        (a, i), (b, j) = axes(h)
        for n in range(2):
            ag_got(k, u, h, 2 + n, block(k, u, h, nb(i, 2), n))
        for n in range(2):
            ag_send(k, u, h, 4 + n, slab(k, u, h, j), b, 1 - 2 * n)

    def ag3(k, u, h, n):
        _, (b, j) = axes(h)
        d = 2 * n - 1
        ag_got(k, u, h, 4 + n, slab(k, u, h, nb(j, d)))
        ag_send(k, u, h, 6 + n, slab(k, u, h, nb(j, d), n), b, -d)

    def ag4(k, u):
        for h in range(2):
            _, (b, j) = axes(h)
            for n in range(2):
                ag_got(k, u, h, 6 + n, slab(k, u, h, nb(j, 2), n))

    def ag_left(k):
        for u in range(2):
            for h in range(2):
                for n in range(2):
                    sems = ((ag_s.at[k, u, h, n + m], ag_r.at[k, u, h, n + m]) for m in (0, 2, 4, 6))
                    for what, (ss, rs) in zip(
                        (block(k, u, h, 0), block(k, u, h, 0, n), slab(k, u, h, 0), slab(k, u, h, 0, n)), sems
                    ):
                        left(what, ss, rs)

    mine = pl.multiple_of(q * rows_h, rows_h)
    theirs = pl.multiple_of((1 - q) * rows_h, rows_h)

    def gu_tile(k, n):
        xi, s = nb(x, order[n]), k % 2
        lhs = gath[k, xi].reshape(part.shape[2], feats)
        for j in range(0, 2 * width, 256):
            cols = pl.ds(j, 256)
            part[s, xi, :, cols] = jnp.dot(lhs, wgu[:, cols], preferred_element_type=F32).astype(BF16)
        send(
            part.at[s, xi, pl.ds(theirs, rows_h)], mate.at[s, xi], q_s.at[k, n], q_r.at[k, n], partner
        )

    def add(ref_a, ref_b):
        return (ref_a[...].astype(F32) + ref_b[...].astype(F32)).astype(BF16)

    def add_rows(ref_a, ref_b):
        def piece(i, carry):
            rows = pl.ds(pl.multiple_of(i * 32, 32), 32)
            ref_a[rows, :] = (ref_a[rows, :].astype(F32) + ref_b[rows, :].astype(F32)).astype(BF16)
            return carry

        lax.fori_loop(0, ref_a.shape[0] // 32, piece, 0)

    def xrows(s, d, lo, count):
        return part.at[s, nb(x, d), pl.ds(pl.multiple_of(mine + lo, rel), count)]

    def gu_finish(k, n):
        d, s = order[n], k % 2
        xi = nb(x, d)
        got(mate.at[s, xi], q_s.at[k, n], q_r.at[k, n])
        whole = xrows(s, d, 0, rows_h)
        add_rows(whole, mate.at[s, xi])
        if d == 2:
            send(xrows(s, 2, 0, rel), xrel.at[k, 0], xr_s.at[k, 0], xr_r.at[k, 0], dev_x(1))
            send(xrows(s, 2, rel, rel), xrel.at[k, 1], xr_s.at[k, 1], xr_r.at[k, 1], dev_x(-1))
        elif d == 1:
            send(xrows(s, 1, rel, rel), xfin.at[k, 0, pl.ds(rel, rel)], xr_s.at[k, 2], xr_r.at[k, 2], dev_x(1))
        elif d == -1:
            send(xrows(s, -1, 0, rel), xfin.at[k, 1, pl.ds(0, rel)], xr_s.at[k, 3], xr_r.at[k, 3], dev_x(-1))

    def x_relay(k, n):
        s, d = k % 2, 1 - 2 * n
        got(xrel.at[k, n], xr_s.at[k, n], xr_r.at[k, n])
        own = xrows(s, d, n * rel, rel)
        add_rows(own, xrel.at[k, n])
        send(own, xfin.at[k, n, pl.ds(n * rel, rel)], xr_s.at[k, 4 + n], xr_r.at[k, 4 + n], dev_x(d))

    def hidden(k):
        s = k % 2
        for n in range(4):
            lo = rel if n in (0, 3) else 0
            got(xfin.at[k, n % 2, pl.ds(lo, rel)], xr_s.at[k, 2 + n], xr_r.at[k, 2 + n])
        own = xrows(s, 0, 0, rows_h)

        def piece(i, carry):
            rows = pl.ds(pl.multiple_of(i * 16, 16), 16)

            def total(cols):
                return (
                    own[rows, cols].astype(F32)
                    + xfin[k, 0, rows, cols].astype(F32)
                    + xfin[k, 1, rows, cols].astype(F32)
                )

            gate, up = total(pl.ds(0, width)), total(pl.ds(width, width))
            act = gate / (1.0 + jnp.exp(-gate)) * up
            hid[k, pl.ds(pl.multiple_of(mine + i * 16, 16), 16), :] = act.astype(BF16)
            return carry

        lax.fori_loop(0, rows_h // 16, piece, 0)
        own_h = hid.at[k, pl.ds(mine, rows_h)]
        send(own_h, own_h, h_s.at[k], h_r.at[k], partner)

    def hidden_got(k):
        got(hid.at[k, pl.ds(theirs, rows_h)], h_s.at[k], h_r.at[k])

    def down_half(k, h):
        s = k % 2
        lhs = hid[k]
        for j in range(h * col_h, (h + 1) * col_h, 256):
            cols = pl.ds(j, 256)
            outp[s, :, :, :, cols] = (
                jnp.dot(lhs, wd[:, cols], preferred_element_type=F32)
                .astype(BF16)
                .reshape(RING, RING, TILE, 256)
            )
        yr0(k, h)

    halves = (pl.ds(0, 2), pl.ds(2, 2))
    cols2 = (pl.ds(0, col_h // 2), pl.ds(col_h // 2, col_h // 2))

    def chunk(k, h, i, others):
        cols = pl.ds(h * col_h, col_h)
        if h == 0:
            return outp.at[k % 2, i, others, :, cols]
        return outp.at[k % 2, others, i, :, cols]

    def raxes(h):
        return (("z", z), ("y", y)) if h == 0 else (("y", y), ("z", z))

    def yr0(k, h):
        (a, i), _ = raxes(h)
        ss, rs = yr_s.at[k, h, 0], yr_r.at[k, h, 0]
        send(chunk(k, h, nb(i, 2), halves[0]), yrel.at[k, h, 0], ss.at[0], rs.at[0], dev_yz(a, 1))
        send(chunk(k, h, nb(i, 2), halves[1]), yrel.at[k, h, 1], ss.at[1], rs.at[1], dev_yz(a, -1))
        send(chunk(k, h, nb(i, 1), halves[1]), yfin.at[k, h, 0, halves[1]], ss.at[2], rs.at[2], dev_yz(a, 1))
        send(chunk(k, h, nb(i, -1), halves[0]), yfin.at[k, h, 1, halves[0]], ss.at[3], rs.at[3], dev_yz(a, -1))

    def yr1(k, h, n):
        (a, i), _ = raxes(h)
        ss, rs = yr_s.at[k, h, 0], yr_r.at[k, h, 0]
        d = 1 - 2 * n
        got(yrel.at[k, h, n], ss.at[n], rs.at[n])
        own = chunk(k, h, nb(i, d), halves[n])
        own[...] = add(own, yrel.at[k, h, n])
        send(own, yfin.at[k, h, n, halves[n]], ss.at[4 + n], rs.at[4 + n], dev_yz(a, d))

    def yr2(k, h):
        (a, i), (b, j) = raxes(h)
        ss, rs = yr_s.at[k, h, 0], yr_r.at[k, h, 0]
        for n in range(4):
            got(yfin.at[k, h, n % 2, halves[1 if n in (0, 3) else 0]], ss.at[2 + n], rs.at[2 + n])
        own = chunk(k, h, i, pl.ds(0, RING))

        def piece(o, carry):
            ysum[k % 2, h, o] = (
                own[o].astype(F32) + yfin[k, h, 0, o].astype(F32) + yfin[k, h, 1, o].astype(F32)
            ).astype(BF16)
            return carry

        lax.fori_loop(0, RING, piece, 0)
        ss, rs = yr_s.at[k, h, 1], yr_r.at[k, h, 1]

        def sums(i, n):
            return ysum.at[k % 2, h, i, :, cols2[n]]

        send(sums(nb(j, 2), 0), y2rel.at[k, h, 0], ss.at[0], rs.at[0], dev_yz(b, 1))
        send(sums(nb(j, 2), 1), y2rel.at[k, h, 1], ss.at[1], rs.at[1], dev_yz(b, -1))
        send(sums(nb(j, 1), 1), y2fin.at[k, h, 0, :, cols2[1]], ss.at[2], rs.at[2], dev_yz(b, 1))
        send(sums(nb(j, -1), 0), y2fin.at[k, h, 1, :, cols2[0]], ss.at[3], rs.at[3], dev_yz(b, -1))

    def yr3(k, h, n):
        _, (b, j) = raxes(h)
        ss, rs = yr_s.at[k, h, 1], yr_r.at[k, h, 1]
        d = 1 - 2 * n
        got(y2rel.at[k, h, n], ss.at[n], rs.at[n])
        own = ysum.at[k % 2, h, nb(j, d), :, cols2[n]]
        own[...] = add(own, y2rel.at[k, h, n])
        send(own, y2fin.at[k, h, n, :, cols2[n]], ss.at[4 + n], rs.at[4 + n], dev_yz(b, d))

    def yr4(k, h):
        _, (b, j) = raxes(h)
        ss, rs = yr_s.at[k, h, 1], yr_r.at[k, h, 1]
        for n in range(4):
            got(y2fin.at[k, h, n % 2, :, cols2[1 if n in (0, 3) else 0]], ss.at[2 + n], rs.at[2 + n])
        total = (
            ysum[k % 2, h, j].astype(F32) + y2fin[k, h, 0].astype(F32) + y2fin[k, h, 1].astype(F32)
        )
        top, bottom = total[0:SUB], total[SUB:TILE]
        first = q == 0
        res[k, :, pl.ds(pl.multiple_of(q * half_d + h * col_h, col_h), col_h)] = jnp.where(first, top, bottom).astype(BF16)
        obuf[k, :, pl.ds(h * col_h, col_h)] = jnp.where(first, bottom, top).astype(BF16)

    def swap(k):
        send(
            obuf.at[k],
            res.at[k, :, pl.ds(pl.multiple_of(q * half_d, half_d), half_d)],
            o_s.at[k],
            o_r.at[k],
            partner,
        )

    def swap_got(k):
        got(res.at[k, :, pl.ds(pl.multiple_of((1 - q) * half_d, half_d), half_d)], o_s.at[k], o_r.at[k])

    def x_left(k):
        for n in range(4):
            left(mate.at[0, 0], q_s.at[k, n], q_r.at[k, n])
        for n in range(6):
            left(xrel.at[0, 0], xr_s.at[k, n], xr_r.at[k, n])

    def y_left(k):
        for h in range(2):
            for n in range(6):
                left(yrel.at[k, h, 0], yr_s.at[k, h, 0, n], yr_r.at[k, h, 0, n])
                left(y2rel.at[k, h, 0], yr_s.at[k, h, 1, n], yr_r.at[k, h, 1, n])

    steps = {
        "ag0": ag0, "ag1": ag1, "ag2": ag2, "ag3": ag3, "ag4": ag4, "gu": gu_tile, "gf": gu_finish,
        "xr": x_relay, "hid": hidden, "hg": hidden_got, "dn": down_half, "yr1": yr1, "yr2": yr2,
        "yr3": yr3, "yr4": yr4, "swap": swap, "xleft": x_left, "yleft": y_left,
        "mgu": mask_gu, "md": mask_d,
    }
    def store(k):
        swap_got(k)
        pltpu.make_async_copy(res.at[k], out.at[k], st_sem.at[k]).start()

    a2a_wait(0)
    exchanged = False
    for name, *args in ORDER:
        if name == "ag0" and args[0] > 0 and not exchanged:
            a2a_wait(1)
            exchanged = True
        steps[name](*args)
        if name == "swap" and args[0] > 0:
            store(args[0] - 1)
    store(STAGES - 1)

    def finish(k, carry):
        ag_left(k)
        left(hid.at[k, pl.ds(mine, rows_h)], h_s.at[k], h_r.at[k])
        left(obuf.at[k], o_s.at[k], o_r.at[k])
        return carry

    lax.fori_loop(0, STAGES, finish, 0)
    for s, (first, count) in enumerate(spans):
        for i in range(1, 2 * RING):
            left(mixed.at[pl.ds(first, count), 0, 0], a2a_s.at[s, i], a2a_r.at[s, i])
    for k in range(STAGES):
        pltpu.make_async_copy(res.at[k], out.at[k], st_sem.at[k]).wait()


def body(tokens, norm_gain, gate_weight, up_weight, down_weight, gate_mask, up_mask, down_mask):
    own, model = tokens.shape
    feats, width = gate_weight.shape
    half_d = model // 2
    rows = RING * RING * TILE
    dma = pltpu.SemaphoreType.DMA
    vmem, anyspace = pl.BlockSpec(memory_space=pltpu.VMEM), pl.BlockSpec(memory_space=pl.ANY)
    result = pl.pallas_call(
        kernel,
        out_shape=jax.ShapeDtypeStruct((STAGES, SUB, model), BF16),
        in_specs=[anyspace, vmem, anyspace, anyspace, anyspace, vmem, vmem, vmem],
        out_specs=anyspace,
        scratch_shapes=[
            pltpu.VMEM((STAGES, SUB, model), BF16),
            pltpu.VMEM((STAGES, SUB, model), BF16),
            pltpu.VMEM((STAGES, RING, 2, SUB, feats), BF16),
            pltpu.VMEM((STAGES, RING, RING, RING, TILE, feats), BF16),
            pltpu.VMEM((feats, 2 * width), BF16),
            pltpu.VMEM((width, half_d), BF16),
            pltpu.VMEM((feats // BLOCK, 2 * width), F32),
            pltpu.VMEM((width // BLOCK, half_d), F32),
            pltpu.VMEM((2, RING, rows, 2 * width), BF16),
            pltpu.VMEM((2, RING, rows // 2, 2 * width), BF16),
            pltpu.VMEM((STAGES, 2, rows // 4, 2 * width), BF16),
            pltpu.VMEM((STAGES, 2, rows // 2, 2 * width), BF16),
            pltpu.VMEM((STAGES, rows, width), BF16),
            pltpu.VMEM((2, RING, RING, TILE, half_d), BF16),
            pltpu.VMEM((STAGES, 2, 2, 2, TILE, half_d // 2), BF16),
            pltpu.VMEM((STAGES, 2, 2, RING, TILE, half_d // 2), BF16),
            pltpu.VMEM((2, 2, RING, TILE, half_d // 2), BF16),
            pltpu.VMEM((STAGES, 2, 2, TILE, half_d // 4), BF16),
            pltpu.VMEM((STAGES, 2, 2, TILE, half_d // 2), BF16),
            pltpu.VMEM((STAGES, SUB, model), BF16),
            pltpu.VMEM((STAGES, SUB, half_d), BF16),
            dma((4,)),
            dma((STAGES,)),
            dma((2, 2 * RING)),
            dma((2, 2 * RING)),
            dma((STAGES, 2, 2, 8)),
            dma((STAGES, 2, 2, 8)),
            dma((STAGES, 4)),
            dma((STAGES, 4)),
            dma((STAGES, 6)),
            dma((STAGES, 6)),
            dma((STAGES,)),
            dma((STAGES,)),
            dma((STAGES, 2, 2, 6)),
            dma((STAGES, 2, 2, 6)),
            dma((STAGES,)),
            dma((STAGES,)),
        ],
        compiler_params=pltpu.CompilerParams(
            collective_id=0, has_side_effects=True, vmem_limit_bytes=67_000_000
        ),
    )(
        tokens.reshape(STAGES, SUB, model),
        norm_gain.reshape(1, model),
        gate_weight,
        up_weight,
        down_weight,
        gate_mask,
        up_mask,
        down_mask,
    )
    return result.reshape(own, model)


def solution(mesh):
    return jax.shard_map(
        body,
        mesh=mesh,
        in_specs=(
            P(("rows", "cols"), None),
            P(),
            P("rows", "cols"),
            P("rows", "cols"),
            P("cols", None),
            P("rows", "cols"),
            P("rows", "cols"),
            P("cols", None),
        ),
        out_specs=P(("rows", "cols"), None),
        check_vma=False,
    )
```

```python
import functools

import jax
import jax.numpy as jnp
from jax import lax
from jax.experimental import pallas as pl
from jax.experimental.pallas import tpu as pltpu
from jax.sharding import PartitionSpec as P

BLOCK = 64
STAGES = 5
SUB = 8
RING = 4
TILE = 2 * SUB
MESH = pl.DeviceIdType.MESH
BF16, F32 = jnp.bfloat16, jnp.float32

ORDER = (
    ("ag0", 0, 0), ("ag0", 0, 1), ("mgu", 0), ("mgu", 1), ("mgu", 2), ("mgu", 3), ("md", 0), ("ag1", 0, 0, 0, 0),
    ("ag1", 0, 0, 0, 1), ("ag1", 0, 0, 1, 0), ("ag1", 0, 0, 1, 1), ("ag1", 0, 1, 0, 0), ("ag1", 0, 1, 0, 1),
    ("ag1", 0, 1, 1, 0), ("ag1", 0, 1, 1, 1), ("ag0", 1, 0), ("ag0", 1, 1), ("ag0", 2, 0), ("md", 1),
    ("ag2", 0, 0, 0), ("ag2", 0, 0, 1), ("ag2", 0, 1, 0), ("ag2", 0, 1, 1), ("md", 2), ("ag1", 1, 0, 0, 0),
    ("ag1", 1, 0, 0, 1), ("ag1", 1, 0, 1, 0), ("ag1", 1, 0, 1, 1), ("ag1", 1, 1, 0, 0), ("ag1", 1, 1, 0, 1),
    ("ag1", 1, 1, 1, 0), ("ag1", 1, 1, 1, 1), ("ag1", 2, 0, 0, 0), ("ag1", 2, 0, 0, 1), ("ag1", 2, 0, 1, 0),
    ("ag1", 2, 0, 1, 1), ("md", 3), ("ag3", 0, 0, 0, 0), ("ag3", 0, 0, 0, 1), ("ag3", 0, 0, 1, 0),
    ("ag3", 0, 0, 1, 1), ("ag0", 2, 1), ("ag3", 0, 1, 0, 0), ("ag3", 0, 1, 0, 1), ("ag3", 0, 1, 1, 0),
    ("ag3", 0, 1, 1, 1), ("ag2", 1, 0, 0), ("ag2", 1, 0, 1), ("ag2", 1, 1, 0), ("ag2", 1, 1, 1), ("ag2", 2, 0, 0),
    ("ag2", 2, 0, 1), ("ag0", 3, 0), ("ag4", 0, 0), ("gu", 0, 0), ("ag1", 2, 1, 0, 0), ("ag1", 2, 1, 0, 1),
    ("ag1", 2, 1, 1, 0), ("ag1", 2, 1, 1, 1), ("gu", 0, 1), ("ag4", 0, 1), ("gu", 0, 2), ("gf", 0, 0),
    ("ag3", 1, 0, 0, 0), ("ag3", 1, 0, 0, 1), ("ag3", 1, 0, 1, 0), ("ag3", 1, 0, 1, 1), ("ag0", 3, 1), ("gf", 0, 1),
    ("gu", 0, 3), ("gf", 0, 2), ("ag3", 1, 1, 0, 0), ("ag3", 1, 1, 0, 1), ("ag3", 1, 1, 1, 0), ("ag3", 1, 1, 1, 1),
    ("ag0", 4, 0), ("gf", 0, 3), ("ag3", 2, 0, 0, 0), ("ag3", 2, 0, 0, 1), ("ag3", 2, 0, 1, 0), ("ag3", 2, 0, 1, 1),
    ("ag1", 3, 0, 0, 0), ("ag1", 3, 0, 0, 1), ("ag1", 3, 0, 1, 0), ("ag1", 3, 0, 1, 1), ("ag2", 2, 1, 0),
    ("ag2", 2, 1, 1), ("ag0", 4, 1), ("xr", 0, 0), ("ag4", 1, 0), ("xr", 0, 1), ("gu", 1, 0), ("ag1", 3, 1, 0, 0),
    ("ag1", 3, 1, 0, 1), ("ag1", 3, 1, 1, 0), ("ag4", 1, 1), ("ag1", 3, 1, 1, 1), ("gu", 1, 1), ("ag1", 4, 0, 0, 0),
    ("ag1", 4, 0, 0, 1), ("ag1", 4, 0, 1, 0), ("ag1", 4, 0, 1, 1), ("ag4", 2, 0), ("ag2", 3, 0, 0), ("ag2", 3, 0, 1),
    ("gf", 1, 0), ("gu", 1, 2), ("gf", 1, 1), ("gu", 1, 3), ("ag1", 4, 1, 0, 0), ("ag1", 4, 1, 0, 1),
    ("ag1", 4, 1, 1, 0), ("ag1", 4, 1, 1, 1), ("ag2", 3, 1, 0), ("ag2", 3, 1, 1), ("ag2", 4, 0, 0), ("ag2", 4, 0, 1),
    ("ag3", 2, 1, 0, 0), ("ag3", 2, 1, 0, 1), ("ag3", 2, 1, 1, 0), ("ag3", 2, 1, 1, 1), ("gf", 1, 2), ("gf", 1, 3),
    ("hid", 0), ("ag3", 3, 0, 0, 0), ("ag2", 4, 1, 0), ("ag2", 4, 1, 1), ("ag3", 3, 0, 0, 1), ("ag3", 3, 0, 1, 0),
    ("ag3", 3, 0, 1, 1), ("hg", 0), ("dn", 0, 0), ("ag3", 3, 1, 0, 0), ("ag3", 3, 1, 0, 1), ("ag3", 3, 1, 1, 0),
    ("ag3", 3, 1, 1, 1), ("xr", 1, 0), ("xr", 1, 1), ("dn", 0, 1), ("xleft", 0), ("gu", 2, 0), ("ag3", 4, 0, 0, 0),
    ("ag3", 4, 0, 0, 1), ("ag4", 2, 1), ("ag3", 4, 0, 1, 0), ("ag3", 4, 0, 1, 1), ("gu", 2, 1), ("gf", 2, 0),
    ("gu", 2, 2), ("ag3", 4, 1, 0, 1), ("ag3", 4, 1, 1, 0), ("ag3", 4, 1, 1, 1), ("gf", 2, 1), ("ag4", 3, 0),
    ("ag3", 4, 1, 0, 0), ("hid", 1), ("gf", 2, 2), ("gu", 2, 3), ("hg", 1), ("yr1", 0, 0, 0), ("yr1", 0, 0, 1),
    ("dn", 1, 0), ("yr1", 0, 1, 0), ("yr1", 0, 1, 1), ("xr", 2, 0), ("xr", 2, 1), ("gf", 2, 3), ("dn", 1, 1),
    ("ag4", 3, 1), ("xleft", 1), ("gu", 3, 0), ("ag4", 4, 0), ("gu", 3, 1), ("ag4", 4, 1), ("gu", 3, 2), ("gf", 3, 0),
    ("gu", 3, 3), ("yr2", 0, 0), ("yr2", 0, 1), ("gf", 3, 1), ("hid", 2), ("yr1", 1, 0, 0), ("yr1", 1, 0, 1),
    ("yr1", 1, 1, 0), ("yr1", 1, 1, 1), ("gf", 3, 2), ("hg", 2), ("gf", 3, 3), ("xleft", 2), ("gu", 4, 0),
    ("yr3", 0, 0, 0), ("yr3", 0, 0, 1), ("yr3", 0, 1, 0), ("yr3", 0, 1, 1), ("yleft", 0), ("xr", 3, 0), ("xr", 3, 1),
    ("dn", 2, 0), ("dn", 2, 1), ("yr2", 1, 0), ("yr2", 1, 1), ("yr4", 0, 0), ("yr4", 0, 1), ("swap", 0), ("gf", 4, 0),
    ("gu", 4, 1), ("gu", 4, 2), ("yr1", 2, 0, 0), ("yr1", 2, 0, 1), ("yr1", 2, 1, 0), ("gf", 4, 1), ("yr1", 2, 1, 1),
    ("hid", 3), ("yr3", 1, 1, 0), ("yr3", 1, 1, 1), ("gf", 4, 2), ("gu", 4, 3), ("hg", 3), ("yr3", 1, 0, 0),
    ("yr3", 1, 0, 1), ("yleft", 1), ("dn", 3, 0), ("yr2", 2, 0), ("xr", 4, 0), ("xr", 4, 1), ("yr2", 2, 1),
    ("gf", 4, 3), ("yr4", 1, 0), ("yr4", 1, 1), ("swap", 1), ("dn", 3, 1), ("xleft", 3), ("yr3", 2, 0, 0),
    ("yr3", 2, 0, 1), ("yr1", 3, 0, 0), ("yr1", 3, 0, 1), ("yr3", 2, 1, 0), ("yr3", 2, 1, 1), ("yleft", 2),
    ("yr1", 3, 1, 0), ("yr1", 3, 1, 1), ("hid", 4), ("yr2", 3, 0), ("hg", 4), ("dn", 4, 0), ("dn", 4, 1),
    ("yr2", 3, 1), ("xleft", 4), ("yr4", 2, 0), ("yr4", 2, 1), ("swap", 2), ("yr3", 3, 0, 0), ("yr3", 3, 0, 1),
    ("yr1", 4, 0, 0), ("yr1", 4, 0, 1), ("yr1", 4, 1, 0), ("yr1", 4, 1, 1), ("yr3", 3, 1, 0), ("yr3", 3, 1, 1),
    ("yleft", 3), ("yr4", 3, 0), ("yr2", 4, 0), ("yr2", 4, 1), ("yr4", 3, 1), ("swap", 3), ("yr3", 4, 0, 0),
    ("yr3", 4, 0, 1), ("yr3", 4, 1, 0), ("yr3", 4, 1, 1), ("yleft", 4), ("yr4", 4, 0), ("yr4", 4, 1), ("swap", 4),
)


def kernel(
    tok, gain_h, gate_w, up_w, down_w, gate_h, up_h, down_h, out,
    gain, gate_m, up_m, down_m, toks, sent, mixed, gath, wgu, wd, mgu, md, part, mate, xrel, xfin, hid,
    outp, yrel, yfin, ysum, y2rel, y2fin, res, obuf,
    sm_sem, ld_sem, st_sem, a2a_s, a2a_r, ag_s, ag_r, q_s, q_r, xr_s, xr_r, h_s, h_r, yr_s, yr_r, o_s, o_r,
):
    r, c = lax.axis_index("rows"), lax.axis_index("cols")
    x, q = r // 2, r % 2
    z, y = c // RING, c % RING
    width = wgu.shape[1] // 2
    feats = wgu.shape[0]
    half_d = wd.shape[1]
    col_h = half_d // 2
    rows_h = part.shape[2] // 2
    rel = rows_h // 2

    def nb(v, d):
        return (v + d + RING) % RING

    def dev_x(d):
        return {"rows": nb(x, d) * 2 + q, "cols": c}

    def dev_yz(axis, d):
        if axis == "y":
            return {"rows": r, "cols": z * RING + nb(y, d)}
        return {"rows": r, "cols": nb(z, d) * RING + y}

    partner = {"rows": x * 2 + (1 - q), "cols": c}

    def copy(src, dst, ss, rs, dev):
        return pltpu.make_async_remote_copy(
            src_ref=src, dst_ref=dst, send_sem=ss, recv_sem=rs, device_id=dev, device_id_type=MESH
        )

    def send(src, dst, ss, rs, dev):
        copy(src, dst, ss, rs, dev).start()

    def got(dst, ss, rs):
        copy(dst, dst, ss, rs, partner).wait_recv()

    def left(src, ss, rs):
        copy(src, src, ss, rs, partner).wait_send()

    ld_first = pltpu.make_async_copy(tok.at[0], toks.at[0], ld_sem.at[4])
    rest = pl.ds(1, STAGES - 1)
    ld_tok = pltpu.make_async_copy(tok.at[rest], toks.at[rest], ld_sem.at[0])
    ld_gate = pltpu.make_async_copy(gate_w, wgu.at[:, pl.ds(0, width)], ld_sem.at[1])
    ld_up = pltpu.make_async_copy(up_w, wgu.at[:, pl.ds(width, width)], ld_sem.at[2])
    ld_down = pltpu.make_async_copy(
        down_w.at[:, pl.ds(pl.multiple_of(q * half_d, half_d), half_d)], wd, ld_sem.at[3]
    )
    barrier = pltpu.get_barrier_semaphore()

    def row_peer(i):
        return (r + i) % (2 * RING)

    for i in (4, 5, 2, 3, 6, 7, 1):
        pl.semaphore_signal(barrier, inc=1, device_id={"rows": row_peer(i), "cols": c}, device_id_type=MESH)
    for axis in ("y", "z"):
        for d in (1, -1):
            pl.semaphore_signal(barrier, inc=1, device_id=dev_yz(axis, d), device_id_type=MESH)
    small = [
        pltpu.make_async_copy(a, b, sm_sem.at[i])
        for i, (a, b) in enumerate(((gain_h, gain), (gate_h, gate_m), (up_h, up_m), (down_h, down_m)))
    ]
    ld_first.start()
    for load in small:
        load.start()
    ld_tok.start()
    ld_first.wait()
    for load in small:
        load.wait()

    def norm(k, carry):
        values = toks[k].astype(F32)
        meansq = jnp.mean(values * values, axis=-1, keepdims=True)
        sent[k] = (values * lax.rsqrt(meansq + 1e-05) * gain[...]).astype(BF16)
        return carry

    norm(0, 0)
    ld_gate.start()
    ld_up.start()
    ld_down.start()
    pl.semaphore_wait(barrier, 2 * RING + 3)

    spans = ((0, 1), (1, STAGES - 1))
    for s, (first, count) in enumerate(spans):
        if s == 1:
            ld_tok.wait()
            lax.fori_loop(1, STAGES, norm, 0)
        for i in (4, 5, 2, 3, 6, 7, 1):
            peer = row_peer(i)
            send(
                sent.at[pl.ds(first, count), :, pl.ds(pl.multiple_of(peer * feats, feats), feats)],
                mixed.at[pl.ds(first, count), x, q],
                a2a_s.at[0],
                a2a_r.at[s],
                {"rows": peer, "cols": c},
            )
    mixed[:, x, q] = sent[:, :, pl.ds(pl.multiple_of(r * feats, feats), feats)]

    def spread(mask, first, count):
        blocks = mask.shape[1]
        row = lax.broadcasted_iota(jnp.int32, (blocks, count * BLOCK), 0)
        col = lax.broadcasted_iota(jnp.int32, (blocks, count * BLOCK), 1)
        place = col - (row - first) * BLOCK
        onehot = jnp.where((place >= 0) & (place < BLOCK), 1.0, 0.0).astype(BF16)
        return jnp.dot(mask[...].astype(F32).astype(BF16), onehot, preferred_element_type=F32)

    def keep(weight, mask, first, count):
        def rows_of(b, carry):
            rows = pl.ds(pl.multiple_of(b * BLOCK, BLOCK), BLOCK)
            weight[rows, :] = weight[rows, :] * mask[pl.ds(b, 1), :].astype(BF16)
            return carry

        lax.fori_loop(first, first + count, rows_of, 0)

    def mask_gu(part_of):
        if part_of == 0:
            mgu[:, 0:width] = spread(gate_m, 0, width // BLOCK)
            mgu[:, width : 2 * width] = spread(up_m, 0, width // BLOCK)
            ld_gate.wait()
            ld_up.wait()
        blocks = feats // BLOCK
        keep(wgu, mgu, part_of * blocks // 4, blocks // 4)

    def mask_d(part_of):
        if part_of == 0:
            md[...] = spread(down_m, q * (half_d // BLOCK), half_d // BLOCK)
            ld_down.wait()
        blocks = width // BLOCK
        first = part_of * blocks // 4
        keep(wd, md, first, (part_of + 1) * blocks // 4 - first)

    def a2a_wait(s):
        first, count = spans[s]
        got(sent.at[pl.ds(first, count), :, pl.ds(0, (2 * RING - 1) * feats)], a2a_s.at[0], a2a_r.at[s])

    order = (2, 1, -1, 0)

    def tile(u, h):
        return nb(x, order[2 * u + h])

    def axes(h):
        return (("y", y), ("z", z)) if h == 0 else (("z", z), ("y", y))

    def block(k, u, h, i, n=None):
        at = (k, tile(u, h), z, i) if h == 0 else (k, tile(u, h), i, y)
        return gath.at[at] if n is None else gath.at[(*at, slice(None), pl.ds(n * (feats // 2), feats // 2))]

    def slab(k, u, h, i, n=None):
        part_of = slice(None) if n is None else pl.ds(2 * n, 2)
        return gath.at[k, tile(u, h), i, part_of] if h == 0 else gath.at[k, tile(u, h), part_of, i]

    def ag_send(k, u, h, n, what, axis, d):
        send(what, what, ag_s.at[k], ag_r.at[k, u, h, n], dev_yz(axis, d))

    def ag_got(k, u, h, n, what):
        got(what, ag_s.at[k], ag_r.at[k, u, h, n])

    def ag0(k, u):
        for h in range(2):
            (a, i), _ = axes(h)
            xi = tile(u, h)
            gath[k, xi, z, y] = jnp.concatenate([mixed[k, xi, 0], mixed[k, xi, 1]], axis=0)
            for n in range(2):
                ag_send(k, u, h, n, block(k, u, h, i), a, 1 - 2 * n)

    def ag1(k, u, h, n):
        (a, i), _ = axes(h)
        d = 2 * n - 1
        ag_got(k, u, h, n, block(k, u, h, nb(i, d)))
        ag_send(k, u, h, 2, block(k, u, h, nb(i, d), n), a, -d)

    def ag2(k, u, h):
        (a, i), (b, j) = axes(h)
        ag_got(k, u, h, 2, block(k, u, h, nb(i, 2)))
        for n in range(2):
            ag_send(k, u, h, 3 + n, slab(k, u, h, j), b, 1 - 2 * n)

    def ag3(k, u, h, n):
        _, (b, j) = axes(h)
        d = 2 * n - 1
        ag_got(k, u, h, 3 + n, slab(k, u, h, nb(j, d)))
        ag_send(k, u, h, 5, slab(k, u, h, nb(j, d), n), b, -d)

    def ag4(k, u):
        for h in range(2):
            _, (b, j) = axes(h)
            ag_got(k, u, h, 5, slab(k, u, h, nb(j, 2)))

    def ag_left(k):
        left(gath.at[:, pl.ds(0, 3), :, pl.ds(0, 1)], ag_s.at[k], ag_r.at[k, 0, 0, 0])

    mine = pl.multiple_of(q * rows_h, rows_h)
    theirs = pl.multiple_of((1 - q) * rows_h, rows_h)

    def gu_tile(k, n):
        xi, s = nb(x, order[n]), k % 2
        lhs = gath[k, xi].reshape(part.shape[2], feats)
        for j in range(0, 2 * width, 256):
            cols = pl.ds(j, 256)
            part[s, xi, :, cols] = jnp.dot(lhs, wgu[:, cols], preferred_element_type=F32).astype(BF16)
        send(
            part.at[s, xi, pl.ds(theirs, rows_h)], mate.at[s, xi], q_s.at[k], q_r.at[k, n], partner
        )

    def add(ref_a, ref_b):
        return (ref_a[...].astype(F32) + ref_b[...].astype(F32)).astype(BF16)

    def add_rows(ref_a, ref_b):
        def piece(i, carry):
            rows = pl.ds(pl.multiple_of(i * 32, 32), 32)
            ref_a[rows, :] = (ref_a[rows, :].astype(F32) + ref_b[rows, :].astype(F32)).astype(BF16)
            return carry

        lax.fori_loop(0, ref_a.shape[0] // 32, piece, 0)

    def xrows(s, d, lo, count):
        return part.at[s, nb(x, d), pl.ds(pl.multiple_of(mine + lo, rel), count)]

    def gu_finish(k, n):
        d, s = order[n], k % 2
        xi = nb(x, d)
        got(mate.at[s, xi], q_s.at[k], q_r.at[k, n])
        whole = xrows(s, d, 0, rows_h)
        add_rows(whole, mate.at[s, xi])
        if d == 2:
            send(xrows(s, 2, 0, rel), xrel.at[k, 0], xr_s.at[k], xr_r.at[k, 0], dev_x(1))
            send(xrows(s, 2, rel, rel), xrel.at[k, 1], xr_s.at[k], xr_r.at[k, 1], dev_x(-1))
        elif d == 1:
            send(xrows(s, 1, rel, rel), xfin.at[k, 0, pl.ds(rel, rel)], xr_s.at[k], xr_r.at[k, 2], dev_x(1))
        elif d == -1:
            send(xrows(s, -1, 0, rel), xfin.at[k, 1, pl.ds(0, rel)], xr_s.at[k], xr_r.at[k, 2], dev_x(-1))

    def x_relay(k, n):
        s, d = k % 2, 1 - 2 * n
        got(xrel.at[k, n], xr_s.at[k], xr_r.at[k, n])
        own = xrows(s, d, n * rel, rel)
        add_rows(own, xrel.at[k, n])
        send(own, xfin.at[k, n, pl.ds(n * rel, rel)], xr_s.at[k], xr_r.at[k, 2], dev_x(d))

    def hidden(k):
        s = k % 2
        got(xfin.at[k], xr_s.at[k], xr_r.at[k, 2])
        own = xrows(s, 0, 0, rows_h)

        def piece(i, carry):
            rows = pl.ds(pl.multiple_of(i * 16, 16), 16)

            def total(cols):
                return (
                    own[rows, cols].astype(F32)
                    + xfin[k, 0, rows, cols].astype(F32)
                    + xfin[k, 1, rows, cols].astype(F32)
                )

            gate, up = total(pl.ds(0, width)), total(pl.ds(width, width))
            act = gate / (1.0 + jnp.exp(-gate)) * up
            hid[k, pl.ds(pl.multiple_of(mine + i * 16, 16), 16), :] = act.astype(BF16)
            return carry

        lax.fori_loop(0, rows_h // 16, piece, 0)
        own_h = hid.at[k, pl.ds(mine, rows_h)]
        send(own_h, own_h, h_s.at[k], h_r.at[k], partner)

    def hidden_got(k):
        got(hid.at[k, pl.ds(theirs, rows_h)], h_s.at[k], h_r.at[k])

    def down_half(k, h):
        s = k % 2
        lhs = hid[k]
        for j in range(h * col_h, (h + 1) * col_h, 256):
            cols = pl.ds(j, 256)
            outp[s, :, :, :, cols] = (
                jnp.dot(lhs, wd[:, cols], preferred_element_type=F32)
                .astype(BF16)
                .reshape(RING, RING, TILE, 256)
            )
        yr0(k, h)

    halves = (pl.ds(0, 2), pl.ds(2, 2))
    cols2 = (pl.ds(0, col_h // 2), pl.ds(col_h // 2, col_h // 2))

    def chunk(k, h, i, others):
        cols = pl.ds(h * col_h, col_h)
        if h == 0:
            return outp.at[k % 2, i, others, :, cols]
        return outp.at[k % 2, others, i, :, cols]

    def raxes(h):
        return (("z", z), ("y", y)) if h == 0 else (("y", y), ("z", z))

    def yr0(k, h):
        (a, i), _ = raxes(h)
        ss, rs = yr_s.at[k, 0], yr_r.at[k, h, 0]
        send(chunk(k, h, nb(i, 2), halves[0]), yrel.at[k, h, 0], ss, rs.at[0], dev_yz(a, 1))
        send(chunk(k, h, nb(i, 2), halves[1]), yrel.at[k, h, 1], ss, rs.at[1], dev_yz(a, -1))
        send(chunk(k, h, nb(i, 1), halves[1]), yfin.at[k, h, 0, halves[1]], ss, rs.at[2], dev_yz(a, 1))
        send(chunk(k, h, nb(i, -1), halves[0]), yfin.at[k, h, 1, halves[0]], ss, rs.at[2], dev_yz(a, -1))

    def yr1(k, h, n):
        (a, i), _ = raxes(h)
        ss, rs = yr_s.at[k, 0], yr_r.at[k, h, 0]
        d = 1 - 2 * n
        got(yrel.at[k, h, n], ss, rs.at[n])
        own = chunk(k, h, nb(i, d), halves[n])
        own[...] = add(own, yrel.at[k, h, n])
        send(own, yfin.at[k, h, n, halves[n]], ss, rs.at[2], dev_yz(a, d))

    def yr2(k, h):
        (a, i), (b, j) = raxes(h)
        ss, rs = yr_s.at[k, 0], yr_r.at[k, h, 0]
        got(yfin.at[k, h], ss, rs.at[2])
        own = chunk(k, h, i, pl.ds(0, RING))

        def piece(o, carry):
            ysum[k % 2, h, o] = (
                own[o].astype(F32) + yfin[k, h, 0, o].astype(F32) + yfin[k, h, 1, o].astype(F32)
            ).astype(BF16)
            return carry

        lax.fori_loop(0, RING, piece, 0)
        ss, rs = yr_s.at[k, 1], yr_r.at[k, h, 1]

        def sums(i, n):
            return ysum.at[k % 2, h, i, :, cols2[n]]

        send(sums(nb(j, 2), 0), y2rel.at[k, h, 0], ss, rs.at[0], dev_yz(b, 1))
        send(sums(nb(j, 2), 1), y2rel.at[k, h, 1], ss, rs.at[1], dev_yz(b, -1))
        send(sums(nb(j, 1), 1), y2fin.at[k, h, 0, :, cols2[1]], ss, rs.at[2], dev_yz(b, 1))
        send(sums(nb(j, -1), 0), y2fin.at[k, h, 1, :, cols2[0]], ss, rs.at[2], dev_yz(b, -1))

    def yr3(k, h, n):
        _, (b, j) = raxes(h)
        ss, rs = yr_s.at[k, 1], yr_r.at[k, h, 1]
        d = 1 - 2 * n
        got(y2rel.at[k, h, n], ss, rs.at[n])
        own = ysum.at[k % 2, h, nb(j, d), :, cols2[n]]
        own[...] = add(own, y2rel.at[k, h, n])
        send(own, y2fin.at[k, h, n, :, cols2[n]], ss, rs.at[2], dev_yz(b, d))

    def yr4(k, h):
        _, (b, j) = raxes(h)
        ss, rs = yr_s.at[k, 1], yr_r.at[k, h, 1]
        got(y2fin.at[k, h], ss, rs.at[2])
        total = (
            ysum[k % 2, h, j].astype(F32) + y2fin[k, h, 0].astype(F32) + y2fin[k, h, 1].astype(F32)
        )
        top, bottom = total[0:SUB], total[SUB:TILE]
        first = q == 0
        res[k, :, pl.ds(pl.multiple_of(q * half_d + h * col_h, col_h), col_h)] = jnp.where(first, top, bottom).astype(BF16)
        obuf[k, :, pl.ds(h * col_h, col_h)] = jnp.where(first, bottom, top).astype(BF16)

    def swap(k):
        send(
            obuf.at[k],
            res.at[k, :, pl.ds(pl.multiple_of(q * half_d, half_d), half_d)],
            o_s.at[k],
            o_r.at[k],
            partner,
        )

    def swap_got(k):
        got(res.at[k, :, pl.ds(pl.multiple_of((1 - q) * half_d, half_d), half_d)], o_s.at[k], o_r.at[k])

    def x_left(k):
        left(mate.at[0], q_s.at[k], q_r.at[k, 0])
        left(xrel.at[pl.ds(0, 3)], xr_s.at[k], xr_r.at[k, 0])

    def y_left(k):
        left(yrel.at[pl.ds(0, 3)], yr_s.at[k, 0], yr_r.at[k, 0, 0, 0])
        left(y2rel.at[pl.ds(0, 3)], yr_s.at[k, 1], yr_r.at[k, 0, 1, 0])

    steps = {
        "ag0": ag0, "ag1": ag1, "ag2": ag2, "ag3": ag3, "ag4": ag4, "gu": gu_tile, "gf": gu_finish,
        "xr": x_relay, "hid": hidden, "hg": hidden_got, "dn": down_half, "yr1": yr1, "yr2": yr2,
        "yr3": yr3, "yr4": yr4, "swap": swap, "xleft": x_left, "yleft": y_left,
        "mgu": mask_gu, "md": mask_d,
    }
    def store(k):
        swap_got(k)
        pltpu.make_async_copy(res.at[k], out.at[k], st_sem.at[k]).start()

    def settle(k):
        ag_left(k)
        left(hid.at[k, pl.ds(mine, rows_h)], h_s.at[k], h_r.at[k])
        if k == 0:
            left(sent.at[:, :, pl.ds(0, (2 * RING - 1) * feats)], a2a_s.at[0], a2a_r.at[0])

    last_half = {args[0]: args[1] for name, *args in ORDER if name == "yr2"}
    a2a_wait(0)
    exchanged = False
    for name, *args in ORDER:
        if name == "ag0" and args[0] > 0 and not exchanged:
            a2a_wait(1)
            exchanged = True
        steps[name](*args)
        if name == "swap" and args[0] > 0:
            store(args[0] - 1)
        if name == "yr2" and args[1] == last_half[args[0]]:
            settle(args[0])
    store(STAGES - 1)

    for k in range(STAGES):
        left(obuf.at[k], o_s.at[k], o_r.at[k])
    for k in range(STAGES):
        pltpu.make_async_copy(res.at[k], out.at[k], st_sem.at[k]).wait()


def body(tokens, norm_gain, gate_weight, up_weight, down_weight, gate_mask, up_mask, down_mask):
    own, model = tokens.shape
    feats, width = gate_weight.shape
    half_d = model // 2
    rows = RING * RING * TILE
    dma = pltpu.SemaphoreType.DMA
    anyspace = pl.BlockSpec(memory_space=pl.ANY)
    result = pl.pallas_call(
        kernel,
        out_shape=jax.ShapeDtypeStruct((STAGES, SUB, model), BF16),
        in_specs=[anyspace] * 8,
        out_specs=anyspace,
        scratch_shapes=[
            pltpu.VMEM((1, model), F32),
            pltpu.VMEM(gate_mask.shape, jnp.int32),
            pltpu.VMEM(up_mask.shape, jnp.int32),
            pltpu.VMEM(down_mask.shape, jnp.int32),
            pltpu.VMEM((STAGES, SUB, model), BF16),
            pltpu.VMEM((STAGES, SUB, model), BF16),
            pltpu.VMEM((STAGES, RING, 2, SUB, feats), BF16),
            pltpu.VMEM((STAGES, RING, RING, RING, TILE, feats), BF16),
            pltpu.VMEM((feats, 2 * width), BF16),
            pltpu.VMEM((width, half_d), BF16),
            pltpu.VMEM((feats // BLOCK, 2 * width), F32),
            pltpu.VMEM((width // BLOCK, half_d), F32),
            pltpu.VMEM((2, RING, rows, 2 * width), BF16),
            pltpu.VMEM((2, RING, rows // 2, 2 * width), BF16),
            pltpu.VMEM((STAGES, 2, rows // 4, 2 * width), BF16),
            pltpu.VMEM((STAGES, 2, rows // 2, 2 * width), BF16),
            pltpu.VMEM((STAGES, rows, width), BF16),
            pltpu.VMEM((2, RING, RING, TILE, half_d), BF16),
            pltpu.VMEM((STAGES, 2, 2, 2, TILE, half_d // 2), BF16),
            pltpu.VMEM((STAGES, 2, 2, RING, TILE, half_d // 2), BF16),
            pltpu.VMEM((2, 2, RING, TILE, half_d // 2), BF16),
            pltpu.VMEM((STAGES, 2, 2, TILE, half_d // 4), BF16),
            pltpu.VMEM((STAGES, 2, 2, TILE, half_d // 2), BF16),
            pltpu.VMEM((STAGES, SUB, model), BF16),
            pltpu.VMEM((STAGES, SUB, half_d), BF16),
            dma((4,)),
            dma((5,)),
            dma((STAGES,)),
            dma((1,)),
            dma((2,)),
            dma((STAGES,)),
            dma((STAGES, 2, 2, 6)),
            dma((STAGES,)),
            dma((STAGES, 4)),
            dma((STAGES,)),
            dma((STAGES, 3)),
            dma((STAGES,)),
            dma((STAGES,)),
            dma((STAGES, 2)),
            dma((STAGES, 2, 2, 3)),
            dma((STAGES,)),
            dma((STAGES,)),
        ],
        compiler_params=pltpu.CompilerParams(
            collective_id=0, has_side_effects=True, vmem_limit_bytes=67_000_000
        ),
    )(
        tokens.reshape(STAGES, SUB, model),
        norm_gain.reshape(1, model),
        gate_weight,
        up_weight,
        down_weight,
        gate_mask,
        up_mask,
        down_mask,
    )
    return result.reshape(own, model)


def solution(mesh):
    return jax.shard_map(
        body,
        mesh=mesh,
        in_specs=(
            P(("rows", "cols"), None),
            P(),
            P("rows", "cols"),
            P("rows", "cols"),
            P("cols", None),
            P("rows", "cols"),
            P("rows", "cols"),
            P("cols", None),
        ),
        out_specs=P(("rows", "cols"), None),
        check_vma=False,
    )
```

```python
import functools

import jax
import jax.numpy as jnp
from jax import lax
from jax.experimental import pallas as pl
from jax.experimental.pallas import tpu as pltpu
from jax.sharding import PartitionSpec as P

BLOCK = 64
STAGES = 5
SUB = 8
RING = 4
TILE = 2 * SUB
MESH = pl.DeviceIdType.MESH
BF16, F32 = jnp.bfloat16, jnp.float32

ORDER = (
    ("ag0", 0, 0), ("ag0", 0, 1), ("ag0", 0, 2), ("ag0", 0, 3), ("mgu", 0), ("mgu", 1), ("mgu", 2),
    ("ag1", 0, 0, 0, 0), ("ag1", 0, 0, 0, 1), ("ag1", 0, 0, 1, 0), ("ag1", 0, 0, 1, 1), ("ag1", 0, 1, 0, 0),
    ("ag1", 0, 1, 0, 1), ("ag1", 0, 1, 1, 0), ("ag1", 0, 1, 1, 1), ("ag1", 0, 2, 0, 0), ("ag1", 0, 2, 0, 1),
    ("ag1", 0, 2, 1, 0), ("ag1", 0, 2, 1, 1), ("ag1", 0, 3, 0, 0), ("ag1", 0, 3, 0, 1), ("ag1", 0, 3, 1, 0),
    ("ag1", 0, 3, 1, 1), ("mgu", 3), ("ag0", 1, 0), ("ag0", 1, 1), ("ag2", 0, 0, 0), ("ag2", 0, 0, 1),
    ("ag2", 0, 1, 0), ("ag2", 0, 1, 1), ("ag2", 0, 2, 0), ("ag2", 0, 2, 1), ("ag2", 0, 3, 0), ("ag2", 0, 3, 1),
    ("md", 0), ("ag1", 1, 0, 0, 0), ("ag1", 1, 0, 0, 1), ("ag1", 1, 0, 1, 0), ("ag1", 1, 0, 1, 1), ("md", 1),
    ("ag1", 1, 1, 0, 0), ("ag1", 1, 1, 0, 1), ("ag1", 1, 1, 1, 0), ("ag1", 1, 1, 1, 1), ("md", 2),
    ("ag3", 0, 0, 0, 0), ("ag3", 0, 0, 0, 1), ("ag3", 0, 0, 1, 0), ("ag3", 0, 0, 1, 1), ("ag0", 2, 0), ("md", 3),
    ("ag3", 0, 1, 0, 0), ("ag3", 0, 1, 0, 1), ("ag3", 0, 1, 1, 0), ("ag3", 0, 1, 1, 1), ("ag0", 2, 1),
    ("ag3", 0, 2, 0, 0), ("ag3", 0, 2, 0, 1), ("ag3", 0, 2, 1, 0), ("ag3", 0, 2, 1, 1), ("ag0", 3, 0),
    ("ag3", 0, 3, 0, 0), ("ag3", 0, 3, 0, 1), ("ag3", 0, 3, 1, 0), ("ag3", 0, 3, 1, 1), ("ag0", 3, 1),
    ("ag2", 1, 0, 0), ("ag2", 1, 0, 1), ("ag2", 1, 1, 0), ("ag2", 1, 1, 1), ("ag4", 0, 0), ("gu", 0, 0),
    ("ag1", 2, 0, 0, 0), ("ag1", 2, 0, 0, 1), ("ag1", 2, 0, 1, 0), ("ag1", 2, 0, 1, 1), ("ag4", 0, 1), ("gu", 0, 1),
    ("ag1", 2, 1, 0, 0), ("ag1", 2, 1, 0, 1), ("ag1", 2, 1, 1, 0), ("ag1", 2, 1, 1, 1), ("gf", 0, 0),
    ("ag1", 3, 0, 0, 0), ("ag1", 3, 0, 0, 1), ("ag1", 3, 0, 1, 0), ("ag1", 3, 0, 1, 1), ("ag4", 0, 2), ("gu", 0, 2),
    ("gf", 0, 1), ("ag1", 3, 1, 0, 0), ("ag1", 3, 1, 0, 1), ("ag1", 3, 1, 1, 0), ("ag1", 3, 1, 1, 1), ("ag4", 0, 3),
    ("gu", 0, 3), ("ag3", 1, 0, 0, 0), ("gf", 0, 2), ("ag3", 1, 0, 0, 1), ("ag3", 1, 0, 1, 0), ("ag3", 1, 0, 1, 1),
    ("ag0", 4, 0), ("gf", 0, 3), ("ag3", 1, 1, 0, 0), ("ag3", 1, 1, 0, 1), ("ag3", 1, 1, 1, 0), ("ag3", 1, 1, 1, 1),
    ("ag0", 4, 1), ("ag2", 2, 0, 0), ("xr", 0, 0), ("xr", 0, 1), ("ag2", 2, 0, 1), ("ag2", 2, 1, 0), ("ag2", 2, 1, 1),
    ("ag2", 3, 0, 0), ("ag2", 3, 0, 1), ("ag2", 3, 1, 0), ("ag2", 3, 1, 1), ("ag4", 1, 0), ("gu", 1, 0), ("gu", 1, 1),
    ("ag4", 1, 1), ("gu", 1, 2), ("gf", 1, 0), ("gu", 1, 3), ("gf", 1, 1), ("ag3", 2, 0, 0, 0), ("ag3", 2, 0, 0, 1),
    ("ag3", 2, 0, 1, 0), ("gf", 1, 2), ("ag3", 2, 0, 1, 1), ("ag1", 4, 0, 0, 0), ("ag1", 4, 0, 0, 1),
    ("ag1", 4, 0, 1, 0), ("ag1", 4, 0, 1, 1), ("ag1", 4, 1, 0, 0), ("ag1", 4, 1, 0, 1), ("ag1", 4, 1, 1, 0),
    ("ag1", 4, 1, 1, 1), ("gf", 1, 3), ("hid", 0), ("ag3", 2, 1, 0, 0), ("ag3", 2, 1, 0, 1), ("ag3", 2, 1, 1, 0),
    ("ag3", 2, 1, 1, 1), ("hg", 0), ("dn", 0, 0), ("dn", 0, 1), ("xr", 1, 0), ("xr", 1, 1), ("xleft", 0),
    ("ag3", 3, 0, 0, 0), ("ag3", 3, 0, 0, 1), ("ag3", 3, 0, 1, 0), ("ag3", 3, 0, 1, 1), ("ag3", 3, 1, 0, 0),
    ("ag3", 3, 1, 0, 1), ("ag3", 3, 1, 1, 0), ("ag3", 3, 1, 1, 1), ("ag4", 2, 0), ("gu", 2, 0), ("gu", 2, 1),
    ("ag4", 2, 1), ("gu", 2, 2), ("gf", 2, 0), ("gu", 2, 3), ("gf", 2, 1), ("yr1", 0, 0, 0), ("gf", 2, 2),
    ("yr1", 0, 0, 1), ("yr1", 0, 1, 0), ("yr1", 0, 1, 1), ("hid", 1), ("gf", 2, 3), ("ag2", 4, 0, 0),
    ("ag2", 4, 0, 1), ("ag2", 4, 1, 0), ("ag2", 4, 1, 1), ("ag4", 3, 0), ("hg", 1), ("dn", 1, 0), ("dn", 1, 1),
    ("xr", 2, 0), ("xr", 2, 1), ("xleft", 1), ("ag4", 3, 1), ("gu", 3, 0), ("yr2", 0, 0), ("yr2", 0, 1), ("gu", 3, 1),
    ("gf", 3, 0), ("ag3", 4, 0, 0, 0), ("ag3", 4, 0, 0, 1), ("ag3", 4, 0, 1, 0), ("ag3", 4, 0, 1, 1), ("gu", 3, 2),
    ("ag3", 4, 1, 0, 0), ("ag3", 4, 1, 0, 1), ("gf", 3, 1), ("ag3", 4, 1, 1, 0), ("ag3", 4, 1, 1, 1), ("gu", 3, 3),
    ("gf", 3, 2), ("yr1", 1, 0, 0), ("hid", 2), ("yr1", 1, 0, 1), ("yr1", 1, 1, 0), ("gf", 3, 3), ("yr1", 1, 1, 1),
    ("hg", 2), ("xleft", 2), ("yr3", 0, 0, 0), ("yr3", 0, 0, 1), ("yr3", 0, 1, 0), ("yr3", 0, 1, 1), ("yleft", 0),
    ("dn", 2, 0), ("dn", 2, 1), ("xr", 3, 0), ("xr", 3, 1), ("ag4", 4, 0), ("ag4", 4, 1), ("gu", 4, 0), ("gu", 4, 1),
    ("yr2", 1, 0), ("yr4", 0, 0), ("yr4", 0, 1), ("swap", 0), ("gf", 4, 0), ("yr2", 1, 1), ("gu", 4, 2), ("gf", 4, 1),
    ("yr1", 2, 0, 0), ("yr1", 2, 0, 1), ("yr1", 2, 1, 0), ("yr1", 2, 1, 1), ("hid", 3), ("gf", 4, 2), ("gu", 4, 3),
    ("yr3", 1, 0, 0), ("yr3", 1, 0, 1), ("yr3", 1, 1, 0), ("yr3", 1, 1, 1), ("yleft", 1), ("hg", 3), ("dn", 3, 0),
    ("dn", 3, 1), ("xr", 4, 0), ("xr", 4, 1), ("gf", 4, 3), ("yr4", 1, 0), ("yr4", 1, 1), ("swap", 1), ("yr2", 2, 0),
    ("yr2", 2, 1), ("xleft", 3), ("yr1", 3, 0, 0), ("yr1", 3, 0, 1), ("yr1", 3, 1, 0), ("yr1", 3, 1, 1),
    ("yr3", 2, 1, 0), ("yr3", 2, 1, 1), ("hid", 4), ("yr3", 2, 0, 0), ("yr3", 2, 0, 1), ("yleft", 2), ("yr2", 3, 0),
    ("hg", 4), ("dn", 4, 0), ("dn", 4, 1), ("yr4", 2, 0), ("yr3", 3, 0, 0), ("yr3", 3, 0, 1), ("yr4", 2, 1),
    ("yr2", 3, 1), ("swap", 2), ("xleft", 4), ("yr1", 4, 0, 0), ("yr1", 4, 0, 1), ("yr1", 4, 1, 0), ("yr1", 4, 1, 1),
    ("yr3", 3, 1, 0), ("yr3", 3, 1, 1), ("yleft", 3), ("yr4", 3, 0), ("yr2", 4, 0), ("yr4", 3, 1), ("yr2", 4, 1),
    ("swap", 3), ("yr3", 4, 0, 0), ("yr3", 4, 0, 1), ("yr3", 4, 1, 0), ("yr3", 4, 1, 1), ("yleft", 4), ("yr4", 4, 0),
    ("yr4", 4, 1), ("swap", 4),
)


def kernel(
    tok, gain_h, gate_w, up_w, down_w, gate_h, up_h, down_h, out,
    gain, gate_m, up_m, down_m, toks, sent, mixed, gath, wgu, wd, mgu, md, part, mate, xrel, xfin, hid,
    outp, yrel, yfin, ysum, y2rel, y2fin, res, obuf,
    sm_sem, ld_sem, st_sem, a2a_s, a2a_r, ag_s, ag_r, q_s, q_r, xr_s, xr_r, h_s, h_r, yr_s, yr_r, o_s, o_r,
):
    r, c = lax.axis_index("rows"), lax.axis_index("cols")
    x, q = r // 2, r % 2
    z, y = c // RING, c % RING
    width = wgu.shape[1] // 2
    feats = wgu.shape[0]
    half_d = wd.shape[1]
    col_h = half_d // 2
    rows_h = part.shape[2] // 2
    rel = rows_h // 2

    def nb(v, d):
        return (v + d + RING) % RING

    def dev_x(d):
        return {"rows": nb(x, d) * 2 + q, "cols": c}

    def dev_yz(axis, d):
        if axis == "y":
            return {"rows": r, "cols": z * RING + nb(y, d)}
        return {"rows": r, "cols": nb(z, d) * RING + y}

    partner = {"rows": x * 2 + (1 - q), "cols": c}

    def copy(src, dst, ss, rs, dev):
        return pltpu.make_async_remote_copy(
            src_ref=src, dst_ref=dst, send_sem=ss, recv_sem=rs, device_id=dev, device_id_type=MESH
        )

    def send(src, dst, ss, rs, dev):
        copy(src, dst, ss, rs, dev).start()

    def got(dst, ss, rs):
        copy(dst, dst, ss, rs, partner).wait_recv()

    def left(src, ss, rs):
        copy(src, src, ss, rs, partner).wait_send()

    ld_first = pltpu.make_async_copy(tok.at[0], toks.at[0], ld_sem.at[4])
    rest = pl.ds(1, STAGES - 1)
    ld_tok = pltpu.make_async_copy(tok.at[rest], toks.at[rest], ld_sem.at[0])
    ld_gate = pltpu.make_async_copy(gate_w, wgu.at[:, pl.ds(0, width)], ld_sem.at[1])
    ld_up = pltpu.make_async_copy(up_w, wgu.at[:, pl.ds(width, width)], ld_sem.at[2])
    ld_down = pltpu.make_async_copy(
        down_w.at[:, pl.ds(pl.multiple_of(q * half_d, half_d), half_d)], wd, ld_sem.at[3]
    )
    barrier = pltpu.get_barrier_semaphore()

    def row_peer(i):
        return (r + i) % (2 * RING)

    for i in (4, 5, 2, 3, 6, 7, 1):
        pl.semaphore_signal(barrier, inc=1, device_id={"rows": row_peer(i), "cols": c}, device_id_type=MESH)
    for axis in ("y", "z"):
        for d in (1, -1):
            pl.semaphore_signal(barrier, inc=1, device_id=dev_yz(axis, d), device_id_type=MESH)
    small = [
        pltpu.make_async_copy(a, b, sm_sem.at[i])
        for i, (a, b) in enumerate(((gain_h, gain), (gate_h, gate_m), (up_h, up_m), (down_h, down_m)))
    ]
    ld_first.start()
    for load in small:
        load.start()
    ld_tok.start()
    ld_first.wait()
    for load in small:
        load.wait()

    def norm(k, carry):
        values = toks[k].astype(F32)
        meansq = jnp.mean(values * values, axis=-1, keepdims=True)
        sent[k] = (values * lax.rsqrt(meansq + 1e-05) * gain[...]).astype(BF16)
        return carry

    norm(0, 0)
    ld_gate.start()
    ld_up.start()
    ld_down.start()
    pl.semaphore_wait(barrier, 2 * RING + 3)

    spans = ((0, 1), (1, STAGES - 1))
    for s, (first, count) in enumerate(spans):
        if s == 1:
            ld_tok.wait()
            lax.fori_loop(1, STAGES, norm, 0)
        for i in (4, 5, 2, 3, 6, 7, 1):
            peer = row_peer(i)
            send(
                sent.at[pl.ds(first, count), :, pl.ds(pl.multiple_of(peer * feats, feats), feats)],
                mixed.at[pl.ds(first, count), x, q],
                a2a_s.at[0],
                a2a_r.at[s],
                {"rows": peer, "cols": c},
            )
    mixed[:, x, q] = sent[:, :, pl.ds(pl.multiple_of(r * feats, feats), feats)]

    def spread(mask, first, count):
        blocks = mask.shape[1]
        row = lax.broadcasted_iota(jnp.int32, (blocks, count * BLOCK), 0)
        col = lax.broadcasted_iota(jnp.int32, (blocks, count * BLOCK), 1)
        place = col - (row - first) * BLOCK
        onehot = jnp.where((place >= 0) & (place < BLOCK), 1.0, 0.0).astype(BF16)
        return jnp.dot(mask[...].astype(F32).astype(BF16), onehot, preferred_element_type=F32)

    def keep(weight, mask, first, count):
        def rows_of(b, carry):
            rows = pl.ds(pl.multiple_of(b * BLOCK, BLOCK), BLOCK)
            weight[rows, :] = weight[rows, :] * mask[pl.ds(b, 1), :].astype(BF16)
            return carry

        lax.fori_loop(first, first + count, rows_of, 0)

    def mask_gu(part_of):
        if part_of == 0:
            mgu[:, 0:width] = spread(gate_m, 0, width // BLOCK)
            mgu[:, width : 2 * width] = spread(up_m, 0, width // BLOCK)
            ld_gate.wait()
            ld_up.wait()
        blocks = feats // BLOCK
        keep(wgu, mgu, part_of * blocks // 4, blocks // 4)

    def mask_d(part_of):
        if part_of == 0:
            md[...] = spread(down_m, q * (half_d // BLOCK), half_d // BLOCK)
            ld_down.wait()
        blocks = width // BLOCK
        first = part_of * blocks // 4
        keep(wd, md, first, (part_of + 1) * blocks // 4 - first)

    def a2a_wait(s):
        first, count = spans[s]
        got(sent.at[pl.ds(first, count), :, pl.ds(0, (2 * RING - 1) * feats)], a2a_s.at[0], a2a_r.at[s])

    order = (2, 1, -1, 0)

    def tile(k, u, h):
        return nb(x, order[u if k == 0 else 2 * u + h])

    def columns(k, h, n=None):
        first, count = (h * (feats // 2), feats // 2) if k == 0 else (0, feats)
        if n is None:
            return pl.ds(first, count)
        return pl.ds(first + n * (count // 2), count // 2)

    def unit(k, u):
        return u if k == 0 else RING + 2 * (k - 1) + u

    def axes(h):
        return (("y", y), ("z", z)) if h == 0 else (("z", z), ("y", y))

    def block(k, u, h, i, n=None):
        at = (k, tile(k, u, h), z, i) if h == 0 else (k, tile(k, u, h), i, y)
        return gath.at[(*at, slice(None), columns(k, h, n))]

    def slab(k, u, h, i, n=None):
        part_of = pl.ds(0, RING) if n is None else pl.ds(2 * n, 2)
        at = (i, part_of) if h == 0 else (part_of, i)
        return gath.at[(k, tile(k, u, h), *at, slice(None), columns(k, h))]

    def ag_send(k, u, h, n, what, axis, d):
        send(what, what, ag_s.at[k], ag_r.at[unit(k, u), h, n], dev_yz(axis, d))

    def ag_got(k, u, h, n, what):
        got(what, ag_s.at[k], ag_r.at[unit(k, u), h, n])

    def ag0(k, u):
        for h in range(2):
            (a, i), _ = axes(h)
            if k or h == 0:
                xi = tile(k, u, h)
                gath[k, xi, z, y] = jnp.concatenate([mixed[k, xi, 0], mixed[k, xi, 1]], axis=0)
            for n in range(2):
                ag_send(k, u, h, n, block(k, u, h, i), a, 1 - 2 * n)

    def ag1(k, u, h, n):
        (a, i), _ = axes(h)
        d = 2 * n - 1
        ag_got(k, u, h, n, block(k, u, h, nb(i, d)))
        ag_send(k, u, h, 2, block(k, u, h, nb(i, d), n), a, -d)

    def ag2(k, u, h):
        (a, i), (b, j) = axes(h)
        ag_got(k, u, h, 2, block(k, u, h, nb(i, 2)))
        for n in range(2):
            ag_send(k, u, h, 3 + n, slab(k, u, h, j), b, 1 - 2 * n)

    def ag3(k, u, h, n):
        _, (b, j) = axes(h)
        d = 2 * n - 1
        ag_got(k, u, h, 3 + n, slab(k, u, h, nb(j, d)))
        ag_send(k, u, h, 5, slab(k, u, h, nb(j, d), n), b, -d)

    def ag4(k, u):
        for h in range(2):
            _, (b, j) = axes(h)
            ag_got(k, u, h, 5, slab(k, u, h, nb(j, 2)))

    def ag_left(k):
        left(gath.at[:, pl.ds(0, 3), :, pl.ds(0, 1)], ag_s.at[k], ag_r.at[0, 0, 0])

    mine = pl.multiple_of(q * rows_h, rows_h)
    theirs = pl.multiple_of((1 - q) * rows_h, rows_h)

    def gu_tile(k, n):
        xi, s = nb(x, order[n]), k % 2
        lhs = gath[k, xi].reshape(part.shape[2], feats)
        for j in range(0, 2 * width, 256):
            cols = pl.ds(j, 256)
            part[s, xi, :, cols] = jnp.dot(lhs, wgu[:, cols], preferred_element_type=F32).astype(BF16)
        send(
            part.at[s, xi, pl.ds(theirs, rows_h)], mate.at[s, xi], q_s.at[k], q_r.at[k, n], partner
        )

    def add(ref_a, ref_b):
        return (ref_a[...].astype(F32) + ref_b[...].astype(F32)).astype(BF16)

    def add_rows(ref_a, ref_b):
        def piece(i, carry):
            rows = pl.ds(pl.multiple_of(i * 32, 32), 32)
            ref_a[rows, :] = (ref_a[rows, :].astype(F32) + ref_b[rows, :].astype(F32)).astype(BF16)
            return carry

        lax.fori_loop(0, ref_a.shape[0] // 32, piece, 0)

    def xrows(s, d, lo, count):
        return part.at[s, nb(x, d), pl.ds(pl.multiple_of(mine + lo, rel), count)]

    def gu_finish(k, n):
        d, s = order[n], k % 2
        xi = nb(x, d)
        got(mate.at[s, xi], q_s.at[k], q_r.at[k, n])
        whole = xrows(s, d, 0, rows_h)
        add_rows(whole, mate.at[s, xi])
        if d == 2:
            send(xrows(s, 2, 0, rel), xrel.at[k, 0], xr_s.at[k], xr_r.at[k, 0], dev_x(1))
            send(xrows(s, 2, rel, rel), xrel.at[k, 1], xr_s.at[k], xr_r.at[k, 1], dev_x(-1))
        elif d == 1:
            send(xrows(s, 1, rel, rel), xfin.at[k, 0, pl.ds(rel, rel)], xr_s.at[k], xr_r.at[k, 2], dev_x(1))
        elif d == -1:
            send(xrows(s, -1, 0, rel), xfin.at[k, 1, pl.ds(0, rel)], xr_s.at[k], xr_r.at[k, 2], dev_x(-1))

    def x_relay(k, n):
        s, d = k % 2, 1 - 2 * n
        got(xrel.at[k, n], xr_s.at[k], xr_r.at[k, n])
        own = xrows(s, d, n * rel, rel)
        add_rows(own, xrel.at[k, n])
        send(own, xfin.at[k, n, pl.ds(n * rel, rel)], xr_s.at[k], xr_r.at[k, 2], dev_x(d))

    def hidden(k):
        s = k % 2
        got(xfin.at[k], xr_s.at[k], xr_r.at[k, 2])
        own = xrows(s, 0, 0, rows_h)

        def piece(i, carry):
            rows = pl.ds(pl.multiple_of(i * 16, 16), 16)

            def total(cols):
                return (
                    own[rows, cols].astype(F32)
                    + xfin[k, 0, rows, cols].astype(F32)
                    + xfin[k, 1, rows, cols].astype(F32)
                )

            gate, up = total(pl.ds(0, width)), total(pl.ds(width, width))
            act = gate / (1.0 + jnp.exp(-gate)) * up
            hid[k, pl.ds(pl.multiple_of(mine + i * 16, 16), 16), :] = act.astype(BF16)
            return carry

        lax.fori_loop(0, rows_h // 16, piece, 0)
        own_h = hid.at[k, pl.ds(mine, rows_h)]
        send(own_h, own_h, h_s.at[k], h_r.at[k], partner)

    def hidden_got(k):
        got(hid.at[k, pl.ds(theirs, rows_h)], h_s.at[k], h_r.at[k])

    def down_half(k, h):
        s = k % 2
        lhs = hid[k]
        for j in range(h * col_h, (h + 1) * col_h, 256):
            cols = pl.ds(j, 256)
            outp[s, :, :, :, cols] = (
                jnp.dot(lhs, wd[:, cols], preferred_element_type=F32)
                .astype(BF16)
                .reshape(RING, RING, TILE, 256)
            )
        yr0(k, h)

    halves = (pl.ds(0, 2), pl.ds(2, 2))
    cols2 = (pl.ds(0, col_h // 2), pl.ds(col_h // 2, col_h // 2))

    def chunk(k, h, i, others):
        cols = pl.ds(h * col_h, col_h)
        if h == 0:
            return outp.at[k % 2, i, others, :, cols]
        return outp.at[k % 2, others, i, :, cols]

    def raxes(h):
        return (("z", z), ("y", y)) if h == 0 else (("y", y), ("z", z))

    def yr0(k, h):
        (a, i), _ = raxes(h)
        ss, rs = yr_s.at[k, 0], yr_r.at[k, h, 0]
        send(chunk(k, h, nb(i, 2), halves[0]), yrel.at[k, h, 0], ss, rs.at[0], dev_yz(a, 1))
        send(chunk(k, h, nb(i, 2), halves[1]), yrel.at[k, h, 1], ss, rs.at[1], dev_yz(a, -1))
        send(chunk(k, h, nb(i, 1), halves[1]), yfin.at[k, h, 0, halves[1]], ss, rs.at[2], dev_yz(a, 1))
        send(chunk(k, h, nb(i, -1), halves[0]), yfin.at[k, h, 1, halves[0]], ss, rs.at[2], dev_yz(a, -1))

    def yr1(k, h, n):
        (a, i), _ = raxes(h)
        ss, rs = yr_s.at[k, 0], yr_r.at[k, h, 0]
        d = 1 - 2 * n
        got(yrel.at[k, h, n], ss, rs.at[n])
        own = chunk(k, h, nb(i, d), halves[n])
        own[...] = add(own, yrel.at[k, h, n])
        send(own, yfin.at[k, h, n, halves[n]], ss, rs.at[2], dev_yz(a, d))

    def yr2(k, h):
        (a, i), (b, j) = raxes(h)
        ss, rs = yr_s.at[k, 0], yr_r.at[k, h, 0]
        got(yfin.at[k, h], ss, rs.at[2])
        own = chunk(k, h, i, pl.ds(0, RING))

        def piece(o, carry):
            ysum[k % 2, h, o] = (
                own[o].astype(F32) + yfin[k, h, 0, o].astype(F32) + yfin[k, h, 1, o].astype(F32)
            ).astype(BF16)
            return carry

        lax.fori_loop(0, RING, piece, 0)
        ss, rs = yr_s.at[k, 1], yr_r.at[k, h, 1]

        def sums(i, n):
            return ysum.at[k % 2, h, i, :, cols2[n]]

        send(sums(nb(j, 2), 0), y2rel.at[k, h, 0], ss, rs.at[0], dev_yz(b, 1))
        send(sums(nb(j, 2), 1), y2rel.at[k, h, 1], ss, rs.at[1], dev_yz(b, -1))
        send(sums(nb(j, 1), 1), y2fin.at[k, h, 0, :, cols2[1]], ss, rs.at[2], dev_yz(b, 1))
        send(sums(nb(j, -1), 0), y2fin.at[k, h, 1, :, cols2[0]], ss, rs.at[2], dev_yz(b, -1))

    def yr3(k, h, n):
        _, (b, j) = raxes(h)
        ss, rs = yr_s.at[k, 1], yr_r.at[k, h, 1]
        d = 1 - 2 * n
        got(y2rel.at[k, h, n], ss, rs.at[n])
        own = ysum.at[k % 2, h, nb(j, d), :, cols2[n]]
        own[...] = add(own, y2rel.at[k, h, n])
        send(own, y2fin.at[k, h, n, :, cols2[n]], ss, rs.at[2], dev_yz(b, d))

    def yr4(k, h):
        _, (b, j) = raxes(h)
        ss, rs = yr_s.at[k, 1], yr_r.at[k, h, 1]
        got(y2fin.at[k, h], ss, rs.at[2])
        total = (
            ysum[k % 2, h, j].astype(F32) + y2fin[k, h, 0].astype(F32) + y2fin[k, h, 1].astype(F32)
        )
        top, bottom = total[0:SUB], total[SUB:TILE]
        first = q == 0
        res[k, :, pl.ds(pl.multiple_of(q * half_d + h * col_h, col_h), col_h)] = jnp.where(first, top, bottom).astype(BF16)
        obuf[k, :, pl.ds(h * col_h, col_h)] = jnp.where(first, bottom, top).astype(BF16)

    def swap(k):
        send(
            obuf.at[k],
            res.at[k, :, pl.ds(pl.multiple_of(q * half_d, half_d), half_d)],
            o_s.at[k],
            o_r.at[k],
            partner,
        )

    def swap_got(k):
        got(res.at[k, :, pl.ds(pl.multiple_of((1 - q) * half_d, half_d), half_d)], o_s.at[k], o_r.at[k])

    def x_left(k):
        left(mate.at[0], q_s.at[k], q_r.at[k, 0])
        left(xrel.at[pl.ds(0, 3)], xr_s.at[k], xr_r.at[k, 0])

    def y_left(k):
        left(yrel.at[pl.ds(0, 3)], yr_s.at[k, 0], yr_r.at[k, 0, 0, 0])
        left(y2rel.at[pl.ds(0, 3)], yr_s.at[k, 1], yr_r.at[k, 0, 1, 0])

    steps = {
        "ag0": ag0, "ag1": ag1, "ag2": ag2, "ag3": ag3, "ag4": ag4, "gu": gu_tile, "gf": gu_finish,
        "xr": x_relay, "hid": hidden, "hg": hidden_got, "dn": down_half, "yr1": yr1, "yr2": yr2,
        "yr3": yr3, "yr4": yr4, "swap": swap, "xleft": x_left, "yleft": y_left,
        "mgu": mask_gu, "md": mask_d,
    }
    def store(k):
        swap_got(k)
        pltpu.make_async_copy(res.at[k], out.at[k], st_sem.at[k]).start()

    def settle(k):
        ag_left(k)
        left(hid.at[k, pl.ds(mine, rows_h)], h_s.at[k], h_r.at[k])
        if k == 0:
            left(sent.at[:, :, pl.ds(0, (2 * RING - 1) * feats)], a2a_s.at[0], a2a_r.at[0])

    last_half = {args[0]: args[1] for name, *args in ORDER if name == "yr2"}
    a2a_wait(0)
    exchanged = False
    for name, *args in ORDER:
        if name == "ag0" and args[0] > 0 and not exchanged:
            a2a_wait(1)
            exchanged = True
        steps[name](*args)
        if name == "swap" and args[0] > 0:
            store(args[0] - 1)
        if name == "yr2" and args[1] == last_half[args[0]]:
            settle(args[0])
    store(STAGES - 1)

    for k in range(STAGES):
        left(obuf.at[k], o_s.at[k], o_r.at[k])
    for k in range(STAGES):
        pltpu.make_async_copy(res.at[k], out.at[k], st_sem.at[k]).wait()


def body(tokens, norm_gain, gate_weight, up_weight, down_weight, gate_mask, up_mask, down_mask):
    own, model = tokens.shape
    feats, width = gate_weight.shape
    half_d = model // 2
    rows = RING * RING * TILE
    dma = pltpu.SemaphoreType.DMA
    anyspace = pl.BlockSpec(memory_space=pl.ANY)
    result = pl.pallas_call(
        kernel,
        out_shape=jax.ShapeDtypeStruct((STAGES, SUB, model), BF16),
        in_specs=[anyspace] * 8,
        out_specs=anyspace,
        scratch_shapes=[
            pltpu.VMEM((1, model), F32),
            pltpu.VMEM(gate_mask.shape, jnp.int32),
            pltpu.VMEM(up_mask.shape, jnp.int32),
            pltpu.VMEM(down_mask.shape, jnp.int32),
            pltpu.VMEM((STAGES, SUB, model), BF16),
            pltpu.VMEM((STAGES, SUB, model), BF16),
            pltpu.VMEM((STAGES, RING, 2, SUB, feats), BF16),
            pltpu.VMEM((STAGES, RING, RING, RING, TILE, feats), BF16),
            pltpu.VMEM((feats, 2 * width), BF16),
            pltpu.VMEM((width, half_d), BF16),
            pltpu.VMEM((feats // BLOCK, 2 * width), F32),
            pltpu.VMEM((width // BLOCK, half_d), F32),
            pltpu.VMEM((2, RING, rows, 2 * width), BF16),
            pltpu.VMEM((2, RING, rows // 2, 2 * width), BF16),
            pltpu.VMEM((STAGES, 2, rows // 4, 2 * width), BF16),
            pltpu.VMEM((STAGES, 2, rows // 2, 2 * width), BF16),
            pltpu.VMEM((STAGES, rows, width), BF16),
            pltpu.VMEM((2, RING, RING, TILE, half_d), BF16),
            pltpu.VMEM((STAGES, 2, 2, 2, TILE, half_d // 2), BF16),
            pltpu.VMEM((STAGES, 2, 2, RING, TILE, half_d // 2), BF16),
            pltpu.VMEM((2, 2, RING, TILE, half_d // 2), BF16),
            pltpu.VMEM((STAGES, 2, 2, TILE, half_d // 4), BF16),
            pltpu.VMEM((STAGES, 2, 2, TILE, half_d // 2), BF16),
            pltpu.VMEM((STAGES, SUB, model), BF16),
            pltpu.VMEM((STAGES, SUB, half_d), BF16),
            dma((4,)),
            dma((5,)),
            dma((STAGES,)),
            dma((1,)),
            dma((2,)),
            dma((STAGES,)),
            dma((RING + 2 * (STAGES - 1), 2, 6)),
            dma((STAGES,)),
            dma((STAGES, 4)),
            dma((STAGES,)),
            dma((STAGES, 3)),
            dma((STAGES,)),
            dma((STAGES,)),
            dma((STAGES, 2)),
            dma((STAGES, 2, 2, 3)),
            dma((STAGES,)),
            dma((STAGES,)),
        ],
        compiler_params=pltpu.CompilerParams(
            collective_id=0, has_side_effects=True, vmem_limit_bytes=67_000_000
        ),
    )(
        tokens.reshape(STAGES, SUB, model),
        norm_gain.reshape(1, model),
        gate_weight,
        up_weight,
        down_weight,
        gate_mask,
        up_mask,
        down_mask,
    )
    return result.reshape(own, model)


def solution(mesh):
    return jax.shard_map(
        body,
        mesh=mesh,
        in_specs=(
            P(("rows", "cols"), None),
            P(),
            P("rows", "cols"),
            P("rows", "cols"),
            P("cols", None),
            P("rows", "cols"),
            P("rows", "cols"),
            P("cols", None),
        ),
        out_specs=P(("rows", "cols"), None),
        check_vma=False,
    )
```

```python
import functools

import jax
import jax.numpy as jnp
from jax import lax
from jax.experimental import pallas as pl
from jax.experimental.pallas import tpu as pltpu
from jax.sharding import PartitionSpec as P

BLOCK = 64
STAGES = 5
SUB = 8
RING = 4
TILE = 2 * SUB
MESH = pl.DeviceIdType.MESH
BF16, F32 = jnp.bfloat16, jnp.float32

ORDER = (
    ("ag0", 0, 0), ("ag0", 0, 1), ("mgu", 0), ("mgu", 1), ("mgu", 2), ("mgu", 3), ("md", 0), ("ag1", 0, 0, 0, 1),
    ("ag1", 0, 0, 1, 1), ("ag1", 0, 0, 0, 0), ("ag1", 0, 1, 0, 0), ("ag1", 0, 1, 1, 0), ("ag1", 0, 1, 1, 1),
    ("ag1", 0, 1, 0, 1), ("ag1", 0, 0, 1, 0), ("ag0", 1, 1), ("ag0", 2, 0), ("md", 1), ("ag0", 3, 1), ("ag0", 1, 0),
    ("ag0", 2, 1), ("ag2", 0, 0, 1), ("ag2", 0, 0, 0), ("ag2", 0, 1, 1), ("ag1", 3, 1, 0, 1), ("ag2", 0, 1, 0),
    ("ag1", 1, 0, 1, 0), ("ag1", 1, 1, 1, 0), ("ag1", 1, 0, 0, 1), ("ag1", 1, 0, 0, 0), ("ag3", 0, 0, 1, 0),
    ("ag1", 1, 0, 1, 1), ("ag3", 0, 0, 0, 0), ("ag1", 1, 1, 0, 0), ("ag3", 0, 0, 0, 1), ("ag3", 0, 0, 1, 1),
    ("ag1", 3, 1, 1, 1), ("ag0", 3, 0), ("ag1", 1, 1, 1, 1), ("ag0", 4, 0), ("ag1", 2, 1, 0, 0), ("ag1", 2, 0, 1, 1),
    ("ag3", 0, 1, 1, 0), ("ag0", 4, 1), ("ag1", 3, 1, 0, 0), ("ag3", 0, 1, 0, 1), ("ag1", 1, 1, 0, 1),
    ("ag3", 0, 1, 0, 0), ("ag3", 0, 1, 1, 1), ("ag2", 1, 0, 1), ("ag1", 2, 1, 0, 1), ("ag1", 2, 0, 0, 1),
    ("ag1", 2, 1, 1, 1), ("ag2", 1, 0, 0), ("ag4", 0, 0), ("gu", 0, 0), ("gu", 0, 1), ("ag1", 4, 0, 1, 0),
    ("gf", 0, 0), ("ag1", 2, 0, 1, 0), ("ag2", 1, 1, 0), ("ag2", 1, 1, 1), ("ag4", 0, 1), ("ag1", 3, 0, 0, 1),
    ("gu", 0, 2), ("ag3", 1, 0, 0, 0), ("ag1", 4, 1, 1, 0), ("ag1", 3, 0, 0, 0), ("ag1", 4, 0, 1, 1),
    ("ag1", 2, 1, 1, 0), ("gf", 0, 1), ("ag1", 4, 1, 0, 0), ("ag1", 2, 0, 0, 0), ("ag3", 1, 0, 0, 1),
    ("ag1", 3, 0, 1, 1), ("ag3", 1, 0, 1, 0), ("ag1", 3, 0, 1, 0), ("ag3", 1, 0, 1, 1), ("gf", 0, 2),
    ("ag2", 2, 1, 0), ("ag1", 4, 1, 1, 1), ("ag2", 2, 0, 1), ("ag3", 1, 1, 1, 0), ("ag1", 4, 0, 0, 0),
    ("ag1", 4, 0, 0, 1), ("ag3", 1, 1, 1, 1), ("ag2", 2, 0, 0), ("ag1", 3, 1, 1, 0), ("md", 2), ("ag3", 1, 1, 0, 0),
    ("ag3", 1, 1, 0, 1), ("xr", 0, 0), ("xr", 0, 1), ("ag1", 4, 1, 0, 1), ("ag2", 3, 1, 0), ("gu", 0, 3),
    ("ag2", 4, 0, 1), ("ag4", 1, 0), ("gu", 1, 0), ("ag3", 2, 1, 0, 1), ("ag3", 2, 0, 1, 1), ("gu", 1, 1),
    ("ag2", 2, 1, 1), ("md", 3), ("ag3", 2, 0, 1, 0), ("ag2", 3, 0, 0), ("gf", 1, 0), ("ag2", 3, 0, 1),
    ("ag2", 3, 1, 1), ("ag3", 2, 1, 0, 0), ("ag4", 1, 1), ("gu", 1, 2), ("ag3", 2, 0, 0, 0), ("ag3", 2, 0, 0, 1),
    ("gf", 1, 1), ("gf", 0, 3), ("hid", 0), ("ag2", 4, 1, 0), ("ag3", 2, 1, 1, 0), ("gf", 1, 2), ("gu", 1, 3),
    ("ag3", 2, 1, 1, 1), ("hg", 0), ("dn", 0, 0), ("xr", 1, 1), ("dn", 0, 1), ("xr", 1, 0), ("ag4", 2, 0),
    ("ag3", 3, 0, 0, 0), ("xleft", 0), ("gu", 2, 0), ("gu", 2, 1), ("ag3", 3, 1, 1, 1), ("ag3", 3, 1, 1, 0),
    ("ag3", 3, 0, 0, 1), ("ag4", 2, 1), ("ag3", 4, 1, 0, 0), ("gu", 2, 2), ("gf", 2, 0), ("ag2", 4, 1, 1),
    ("gf", 2, 1), ("ag3", 3, 0, 1, 0), ("ag3", 4, 0, 1, 0), ("gu", 2, 3), ("ag2", 4, 0, 0), ("gf", 1, 3),
    ("ag3", 3, 1, 0, 0), ("ag3", 3, 1, 0, 1), ("yr1", 0, 0, 1), ("ag3", 3, 0, 1, 1), ("yr1", 0, 1, 1), ("gf", 2, 2),
    ("hid", 1), ("ag3", 4, 1, 0, 1), ("yr1", 0, 1, 0), ("gf", 2, 3), ("yr1", 0, 0, 0), ("hg", 1), ("xleft", 1),
    ("dn", 1, 0), ("xr", 2, 1), ("xr", 2, 0), ("dn", 1, 1), ("ag3", 4, 0, 1, 1), ("ag4", 3, 0), ("gu", 3, 0),
    ("gu", 3, 1), ("yr2", 0, 0), ("gf", 3, 0), ("gf", 3, 1), ("ag3", 4, 0, 0, 1), ("ag4", 3, 1), ("gu", 3, 2),
    ("yr1", 1, 1, 0), ("ag3", 4, 0, 0, 0), ("ag3", 4, 1, 1, 0), ("yr2", 0, 1), ("hid", 2), ("yr1", 1, 1, 1),
    ("yr1", 1, 0, 0), ("gf", 3, 2), ("yr1", 1, 0, 1), ("gu", 3, 3), ("ag3", 4, 1, 1, 1), ("ag4", 4, 0), ("hg", 2),
    ("xleft", 2), ("yr3", 0, 0, 0), ("gu", 4, 0), ("xr", 3, 0), ("xr", 3, 1), ("yr3", 0, 0, 1), ("yr3", 0, 1, 1),
    ("yr3", 0, 1, 0), ("yleft", 0), ("dn", 2, 0), ("yr2", 1, 0), ("gf", 4, 0), ("yr2", 1, 1), ("dn", 2, 1),
    ("gu", 4, 1), ("ag4", 4, 1), ("gu", 4, 2), ("yr1", 2, 0, 1), ("gf", 3, 3), ("hid", 3), ("yr3", 1, 0, 0),
    ("gf", 4, 2), ("yr4", 0, 1), ("gf", 4, 1), ("yr1", 2, 1, 1), ("yr1", 2, 1, 0), ("hg", 3), ("yr3", 1, 1, 1),
    ("yr1", 2, 0, 0), ("yr3", 1, 1, 0), ("yr3", 1, 0, 1), ("yleft", 1), ("dn", 3, 1), ("dn", 3, 0), ("xr", 4, 0),
    ("xr", 4, 1), ("gu", 4, 3), ("yr4", 0, 0), ("yr4", 1, 0), ("yr2", 2, 0), ("yr2", 2, 1), ("yr1", 3, 0, 1),
    ("gf", 4, 3), ("yr1", 3, 1, 1), ("yr1", 3, 1, 0), ("swap", 0), ("hid", 4), ("yr3", 2, 0, 0), ("yr3", 2, 1, 1),
    ("yr4", 1, 1), ("yr1", 3, 0, 0), ("yr3", 2, 0, 1), ("yr3", 2, 1, 0), ("yleft", 2), ("hg", 4), ("dn", 4, 1),
    ("dn", 4, 0), ("yr4", 2, 1), ("yr4", 2, 0), ("yr1", 4, 1, 1), ("yr1", 4, 1, 0), ("yr1", 4, 0, 0),
    ("yr1", 4, 0, 1), ("yr2", 3, 0), ("yr2", 3, 1), ("xleft", 4), ("yr2", 4, 1), ("yr3", 3, 0, 0), ("yr2", 4, 0),
    ("yr3", 3, 1, 0), ("yr3", 3, 1, 1), ("swap", 1), ("xleft", 3), ("yr3", 4, 1, 1), ("yr3", 3, 0, 1), ("yleft", 3),
    ("yr3", 4, 1, 0), ("yr3", 4, 0, 1), ("yr3", 4, 0, 0), ("yr4", 4, 1), ("yr4", 3, 1), ("swap", 2), ("yleft", 4),
    ("yr4", 3, 0), ("swap", 3), ("yr4", 4, 0), ("swap", 4),
)


def kernel(
    tok, gain_h, gate_w, up_w, down_w, gate_h, up_h, down_h, out,
    gain, gate_m, up_m, down_m, toks, sent, mixed, gath, wgu, wd, mgu, md, part, mate, xrel, xfin, hid,
    outp, yrel, yfin, ysum, y2rel, y2fin, res, obuf,
    sm_sem, ld_sem, st_sem, a2a_s, a2a_r, ag_s, ag_r, q_s, q_r, xr_s, xr_r, h_s, h_r, yr_s, yr_r, o_s, o_r,
):
    r, c = lax.axis_index("rows"), lax.axis_index("cols")
    x, q = r // 2, r % 2
    z, y = c // RING, c % RING
    width = wgu.shape[1] // 2
    feats = wgu.shape[0]
    half_d = wd.shape[1]
    col_h = half_d // 2
    rows_h = part.shape[2] // 2
    rel = rows_h // 2

    def nb(v, d):
        return (v + d + RING) % RING

    def dev_x(d):
        return {"rows": nb(x, d) * 2 + q, "cols": c}

    def dev_yz(axis, d):
        if axis == "y":
            return {"rows": r, "cols": z * RING + nb(y, d)}
        return {"rows": r, "cols": nb(z, d) * RING + y}

    partner = {"rows": x * 2 + (1 - q), "cols": c}

    def copy(src, dst, ss, rs, dev):
        return pltpu.make_async_remote_copy(
            src_ref=src, dst_ref=dst, send_sem=ss, recv_sem=rs, device_id=dev, device_id_type=MESH
        )

    def send(src, dst, ss, rs, dev):
        copy(src, dst, ss, rs, dev).start()

    def got(dst, ss, rs):
        copy(dst, dst, ss, rs, partner).wait_recv()

    def left(src, ss, rs):
        copy(src, src, ss, rs, partner).wait_send()

    ld_first = pltpu.make_async_copy(tok.at[0], toks.at[0], ld_sem.at[4])
    rest = pl.ds(1, STAGES - 1)
    ld_tok = pltpu.make_async_copy(tok.at[rest], toks.at[rest], ld_sem.at[0])
    ld_gate = pltpu.make_async_copy(gate_w, wgu.at[:, pl.ds(0, width)], ld_sem.at[1])
    ld_up = pltpu.make_async_copy(up_w, wgu.at[:, pl.ds(width, width)], ld_sem.at[2])
    ld_down = pltpu.make_async_copy(
        down_w.at[:, pl.ds(pl.multiple_of(q * half_d, half_d), half_d)], wd, ld_sem.at[3]
    )
    barrier = pltpu.get_barrier_semaphore()

    def row_peer(i):
        return (r + i) % (2 * RING)

    for i in (4, 5, 2, 3, 6, 7, 1):
        pl.semaphore_signal(barrier, inc=1, device_id={"rows": row_peer(i), "cols": c}, device_id_type=MESH)
    for axis in ("y", "z"):
        for d in (1, -1):
            pl.semaphore_signal(barrier, inc=1, device_id=dev_yz(axis, d), device_id_type=MESH)
    small = [
        pltpu.make_async_copy(a, b, sm_sem.at[i])
        for i, (a, b) in enumerate(((gain_h, gain), (gate_h, gate_m), (up_h, up_m), (down_h, down_m)))
    ]
    ld_first.start()
    for load in small:
        load.start()
    ld_tok.start()
    ld_first.wait()
    for load in small:
        load.wait()

    def norm(k, carry):
        values = toks[k].astype(F32)
        meansq = jnp.mean(values * values, axis=-1, keepdims=True)
        sent[k] = (values * lax.rsqrt(meansq + 1e-05) * gain[...]).astype(BF16)
        return carry

    norm(0, 0)
    ld_gate.start()
    ld_up.start()
    ld_down.start()
    pl.semaphore_wait(barrier, 2 * RING + 3)

    spans = ((0, 1), (1, STAGES - 1))
    for s, (first, count) in enumerate(spans):
        if s == 1:
            ld_tok.wait()
            lax.fori_loop(1, STAGES, norm, 0)
        for i in (4, 5, 2, 3, 6, 7, 1):
            peer = row_peer(i)
            send(
                sent.at[pl.ds(first, count), :, pl.ds(pl.multiple_of(peer * feats, feats), feats)],
                mixed.at[pl.ds(first, count), x, q],
                a2a_s.at[0],
                a2a_r.at[s],
                {"rows": peer, "cols": c},
            )
    mixed[:, x, q] = sent[:, :, pl.ds(pl.multiple_of(r * feats, feats), feats)]

    def spread(mask, first, count):
        blocks = mask.shape[1]
        row = lax.broadcasted_iota(jnp.int32, (blocks, count * BLOCK), 0)
        col = lax.broadcasted_iota(jnp.int32, (blocks, count * BLOCK), 1)
        place = col - (row - first) * BLOCK
        onehot = jnp.where((place >= 0) & (place < BLOCK), 1.0, 0.0).astype(BF16)
        return jnp.dot(mask[...].astype(F32).astype(BF16), onehot, preferred_element_type=F32)

    def keep(weight, mask, first, count):
        def rows_of(b, carry):
            rows = pl.ds(pl.multiple_of(b * BLOCK, BLOCK), BLOCK)
            weight[rows, :] = weight[rows, :] * mask[pl.ds(b, 1), :].astype(BF16)
            return carry

        lax.fori_loop(first, first + count, rows_of, 0)

    def mask_gu(part_of):
        if part_of == 0:
            mgu[:, 0:width] = spread(gate_m, 0, width // BLOCK)
            mgu[:, width : 2 * width] = spread(up_m, 0, width // BLOCK)
            ld_gate.wait()
            ld_up.wait()
        blocks = feats // BLOCK
        keep(wgu, mgu, part_of * blocks // 4, blocks // 4)

    def mask_d(part_of):
        if part_of == 0:
            md[...] = spread(down_m, q * (half_d // BLOCK), half_d // BLOCK)
            ld_down.wait()
        blocks = width // BLOCK
        first = part_of * blocks // 4
        keep(wd, md, first, (part_of + 1) * blocks // 4 - first)

    def a2a_wait(s):
        first, count = spans[s]
        got(sent.at[pl.ds(first, count), :, pl.ds(0, (2 * RING - 1) * feats)], a2a_s.at[0], a2a_r.at[s])

    order = (2, 1, -1, 0)

    def tile(u, h):
        return nb(x, order[2 * u + h])

    def axes(h):
        return (("y", y), ("z", z)) if h == 0 else (("z", z), ("y", y))

    def block(k, u, h, i, n=None):
        at = (k, tile(u, h), z, i) if h == 0 else (k, tile(u, h), i, y)
        return gath.at[at] if n is None else gath.at[(*at, slice(None), pl.ds(n * (feats // 2), feats // 2))]

    def slab(k, u, h, i, n=None):
        part_of = slice(None) if n is None else pl.ds(2 * n, 2)
        return gath.at[k, tile(u, h), i, part_of] if h == 0 else gath.at[k, tile(u, h), part_of, i]

    def ag_send(k, u, h, n, what, axis, d):
        send(what, what, ag_s.at[k], ag_r.at[k, u, h, n], dev_yz(axis, d))

    def ag_got(k, u, h, n, what):
        got(what, ag_s.at[k], ag_r.at[k, u, h, n])

    def ag0(k, u):
        for h in range(2):
            (a, i), _ = axes(h)
            xi = tile(u, h)
            gath[k, xi, z, y] = jnp.concatenate([mixed[k, xi, 0], mixed[k, xi, 1]], axis=0)
            for n in range(2):
                ag_send(k, u, h, n, block(k, u, h, i), a, 1 - 2 * n)

    def ag1(k, u, h, n):
        (a, i), _ = axes(h)
        d = 2 * n - 1
        ag_got(k, u, h, n, block(k, u, h, nb(i, d)))
        ag_send(k, u, h, 2, block(k, u, h, nb(i, d), n), a, -d)

    def ag2(k, u, h):
        (a, i), (b, j) = axes(h)
        ag_got(k, u, h, 2, block(k, u, h, nb(i, 2)))
        for n in range(2):
            ag_send(k, u, h, 3 + n, slab(k, u, h, j), b, 1 - 2 * n)

    def ag3(k, u, h, n):
        _, (b, j) = axes(h)
        d = 2 * n - 1
        ag_got(k, u, h, 3 + n, slab(k, u, h, nb(j, d)))
        ag_send(k, u, h, 5, slab(k, u, h, nb(j, d), n), b, -d)

    def ag4(k, u):
        for h in range(2):
            _, (b, j) = axes(h)
            ag_got(k, u, h, 5, slab(k, u, h, nb(j, 2)))

    def ag_left(k):
        left(gath.at[:, pl.ds(0, 3), :, pl.ds(0, 1)], ag_s.at[k], ag_r.at[k, 0, 0, 0])

    mine = pl.multiple_of(q * rows_h, rows_h)
    theirs = pl.multiple_of((1 - q) * rows_h, rows_h)

    def gu_tile(k, n):
        xi, s = nb(x, order[n]), k % 2
        lhs = gath[k, xi].reshape(part.shape[2], feats)
        for j in range(0, 2 * width, 256):
            cols = pl.ds(j, 256)
            part[s, xi, :, cols] = jnp.dot(lhs, wgu[:, cols], preferred_element_type=F32).astype(BF16)
        send(
            part.at[s, xi, pl.ds(theirs, rows_h)], mate.at[s, xi], q_s.at[k], q_r.at[k, n], partner
        )

    def add(ref_a, ref_b):
        return (ref_a[...].astype(F32) + ref_b[...].astype(F32)).astype(BF16)

    def add_rows(ref_a, ref_b):
        def piece(i, carry):
            rows = pl.ds(pl.multiple_of(i * 32, 32), 32)
            ref_a[rows, :] = (ref_a[rows, :].astype(F32) + ref_b[rows, :].astype(F32)).astype(BF16)
            return carry

        lax.fori_loop(0, ref_a.shape[0] // 32, piece, 0)

    def xrows(s, d, lo, count):
        return part.at[s, nb(x, d), pl.ds(pl.multiple_of(mine + lo, rel), count)]

    def gu_finish(k, n):
        d, s = order[n], k % 2
        xi = nb(x, d)
        got(mate.at[s, xi], q_s.at[k], q_r.at[k, n])
        whole = xrows(s, d, 0, rows_h)
        add_rows(whole, mate.at[s, xi])
        if d == 2:
            send(xrows(s, 2, 0, rel), xrel.at[k, 0], xr_s.at[k], xr_r.at[k, 0], dev_x(1))
            send(xrows(s, 2, rel, rel), xrel.at[k, 1], xr_s.at[k], xr_r.at[k, 1], dev_x(-1))
        elif d == 1:
            send(xrows(s, 1, rel, rel), xfin.at[k, 0, pl.ds(rel, rel)], xr_s.at[k], xr_r.at[k, 2], dev_x(1))
        elif d == -1:
            send(xrows(s, -1, 0, rel), xfin.at[k, 1, pl.ds(0, rel)], xr_s.at[k], xr_r.at[k, 2], dev_x(-1))

    def x_relay(k, n):
        s, d = k % 2, 1 - 2 * n
        got(xrel.at[k, n], xr_s.at[k], xr_r.at[k, n])
        own = xrows(s, d, n * rel, rel)
        add_rows(own, xrel.at[k, n])
        send(own, xfin.at[k, n, pl.ds(n * rel, rel)], xr_s.at[k], xr_r.at[k, 2], dev_x(d))

    def hidden(k):
        s = k % 2
        got(xfin.at[k], xr_s.at[k], xr_r.at[k, 2])
        own = xrows(s, 0, 0, rows_h)

        def piece(i, carry):
            rows = pl.ds(pl.multiple_of(i * 16, 16), 16)

            def total(cols):
                return (
                    own[rows, cols].astype(F32)
                    + xfin[k, 0, rows, cols].astype(F32)
                    + xfin[k, 1, rows, cols].astype(F32)
                )

            gate, up = total(pl.ds(0, width)), total(pl.ds(width, width))
            act = gate / (1.0 + jnp.exp(-gate)) * up
            hid[k, pl.ds(pl.multiple_of(mine + i * 16, 16), 16), :] = act.astype(BF16)
            return carry

        lax.fori_loop(0, rows_h // 16, piece, 0)
        own_h = hid.at[k, pl.ds(mine, rows_h)]
        send(own_h, own_h, h_s.at[k], h_r.at[k], partner)

    def hidden_got(k):
        got(hid.at[k, pl.ds(theirs, rows_h)], h_s.at[k], h_r.at[k])

    def down_half(k, h):
        s = k % 2
        lhs = hid[k]
        for j in range(h * col_h, (h + 1) * col_h, 256):
            cols = pl.ds(j, 256)
            outp[s, :, :, :, cols] = (
                jnp.dot(lhs, wd[:, cols], preferred_element_type=F32)
                .astype(BF16)
                .reshape(RING, RING, TILE, 256)
            )
        yr0(k, h)

    halves = (pl.ds(0, 2), pl.ds(2, 2))
    cols2 = (pl.ds(0, col_h // 2), pl.ds(col_h // 2, col_h // 2))

    def chunk(k, h, i, others):
        cols = pl.ds(h * col_h, col_h)
        if h == 0:
            return outp.at[k % 2, i, others, :, cols]
        return outp.at[k % 2, others, i, :, cols]

    def raxes(h):
        return (("z", z), ("y", y)) if h == 0 else (("y", y), ("z", z))

    def yr0(k, h):
        (a, i), _ = raxes(h)
        ss, rs = yr_s.at[k, 0], yr_r.at[k, h, 0]
        send(chunk(k, h, nb(i, 2), halves[0]), yrel.at[k, h, 0], ss, rs.at[0], dev_yz(a, 1))
        send(chunk(k, h, nb(i, 2), halves[1]), yrel.at[k, h, 1], ss, rs.at[1], dev_yz(a, -1))
        send(chunk(k, h, nb(i, 1), halves[1]), yfin.at[k, h, 0, halves[1]], ss, rs.at[2], dev_yz(a, 1))
        send(chunk(k, h, nb(i, -1), halves[0]), yfin.at[k, h, 1, halves[0]], ss, rs.at[2], dev_yz(a, -1))

    def yr1(k, h, n):
        (a, i), _ = raxes(h)
        ss, rs = yr_s.at[k, 0], yr_r.at[k, h, 0]
        d = 1 - 2 * n
        got(yrel.at[k, h, n], ss, rs.at[n])
        own = chunk(k, h, nb(i, d), halves[n])
        own[...] = add(own, yrel.at[k, h, n])
        send(own, yfin.at[k, h, n, halves[n]], ss, rs.at[2], dev_yz(a, d))

    def yr2(k, h):
        (a, i), (b, j) = raxes(h)
        ss, rs = yr_s.at[k, 0], yr_r.at[k, h, 0]
        got(yfin.at[k, h], ss, rs.at[2])
        own = chunk(k, h, i, pl.ds(0, RING))

        def piece(o, carry):
            ysum[k % 2, h, o] = (
                own[o].astype(F32) + yfin[k, h, 0, o].astype(F32) + yfin[k, h, 1, o].astype(F32)
            ).astype(BF16)
            return carry

        lax.fori_loop(0, RING, piece, 0)
        ss, rs = yr_s.at[k, 1], yr_r.at[k, h, 1]

        def sums(i, n):
            return ysum.at[k % 2, h, i, :, cols2[n]]

        send(sums(nb(j, 2), 0), y2rel.at[k, h, 0], ss, rs.at[0], dev_yz(b, 1))
        send(sums(nb(j, 2), 1), y2rel.at[k, h, 1], ss, rs.at[1], dev_yz(b, -1))
        send(sums(nb(j, 1), 1), y2fin.at[k, h, 0, :, cols2[1]], ss, rs.at[2], dev_yz(b, 1))
        send(sums(nb(j, -1), 0), y2fin.at[k, h, 1, :, cols2[0]], ss, rs.at[2], dev_yz(b, -1))

    def yr3(k, h, n):
        _, (b, j) = raxes(h)
        ss, rs = yr_s.at[k, 1], yr_r.at[k, h, 1]
        d = 1 - 2 * n
        got(y2rel.at[k, h, n], ss, rs.at[n])
        own = ysum.at[k % 2, h, nb(j, d), :, cols2[n]]
        own[...] = add(own, y2rel.at[k, h, n])
        send(own, y2fin.at[k, h, n, :, cols2[n]], ss, rs.at[2], dev_yz(b, d))

    def yr4(k, h):
        _, (b, j) = raxes(h)
        ss, rs = yr_s.at[k, 1], yr_r.at[k, h, 1]
        got(y2fin.at[k, h], ss, rs.at[2])
        total = (
            ysum[k % 2, h, j].astype(F32) + y2fin[k, h, 0].astype(F32) + y2fin[k, h, 1].astype(F32)
        )
        top, bottom = total[0:SUB], total[SUB:TILE]
        first = q == 0
        res[k, :, pl.ds(pl.multiple_of(q * half_d + h * col_h, col_h), col_h)] = jnp.where(first, top, bottom).astype(BF16)
        obuf[k, :, pl.ds(h * col_h, col_h)] = jnp.where(first, bottom, top).astype(BF16)

    def swap(k):
        send(
            obuf.at[k],
            res.at[k, :, pl.ds(pl.multiple_of(q * half_d, half_d), half_d)],
            o_s.at[k],
            o_r.at[k],
            partner,
        )

    def swap_got(k):
        got(res.at[k, :, pl.ds(pl.multiple_of((1 - q) * half_d, half_d), half_d)], o_s.at[k], o_r.at[k])

    def x_left(k):
        left(mate.at[0], q_s.at[k], q_r.at[k, 0])
        left(xrel.at[pl.ds(0, 3)], xr_s.at[k], xr_r.at[k, 0])

    def y_left(k):
        left(yrel.at[pl.ds(0, 3)], yr_s.at[k, 0], yr_r.at[k, 0, 0, 0])
        left(y2rel.at[pl.ds(0, 3)], yr_s.at[k, 1], yr_r.at[k, 0, 1, 0])

    steps = {
        "ag0": ag0, "ag1": ag1, "ag2": ag2, "ag3": ag3, "ag4": ag4, "gu": gu_tile, "gf": gu_finish,
        "xr": x_relay, "hid": hidden, "hg": hidden_got, "dn": down_half, "yr1": yr1, "yr2": yr2,
        "yr3": yr3, "yr4": yr4, "swap": swap, "xleft": x_left, "yleft": y_left,
        "mgu": mask_gu, "md": mask_d,
    }
    def store(k):
        swap_got(k)
        pltpu.make_async_copy(res.at[k], out.at[k], st_sem.at[k]).start()

    def settle(k):
        ag_left(k)
        left(hid.at[k, pl.ds(mine, rows_h)], h_s.at[k], h_r.at[k])
        if k == 0:
            left(sent.at[:, :, pl.ds(0, (2 * RING - 1) * feats)], a2a_s.at[0], a2a_r.at[0])

    last_half = {args[0]: args[1] for name, *args in ORDER if name == "yr2"}
    a2a_wait(0)
    exchanged = False
    for name, *args in ORDER:
        if name == "ag0" and args[0] > 0 and not exchanged:
            a2a_wait(1)
            exchanged = True
        steps[name](*args)
        if name == "swap" and args[0] > 0:
            store(args[0] - 1)
        if name == "yr2" and args[1] == last_half[args[0]]:
            settle(args[0])
    store(STAGES - 1)

    for k in range(STAGES):
        left(obuf.at[k], o_s.at[k], o_r.at[k])
    for k in range(STAGES):
        pltpu.make_async_copy(res.at[k], out.at[k], st_sem.at[k]).wait()


def body(tokens, norm_gain, gate_weight, up_weight, down_weight, gate_mask, up_mask, down_mask):
    own, model = tokens.shape
    feats, width = gate_weight.shape
    half_d = model // 2
    rows = RING * RING * TILE
    dma = pltpu.SemaphoreType.DMA
    anyspace = pl.BlockSpec(memory_space=pl.ANY)
    result = pl.pallas_call(
        kernel,
        out_shape=jax.ShapeDtypeStruct((STAGES, SUB, model), BF16),
        in_specs=[anyspace] * 8,
        out_specs=anyspace,
        scratch_shapes=[
            pltpu.VMEM((1, model), F32),
            pltpu.VMEM(gate_mask.shape, jnp.int32),
            pltpu.VMEM(up_mask.shape, jnp.int32),
            pltpu.VMEM(down_mask.shape, jnp.int32),
            pltpu.VMEM((STAGES, SUB, model), BF16),
            pltpu.VMEM((STAGES, SUB, model), BF16),
            pltpu.VMEM((STAGES, RING, 2, SUB, feats), BF16),
            pltpu.VMEM((STAGES, RING, RING, RING, TILE, feats), BF16),
            pltpu.VMEM((feats, 2 * width), BF16),
            pltpu.VMEM((width, half_d), BF16),
            pltpu.VMEM((feats // BLOCK, 2 * width), F32),
            pltpu.VMEM((width // BLOCK, half_d), F32),
            pltpu.VMEM((2, RING, rows, 2 * width), BF16),
            pltpu.VMEM((2, RING, rows // 2, 2 * width), BF16),
            pltpu.VMEM((STAGES, 2, rows // 4, 2 * width), BF16),
            pltpu.VMEM((STAGES, 2, rows // 2, 2 * width), BF16),
            pltpu.VMEM((STAGES, rows, width), BF16),
            pltpu.VMEM((2, RING, RING, TILE, half_d), BF16),
            pltpu.VMEM((STAGES, 2, 2, 2, TILE, half_d // 2), BF16),
            pltpu.VMEM((STAGES, 2, 2, RING, TILE, half_d // 2), BF16),
            pltpu.VMEM((2, 2, RING, TILE, half_d // 2), BF16),
            pltpu.VMEM((STAGES, 2, 2, TILE, half_d // 4), BF16),
            pltpu.VMEM((STAGES, 2, 2, TILE, half_d // 2), BF16),
            pltpu.VMEM((STAGES, SUB, model), BF16),
            pltpu.VMEM((STAGES, SUB, half_d), BF16),
            dma((4,)),
            dma((5,)),
            dma((STAGES,)),
            dma((1,)),
            dma((2,)),
            dma((STAGES,)),
            dma((STAGES, 2, 2, 6)),
            dma((STAGES,)),
            dma((STAGES, 4)),
            dma((STAGES,)),
            dma((STAGES, 3)),
            dma((STAGES,)),
            dma((STAGES,)),
            dma((STAGES, 2)),
            dma((STAGES, 2, 2, 3)),
            dma((STAGES,)),
            dma((STAGES,)),
        ],
        compiler_params=pltpu.CompilerParams(
            collective_id=0, has_side_effects=True, vmem_limit_bytes=67_000_000
        ),
    )(
        tokens.reshape(STAGES, SUB, model),
        norm_gain.reshape(1, model),
        gate_weight,
        up_weight,
        down_weight,
        gate_mask,
        up_mask,
        down_mask,
    )
    return result.reshape(own, model)


def solution(mesh):
    return jax.shard_map(
        body,
        mesh=mesh,
        in_specs=(
            P(("rows", "cols"), None),
            P(),
            P("rows", "cols"),
            P("rows", "cols"),
            P("cols", None),
            P("rows", "cols"),
            P("rows", "cols"),
            P("cols", None),
        ),
        out_specs=P(("rows", "cols"), None),
        check_vma=False,
    )
```

```python
import functools

import jax
import jax.numpy as jnp
from jax import lax
from jax.experimental import pallas as pl
from jax.experimental.pallas import tpu as pltpu
from jax.sharding import PartitionSpec as P

BLOCK = 64
STAGES = 5
SUB = 8
RING = 4
TILE = 2 * SUB
MESH = pl.DeviceIdType.MESH
BF16, F32 = jnp.bfloat16, jnp.float32

ORDER = (
    ("ag0", 0, 0), ("ag0", 0, 1), ("mgu", 0), ("mgu", 1), ("mgu", 2), ("mgu", 3), ("md", 0), ("ag1", 0, 0, 0, 0),
    ("ag1", 0, 0, 0, 1), ("ag1", 0, 0, 1, 0), ("ag1", 0, 0, 1, 1), ("ag1", 0, 1, 0, 0), ("ag1", 0, 1, 0, 1),
    ("ag1", 0, 1, 1, 0), ("ag1", 0, 1, 1, 1), ("ag0", 1, 0), ("ag0", 1, 1), ("ag0", 2, 0), ("md", 1),
    ("ag2", 0, 0, 0), ("ag2", 0, 0, 1), ("ag2", 0, 1, 0), ("ag2", 0, 1, 1), ("md", 2), ("ag1", 1, 0, 0, 0),
    ("ag1", 1, 0, 0, 1), ("ag1", 1, 0, 1, 0), ("ag1", 1, 0, 1, 1), ("ag1", 1, 1, 0, 0), ("ag1", 1, 1, 0, 1),
    ("ag1", 1, 1, 1, 0), ("ag1", 1, 1, 1, 1), ("ag1", 2, 0, 0, 0), ("ag1", 2, 0, 0, 1), ("ag1", 2, 0, 1, 0),
    ("ag1", 2, 0, 1, 1), ("md", 3), ("ag3", 0, 0, 0, 0), ("ag3", 0, 0, 0, 1), ("ag3", 0, 0, 1, 0),
    ("ag3", 0, 0, 1, 1), ("ag0", 2, 1), ("ag3", 0, 1, 0, 0), ("ag3", 0, 1, 0, 1), ("ag3", 0, 1, 1, 0),
    ("ag3", 0, 1, 1, 1), ("ag2", 1, 0, 0), ("ag2", 1, 0, 1), ("ag2", 1, 1, 0), ("ag2", 1, 1, 1), ("ag2", 2, 0, 0),
    ("ag2", 2, 0, 1), ("ag0", 3, 0), ("ag4", 0, 0), ("gu", 0, 0), ("ag1", 2, 1, 0, 0), ("ag1", 2, 1, 0, 1),
    ("ag1", 2, 1, 1, 0), ("ag1", 2, 1, 1, 1), ("gu", 0, 1), ("ag4", 0, 1), ("gu", 0, 2), ("gf", 0, 0),
    ("ag3", 1, 0, 0, 0), ("ag3", 1, 0, 0, 1), ("ag3", 1, 0, 1, 0), ("ag3", 1, 0, 1, 1), ("ag0", 3, 1), ("gf", 0, 1),
    ("gu", 0, 3), ("gf", 0, 2), ("ag3", 1, 1, 0, 0), ("ag3", 1, 1, 0, 1), ("ag3", 1, 1, 1, 0), ("ag3", 1, 1, 1, 1),
    ("ag0", 4, 0), ("gf", 0, 3), ("ag3", 2, 0, 0, 0), ("ag3", 2, 0, 0, 1), ("ag3", 2, 0, 1, 0), ("ag3", 2, 0, 1, 1),
    ("ag1", 3, 0, 0, 0), ("ag1", 3, 0, 0, 1), ("ag1", 3, 0, 1, 0), ("ag1", 3, 0, 1, 1), ("ag2", 2, 1, 0),
    ("ag2", 2, 1, 1), ("ag0", 4, 1), ("xr", 0, 0), ("ag4", 1, 0), ("xr", 0, 1), ("gu", 1, 0), ("ag1", 3, 1, 0, 0),
    ("ag1", 3, 1, 0, 1), ("ag1", 3, 1, 1, 0), ("ag4", 1, 1), ("ag1", 3, 1, 1, 1), ("gu", 1, 1), ("ag1", 4, 0, 0, 0),
    ("ag1", 4, 0, 0, 1), ("ag1", 4, 0, 1, 0), ("ag1", 4, 0, 1, 1), ("ag4", 2, 0), ("ag2", 3, 0, 0), ("ag2", 3, 0, 1),
    ("gf", 1, 0), ("gu", 1, 2), ("gf", 1, 1), ("gu", 1, 3), ("ag1", 4, 1, 0, 0), ("ag1", 4, 1, 0, 1),
    ("ag1", 4, 1, 1, 0), ("ag1", 4, 1, 1, 1), ("ag2", 3, 1, 0), ("ag2", 3, 1, 1), ("ag2", 4, 0, 0), ("ag2", 4, 0, 1),
    ("ag3", 2, 1, 0, 0), ("ag3", 2, 1, 0, 1), ("ag3", 2, 1, 1, 0), ("ag3", 2, 1, 1, 1), ("gf", 1, 2), ("gf", 1, 3),
    ("hid", 0), ("ag3", 3, 0, 0, 0), ("ag2", 4, 1, 0), ("ag2", 4, 1, 1), ("ag3", 3, 0, 0, 1), ("ag3", 3, 0, 1, 0),
    ("ag3", 3, 0, 1, 1), ("hg", 0), ("dn", 0, 0), ("ag3", 3, 1, 0, 0), ("ag3", 3, 1, 0, 1), ("ag3", 3, 1, 1, 0),
    ("ag3", 3, 1, 1, 1), ("xr", 1, 0), ("xr", 1, 1), ("dn", 0, 1), ("xleft", 0), ("gu", 2, 0), ("ag3", 4, 0, 0, 0),
    ("ag3", 4, 0, 0, 1), ("ag4", 2, 1), ("ag3", 4, 0, 1, 0), ("ag3", 4, 0, 1, 1), ("gu", 2, 1), ("gf", 2, 0),
    ("gu", 2, 2), ("ag3", 4, 1, 0, 1), ("ag3", 4, 1, 1, 0), ("ag3", 4, 1, 1, 1), ("gf", 2, 1), ("ag4", 3, 0),
    ("ag3", 4, 1, 0, 0), ("hid", 1), ("gf", 2, 2), ("gu", 2, 3), ("hg", 1), ("yr1", 0, 0, 0), ("yr1", 0, 0, 1),
    ("dn", 1, 0), ("yr1", 0, 1, 0), ("yr1", 0, 1, 1), ("xr", 2, 0), ("xr", 2, 1), ("gf", 2, 3), ("dn", 1, 1),
    ("ag4", 3, 1), ("xleft", 1), ("gu", 3, 0), ("ag4", 4, 0), ("gu", 3, 1), ("ag4", 4, 1), ("gu", 3, 2), ("gf", 3, 0),
    ("gu", 3, 3), ("yr2", 0, 0), ("yr2", 0, 1), ("gf", 3, 1), ("hid", 2), ("yr1", 1, 0, 0), ("yr1", 1, 0, 1),
    ("yr1", 1, 1, 0), ("yr1", 1, 1, 1), ("gf", 3, 2), ("hg", 2), ("gf", 3, 3), ("xleft", 2), ("gu", 4, 0),
    ("yr3", 0, 0, 0), ("yr3", 0, 0, 1), ("yr3", 0, 1, 0), ("yr3", 0, 1, 1), ("yleft", 0), ("xr", 3, 0), ("xr", 3, 1),
    ("dn", 2, 0), ("dn", 2, 1), ("yr2", 1, 0), ("yr2", 1, 1), ("yr4", 0, 0), ("yr4", 0, 1), ("swap", 0), ("gf", 4, 0),
    ("gu", 4, 1), ("gu", 4, 2), ("yr1", 2, 0, 0), ("yr1", 2, 0, 1), ("yr1", 2, 1, 0), ("gf", 4, 1), ("yr1", 2, 1, 1),
    ("hid", 3), ("yr3", 1, 1, 0), ("yr3", 1, 1, 1), ("gf", 4, 2), ("gu", 4, 3), ("hg", 3), ("yr3", 1, 0, 0),
    ("yr3", 1, 0, 1), ("yleft", 1), ("dn", 3, 0), ("yr2", 2, 0), ("xr", 4, 0), ("xr", 4, 1), ("yr2", 2, 1),
    ("gf", 4, 3), ("yr4", 1, 0), ("yr4", 1, 1), ("swap", 1), ("dn", 3, 1), ("xleft", 3), ("yr3", 2, 0, 0),
    ("yr3", 2, 0, 1), ("yr1", 3, 0, 0), ("yr1", 3, 0, 1), ("yr3", 2, 1, 0), ("yr3", 2, 1, 1), ("yleft", 2),
    ("yr1", 3, 1, 0), ("yr1", 3, 1, 1), ("hid", 4), ("yr2", 3, 0), ("hg", 4), ("dn", 4, 0), ("dn", 4, 1),
    ("yr2", 3, 1), ("xleft", 4), ("yr4", 2, 0), ("yr4", 2, 1), ("swap", 2), ("yr3", 3, 0, 0), ("yr3", 3, 0, 1),
    ("yr1", 4, 0, 0), ("yr1", 4, 0, 1), ("yr1", 4, 1, 0), ("yr1", 4, 1, 1), ("yr3", 3, 1, 0), ("yr3", 3, 1, 1),
    ("yleft", 3), ("yr4", 3, 0), ("yr2", 4, 0), ("yr2", 4, 1), ("yr4", 3, 1), ("swap", 3), ("yr3", 4, 0, 0),
    ("yr3", 4, 0, 1), ("yr3", 4, 1, 0), ("yr3", 4, 1, 1), ("yleft", 4), ("yr4", 4, 0), ("yr4", 4, 1), ("swap", 4),
)


def kernel(
    tok, gain_h, gate_w, up_w, down_w, gate_h, up_h, down_h, out,
    gain, gate_m, up_m, down_m, toks, sent, mixed, gath, wgu, wd, mgu, md, part, mate, xrel, xfin, hid,
    outp, yrel, yfin, ysum, y2rel, y2fin, res, obuf,
    sm_sem, ld_sem, st_sem, a2a_s, a2a_r, ag_s, ag_r, q_s, q_r, xr_s, xr_r, h_s, h_r, yr_s, yr_r, o_s, o_r,
):
    r, c = lax.axis_index("rows"), lax.axis_index("cols")
    x, q = r // 2, r % 2
    z, y = c // RING, c % RING
    width = wgu.shape[1] // 2
    feats = wgu.shape[0]
    half_d = wd.shape[1]
    col_h = half_d // 2
    rows_h = part.shape[2] // 2
    rel = rows_h // 2

    def nb(v, d):
        return (v + d + RING) % RING

    def dev_x(d):
        return {"rows": nb(x, d) * 2 + q, "cols": c}

    def dev_yz(axis, d):
        if axis == "y":
            return {"rows": r, "cols": z * RING + nb(y, d)}
        return {"rows": r, "cols": nb(z, d) * RING + y}

    partner = {"rows": x * 2 + (1 - q), "cols": c}

    def copy(src, dst, ss, rs, dev):
        return pltpu.make_async_remote_copy(
            src_ref=src, dst_ref=dst, send_sem=ss, recv_sem=rs, device_id=dev, device_id_type=MESH
        )

    def send(src, dst, ss, rs, dev):
        copy(src, dst, ss, rs, dev).start()

    def got(dst, ss, rs):
        copy(dst, dst, ss, rs, partner).wait_recv()

    def left(src, ss, rs):
        copy(src, src, ss, rs, partner).wait_send()

    ld_first = pltpu.make_async_copy(tok.at[0], toks.at[0], ld_sem.at[4])
    rest = pl.ds(1, STAGES - 1)
    ld_tok = pltpu.make_async_copy(tok.at[rest], toks.at[rest], ld_sem.at[0])
    ld_gate = pltpu.make_async_copy(gate_w, wgu.at[:, pl.ds(0, width)], ld_sem.at[1])
    ld_up = pltpu.make_async_copy(up_w, wgu.at[:, pl.ds(width, width)], ld_sem.at[2])
    ld_down = pltpu.make_async_copy(
        down_w.at[:, pl.ds(pl.multiple_of(q * half_d, half_d), half_d)], wd, ld_sem.at[3]
    )
    barrier = pltpu.get_barrier_semaphore()

    def row_peer(i):
        return (r + i) % (2 * RING)

    for i in (4, 5, 2, 3, 6, 7, 1):
        pl.semaphore_signal(barrier, inc=1, device_id={"rows": row_peer(i), "cols": c}, device_id_type=MESH)
    for axis in ("y", "z"):
        for d in (1, -1):
            pl.semaphore_signal(barrier, inc=1, device_id=dev_yz(axis, d), device_id_type=MESH)
    small = [
        pltpu.make_async_copy(a, b, sm_sem.at[i])
        for i, (a, b) in enumerate(((gain_h, gain), (gate_h, gate_m), (up_h, up_m), (down_h, down_m)))
    ]
    ld_first.start()
    for load in small:
        load.start()
    ld_tok.start()
    ld_first.wait()
    for load in small:
        load.wait()

    def norm(k, carry):
        values = toks[k].astype(F32)
        meansq = jnp.mean(values * values, axis=-1, keepdims=True)
        sent[k] = (values * lax.rsqrt(meansq + 1e-05) * gain[...]).astype(BF16)
        return carry

    norm(0, 0)
    ld_gate.start()
    ld_up.start()
    ld_down.start()
    pl.semaphore_wait(barrier, 2 * RING + 3)

    spans = ((0, 1), (1, STAGES - 1))
    for s, (first, count) in enumerate(spans):
        if s == 1:
            ld_tok.wait()
            lax.fori_loop(1, STAGES, norm, 0)
        for i in (4, 5, 2, 3, 6, 7, 1):
            peer = row_peer(i)
            send(
                sent.at[pl.ds(first, count), :, pl.ds(pl.multiple_of(peer * feats, feats), feats)],
                mixed.at[pl.ds(first, count), x, q],
                a2a_s.at[0],
                a2a_r.at[s],
                {"rows": peer, "cols": c},
            )
    mixed[:, x, q] = sent[:, :, pl.ds(pl.multiple_of(r * feats, feats), feats)]

    def spread(mask, first, count):
        blocks = mask.shape[1]
        row = lax.broadcasted_iota(jnp.int32, (blocks, count * BLOCK), 0)
        col = lax.broadcasted_iota(jnp.int32, (blocks, count * BLOCK), 1)
        place = col - (row - first) * BLOCK
        onehot = jnp.where((place >= 0) & (place < BLOCK), 1.0, 0.0).astype(BF16)
        return jnp.dot(mask[...].astype(F32).astype(BF16), onehot, preferred_element_type=F32)

    def keep(weight, mask, first, count):
        def rows_of(b, carry):
            rows = pl.ds(pl.multiple_of(b * BLOCK, BLOCK), BLOCK)
            weight[rows, :] = weight[rows, :] * mask[pl.ds(b, 1), :].astype(BF16)
            return carry

        lax.fori_loop(first, first + count, rows_of, 0)

    def mask_gu(part_of):
        if part_of == 0:
            mgu[:, 0:width] = spread(gate_m, 0, width // BLOCK)
            mgu[:, width : 2 * width] = spread(up_m, 0, width // BLOCK)
            ld_gate.wait()
            ld_up.wait()
        blocks = feats // BLOCK
        keep(wgu, mgu, part_of * blocks // 4, blocks // 4)

    def mask_d(part_of):
        if part_of == 0:
            md[...] = spread(down_m, q * (half_d // BLOCK), half_d // BLOCK)
            ld_down.wait()
        blocks = width // BLOCK
        first = part_of * blocks // 4
        keep(wd, md, first, (part_of + 1) * blocks // 4 - first)

    def a2a_wait(s):
        first, count = spans[s]
        got(sent.at[pl.ds(first, count), :, pl.ds(0, (2 * RING - 1) * feats)], a2a_s.at[0], a2a_r.at[s])

    order = (2, 1, -1, 0)

    def tile(u, h):
        return nb(x, order[2 * u + h])

    def axes(h):
        return (("y", y), ("z", z)) if h == 0 else (("z", z), ("y", y))

    def block(k, u, h, i, n=None):
        at = (k, tile(u, h), z, i) if h == 0 else (k, tile(u, h), i, y)
        return gath.at[at] if n is None else gath.at[(*at, slice(None), pl.ds(n * (feats // 2), feats // 2))]

    def slab(k, u, h, i, n=None):
        part_of = slice(None) if n is None else pl.ds(2 * n, 2)
        return gath.at[k, tile(u, h), i, part_of] if h == 0 else gath.at[k, tile(u, h), part_of, i]

    def ag_send(k, u, h, n, what, axis, d):
        send(what, what, ag_s.at[k], ag_r.at[k, u, h, n], dev_yz(axis, d))

    def ag_got(k, u, h, n, what):
        got(what, ag_s.at[k], ag_r.at[k, u, h, n])

    def ag0(k, u):
        for h in range(2):
            (a, i), _ = axes(h)
            xi = tile(u, h)
            gath[k, xi, z, y] = jnp.concatenate([mixed[k, xi, 0], mixed[k, xi, 1]], axis=0)
            for n in range(2):
                ag_send(k, u, h, n, block(k, u, h, i), a, 1 - 2 * n)

    def ag1(k, u, h, n):
        (a, i), _ = axes(h)
        d = 2 * n - 1
        ag_got(k, u, h, n, block(k, u, h, nb(i, d)))
        ag_send(k, u, h, 2, block(k, u, h, nb(i, d), n), a, -d)

    def ag2(k, u, h):
        (a, i), (b, j) = axes(h)
        ag_got(k, u, h, 2, block(k, u, h, nb(i, 2)))
        for n in range(2):
            ag_send(k, u, h, 3 + n, slab(k, u, h, j), b, 1 - 2 * n)

    def ag3(k, u, h, n):
        _, (b, j) = axes(h)
        d = 2 * n - 1
        ag_got(k, u, h, 3 + n, slab(k, u, h, nb(j, d)))
        ag_send(k, u, h, 5, slab(k, u, h, nb(j, d), n), b, -d)

    def ag4(k, u):
        for h in range(2):
            _, (b, j) = axes(h)
            ag_got(k, u, h, 5, slab(k, u, h, nb(j, 2)))

    def ag_left(k):
        left(gath.at[:, pl.ds(0, 3), :, pl.ds(0, 1)], ag_s.at[k], ag_r.at[k, 0, 0, 0])

    mine = pl.multiple_of(q * rows_h, rows_h)
    theirs = pl.multiple_of((1 - q) * rows_h, rows_h)

    def gu_tile(k, n):
        xi, s = nb(x, order[n]), k % 2
        lhs = gath[k, xi].reshape(part.shape[2], feats)
        for j in range(0, 2 * width, 256):
            cols = pl.ds(j, 256)
            part[s, xi, :, cols] = jnp.dot(lhs, wgu[:, cols], preferred_element_type=F32).astype(BF16)
        send(
            part.at[s, xi, pl.ds(theirs, rows_h)], mate.at[s, xi], q_s.at[k], q_r.at[k, n], partner
        )

    def add(ref_a, ref_b):
        return (ref_a[...].astype(F32) + ref_b[...].astype(F32)).astype(BF16)

    def add_rows(ref_a, ref_b):
        def piece(i, carry):
            rows = pl.ds(pl.multiple_of(i * 32, 32), 32)
            ref_a[rows, :] = (ref_a[rows, :].astype(F32) + ref_b[rows, :].astype(F32)).astype(BF16)
            return carry

        lax.fori_loop(0, ref_a.shape[0] // 32, piece, 0)

    def xrows(s, d, lo, count):
        return part.at[s, nb(x, d), pl.ds(pl.multiple_of(mine + lo, rel), count)]

    def gu_finish(k, n):
        d, s = order[n], k % 2
        xi = nb(x, d)
        got(mate.at[s, xi], q_s.at[k], q_r.at[k, n])
        whole = xrows(s, d, 0, rows_h)
        add_rows(whole, mate.at[s, xi])
        if d == 2:
            send(xrows(s, 2, 0, rel), xrel.at[k, 0], xr_s.at[k], xr_r.at[k, 0], dev_x(1))
            send(xrows(s, 2, rel, rel), xrel.at[k, 1], xr_s.at[k], xr_r.at[k, 1], dev_x(-1))
        elif d == 1:
            send(xrows(s, 1, rel, rel), xfin.at[k, 0, pl.ds(rel, rel)], xr_s.at[k], xr_r.at[k, 2], dev_x(1))
        elif d == -1:
            send(xrows(s, -1, 0, rel), xfin.at[k, 1, pl.ds(0, rel)], xr_s.at[k], xr_r.at[k, 2], dev_x(-1))

    def x_relay(k, n):
        s, d = k % 2, 1 - 2 * n
        got(xrel.at[k, n], xr_s.at[k], xr_r.at[k, n])
        own = xrows(s, d, n * rel, rel)
        add_rows(own, xrel.at[k, n])
        send(own, xfin.at[k, n, pl.ds(n * rel, rel)], xr_s.at[k], xr_r.at[k, 2], dev_x(d))

    def hidden(k):
        s = k % 2
        got(xfin.at[k], xr_s.at[k], xr_r.at[k, 2])
        own = xrows(s, 0, 0, rows_h)

        def piece(i, carry):
            rows = pl.ds(pl.multiple_of(i * 16, 16), 16)

            def total(cols):
                return (
                    own[rows, cols].astype(F32)
                    + xfin[k, 0, rows, cols].astype(F32)
                    + xfin[k, 1, rows, cols].astype(F32)
                )

            gate, up = total(pl.ds(0, width)), total(pl.ds(width, width))
            act = gate / (1.0 + jnp.exp(-gate)) * up
            hid[k, pl.ds(pl.multiple_of(mine + i * 16, 16), 16), :] = act.astype(BF16)
            return carry

        lax.fori_loop(0, rows_h // 16, piece, 0, unroll=2)
        own_h = hid.at[k, pl.ds(mine, rows_h)]
        send(own_h, own_h, h_s.at[k], h_r.at[k], partner)

    def hidden_got(k):
        got(hid.at[k, pl.ds(theirs, rows_h)], h_s.at[k], h_r.at[k])

    def down_half(k, h):
        s = k % 2
        lhs = hid[k]
        for j in range(h * col_h, (h + 1) * col_h, 256):
            cols = pl.ds(j, 256)
            outp[s, :, :, :, cols] = (
                jnp.dot(lhs, wd[:, cols], preferred_element_type=F32)
                .astype(BF16)
                .reshape(RING, RING, TILE, 256)
            )
        yr0(k, h)

    halves = (pl.ds(0, 2), pl.ds(2, 2))
    cols2 = (pl.ds(0, col_h // 2), pl.ds(col_h // 2, col_h // 2))

    def chunk(k, h, i, others):
        cols = pl.ds(h * col_h, col_h)
        if h == 0:
            return outp.at[k % 2, i, others, :, cols]
        return outp.at[k % 2, others, i, :, cols]

    def raxes(h):
        return (("z", z), ("y", y)) if h == 0 else (("y", y), ("z", z))

    def yr0(k, h):
        (a, i), _ = raxes(h)
        ss, rs = yr_s.at[k, 0], yr_r.at[k, h, 0]
        send(chunk(k, h, nb(i, 2), halves[0]), yrel.at[k, h, 0], ss, rs.at[0], dev_yz(a, 1))
        send(chunk(k, h, nb(i, 2), halves[1]), yrel.at[k, h, 1], ss, rs.at[1], dev_yz(a, -1))
        send(chunk(k, h, nb(i, 1), halves[1]), yfin.at[k, h, 0, halves[1]], ss, rs.at[2], dev_yz(a, 1))
        send(chunk(k, h, nb(i, -1), halves[0]), yfin.at[k, h, 1, halves[0]], ss, rs.at[2], dev_yz(a, -1))

    def yr1(k, h, n):
        (a, i), _ = raxes(h)
        ss, rs = yr_s.at[k, 0], yr_r.at[k, h, 0]
        d = 1 - 2 * n
        got(yrel.at[k, h, n], ss, rs.at[n])
        own = chunk(k, h, nb(i, d), halves[n])
        own[...] = add(own, yrel.at[k, h, n])
        send(own, yfin.at[k, h, n, halves[n]], ss, rs.at[2], dev_yz(a, d))

    def yr2(k, h):
        (a, i), (b, j) = raxes(h)
        ss, rs = yr_s.at[k, 0], yr_r.at[k, h, 0]
        got(yfin.at[k, h], ss, rs.at[2])
        own = chunk(k, h, i, pl.ds(0, RING))

        def piece(o, carry):
            ysum[k % 2, h, o] = (
                own[o].astype(F32) + yfin[k, h, 0, o].astype(F32) + yfin[k, h, 1, o].astype(F32)
            ).astype(BF16)
            return carry

        lax.fori_loop(0, RING, piece, 0)
        ss, rs = yr_s.at[k, 1], yr_r.at[k, h, 1]

        def sums(i, n):
            return ysum.at[k % 2, h, i, :, cols2[n]]

        send(sums(nb(j, 2), 0), y2rel.at[k, h, 0], ss, rs.at[0], dev_yz(b, 1))
        send(sums(nb(j, 2), 1), y2rel.at[k, h, 1], ss, rs.at[1], dev_yz(b, -1))
        send(sums(nb(j, 1), 1), y2fin.at[k, h, 0, :, cols2[1]], ss, rs.at[2], dev_yz(b, 1))
        send(sums(nb(j, -1), 0), y2fin.at[k, h, 1, :, cols2[0]], ss, rs.at[2], dev_yz(b, -1))

    def yr3(k, h, n):
        _, (b, j) = raxes(h)
        ss, rs = yr_s.at[k, 1], yr_r.at[k, h, 1]
        d = 1 - 2 * n
        got(y2rel.at[k, h, n], ss, rs.at[n])
        own = ysum.at[k % 2, h, nb(j, d), :, cols2[n]]
        own[...] = add(own, y2rel.at[k, h, n])
        send(own, y2fin.at[k, h, n, :, cols2[n]], ss, rs.at[2], dev_yz(b, d))

    def yr4(k, h):
        _, (b, j) = raxes(h)
        ss, rs = yr_s.at[k, 1], yr_r.at[k, h, 1]
        got(y2fin.at[k, h], ss, rs.at[2])
        total = (
            ysum[k % 2, h, j].astype(F32) + y2fin[k, h, 0].astype(F32) + y2fin[k, h, 1].astype(F32)
        )
        top, bottom = total[0:SUB], total[SUB:TILE]
        first = q == 0
        res[k, :, pl.ds(pl.multiple_of(q * half_d + h * col_h, col_h), col_h)] = jnp.where(first, top, bottom).astype(BF16)
        obuf[k, :, pl.ds(h * col_h, col_h)] = jnp.where(first, bottom, top).astype(BF16)

    def swap(k):
        send(
            obuf.at[k],
            res.at[k, :, pl.ds(pl.multiple_of(q * half_d, half_d), half_d)],
            o_s.at[k],
            o_r.at[k],
            partner,
        )

    def swap_got(k):
        got(res.at[k, :, pl.ds(pl.multiple_of((1 - q) * half_d, half_d), half_d)], o_s.at[k], o_r.at[k])

    def x_left(k):
        left(mate.at[0], q_s.at[k], q_r.at[k, 0])
        left(xrel.at[pl.ds(0, 3)], xr_s.at[k], xr_r.at[k, 0])

    def y_left(k):
        left(yrel.at[pl.ds(0, 3)], yr_s.at[k, 0], yr_r.at[k, 0, 0, 0])
        left(y2rel.at[pl.ds(0, 3)], yr_s.at[k, 1], yr_r.at[k, 0, 1, 0])

    steps = {
        "ag0": ag0, "ag1": ag1, "ag2": ag2, "ag3": ag3, "ag4": ag4, "gu": gu_tile, "gf": gu_finish,
        "xr": x_relay, "hid": hidden, "hg": hidden_got, "dn": down_half, "yr1": yr1, "yr2": yr2,
        "yr3": yr3, "yr4": yr4, "swap": swap, "xleft": x_left, "yleft": y_left,
        "mgu": mask_gu, "md": mask_d,
    }
    def store(k):
        swap_got(k)
        pltpu.make_async_copy(res.at[k], out.at[k], st_sem.at[k]).start()

    def settle(k):
        ag_left(k)
        left(hid.at[k, pl.ds(mine, rows_h)], h_s.at[k], h_r.at[k])
        if k == 0:
            left(sent.at[:, :, pl.ds(0, (2 * RING - 1) * feats)], a2a_s.at[0], a2a_r.at[0])

    last_half = {args[0]: args[1] for name, *args in ORDER if name == "yr2"}
    a2a_wait(0)
    exchanged = False
    for name, *args in ORDER:
        if name == "ag0" and args[0] > 0 and not exchanged:
            a2a_wait(1)
            exchanged = True
        steps[name](*args)
        if name == "swap" and args[0] > 0:
            store(args[0] - 1)
        if name == "yr2" and args[1] == last_half[args[0]]:
            settle(args[0])
    store(STAGES - 1)

    for k in range(STAGES):
        left(obuf.at[k], o_s.at[k], o_r.at[k])
    for k in range(STAGES):
        pltpu.make_async_copy(res.at[k], out.at[k], st_sem.at[k]).wait()


def body(tokens, norm_gain, gate_weight, up_weight, down_weight, gate_mask, up_mask, down_mask):
    own, model = tokens.shape
    feats, width = gate_weight.shape
    half_d = model // 2
    rows = RING * RING * TILE
    dma = pltpu.SemaphoreType.DMA
    anyspace = pl.BlockSpec(memory_space=pl.ANY)
    result = pl.pallas_call(
        kernel,
        out_shape=jax.ShapeDtypeStruct((STAGES, SUB, model), BF16),
        in_specs=[anyspace] * 8,
        out_specs=anyspace,
        scratch_shapes=[
            pltpu.VMEM((1, model), F32),
            pltpu.VMEM(gate_mask.shape, jnp.int32),
            pltpu.VMEM(up_mask.shape, jnp.int32),
            pltpu.VMEM(down_mask.shape, jnp.int32),
            pltpu.VMEM((STAGES, SUB, model), BF16),
            pltpu.VMEM((STAGES, SUB, model), BF16),
            pltpu.VMEM((STAGES, RING, 2, SUB, feats), BF16),
            pltpu.VMEM((STAGES, RING, RING, RING, TILE, feats), BF16),
            pltpu.VMEM((feats, 2 * width), BF16),
            pltpu.VMEM((width, half_d), BF16),
            pltpu.VMEM((feats // BLOCK, 2 * width), F32),
            pltpu.VMEM((width // BLOCK, half_d), F32),
            pltpu.VMEM((2, RING, rows, 2 * width), BF16),
            pltpu.VMEM((2, RING, rows // 2, 2 * width), BF16),
            pltpu.VMEM((STAGES, 2, rows // 4, 2 * width), BF16),
            pltpu.VMEM((STAGES, 2, rows // 2, 2 * width), BF16),
            pltpu.VMEM((STAGES, rows, width), BF16),
            pltpu.VMEM((2, RING, RING, TILE, half_d), BF16),
            pltpu.VMEM((STAGES, 2, 2, 2, TILE, half_d // 2), BF16),
            pltpu.VMEM((STAGES, 2, 2, RING, TILE, half_d // 2), BF16),
            pltpu.VMEM((2, 2, RING, TILE, half_d // 2), BF16),
            pltpu.VMEM((STAGES, 2, 2, TILE, half_d // 4), BF16),
            pltpu.VMEM((STAGES, 2, 2, TILE, half_d // 2), BF16),
            pltpu.VMEM((STAGES, SUB, model), BF16),
            pltpu.VMEM((STAGES, SUB, half_d), BF16),
            dma((4,)),
            dma((5,)),
            dma((STAGES,)),
            dma((1,)),
            dma((2,)),
            dma((STAGES,)),
            dma((STAGES, 2, 2, 6)),
            dma((STAGES,)),
            dma((STAGES, 4)),
            dma((STAGES,)),
            dma((STAGES, 3)),
            dma((STAGES,)),
            dma((STAGES,)),
            dma((STAGES, 2)),
            dma((STAGES, 2, 2, 3)),
            dma((STAGES,)),
            dma((STAGES,)),
        ],
        compiler_params=pltpu.CompilerParams(
            collective_id=0, has_side_effects=True, vmem_limit_bytes=67_000_000
        ),
    )(
        tokens.reshape(STAGES, SUB, model),
        norm_gain.reshape(1, model),
        gate_weight,
        up_weight,
        down_weight,
        gate_mask,
        up_mask,
        down_mask,
    )
    return result.reshape(own, model)


def solution(mesh):
    return jax.shard_map(
        body,
        mesh=mesh,
        in_specs=(
            P(("rows", "cols"), None),
            P(),
            P("rows", "cols"),
            P("rows", "cols"),
            P("cols", None),
            P("rows", "cols"),
            P("rows", "cols"),
            P("cols", None),
        ),
        out_specs=P(("rows", "cols"), None),
        check_vma=False,
    )
```
